32 devices in a mesh: dp: 4 (over y, x), blk: 8 (over z, core).
Axes of the slice: x: 2, y: 2, z: 4, core: 2. Of those that a mesh axis runs over, the one named last changes fastest.
Arguments:
- tokens: bfloat16 [16, 512, 1024], P('dp', 'blk'), may hold values from -6 to 6
- first_values: bfloat16 [16, 512, 1024], P('dp', 'blk'), may hold values from -6 to 6
- docs: int32 [16, 512], P('dp', 'blk'), may hold values from 0 to 3, never falling along the last dimension, each value on 1 to 384 neighbouring positions
- cotangent: bfloat16 [16, 512, 1024], P('dp', 'blk'), may hold values from -6 to 6
- w_qkv: bfloat16 [1024, 3072], replicated, may hold values from -0.1875 to 0.1875
- w_out: bfloat16 [1024, 1024], replicated, may hold values from -3 to 3
- w_gate: bfloat16 [1024, 2816], replicated, may hold values from -0.1875 to 0.1875
- w_up: bfloat16 [1024, 2816], replicated, may hold values from -0.1875 to 0.1875
- w_down: bfloat16 [2816, 1024], replicated, may hold values from -0.109375 to 0.109375
- gain_attn: float32 [1024], replicated, may hold values from 0.5 to 1.5
- gain_ffn: float32 [1024], replicated, may hold values from 0.5 to 1.5
Outputs:
- output: bfloat16 [16, 512, 1024], P('dp', 'blk')
- grad_tokens: bfloat16 [16, 512, 1024], P('dp', 'blk')
- grad_first_values: bfloat16 [16, 512, 1024], P('dp', 'blk')
- grad_qkv: float32 [1024, 3072], P(('dp', 'blk'))
- grad_out: float32 [1024, 1024], P(('dp', 'blk'))
- grad_gate: float32 [1024, 2816], P(('dp', 'blk'))
- grad_up: float32 [1024, 2816], P(('dp', 'blk'))
- grad_down: float32 [2816, 1024], P(('dp', 'blk'))
- grad_gain_attn: float32 [1024], P(('dp', 'blk'))
- grad_gain_ffn: float32 [1024], P(('dp', 'blk'))
The draws below stay inside these ranges and needn't reach their ends.
Inputs may be any that keep to these rules, and one draw needn't show every extreme that they name: `docs`: along each sequence the document ids never fall, begin at 0 and take every value up to 3; each document has 1 to 384 positions.
All inputs are finite; a program needn't handle non-finite values.
Results may differ from the reference program's by a relative error of at most 0.023.
Values may be sent and summed in bfloat16 or wider, within the bound.
No kernel may reach another device: no remote copies, remote signals or barrier semaphores. Data moves between devices by JAX's collectives and lax.ppermute only.
A program may use at most 320 MiB of HBM per device.

```python
import math
import jax
import jax.numpy as jnp
import numpy as np
from jax import lax

D = 1024
HEADS = 16
HEAD_DIM = 64
FF = 2816
DOCS = 4
SEQS = 16
LEN = 512
DOC_MOST = 384


def block_scale(key, extent, shards, low, high):
    def one(position, parts):
        draws = jax.random.uniform(jax.random.fold_in(jax.random.fold_in(key, 6), position), (parts,), jnp.float32, low / len(shards), high / len(shards))
        return jnp.repeat(jnp.exp(draws), extent[position] // parts).reshape((-1,) + (1,) * (len(extent) - position - 1))

    gain = one(*shards[0])
    for cut in shards[1:]:
        gain = gain * one(*cut)
    return gain


def profile(count, total, limit, skew):
    loads = [(1 << 20) // math.isqrt(rank ** skew) + 1 for rank in range(2, count + 1)]
    surplus, given = total - limit - (count - 1), [1] * (count - 1)
    while surplus > 0:
        movable = [i for i in range(count - 1) if given[i] < limit]
        whole, budget = sum([loads[i] for i in movable]), surplus
        for i in movable:
            addition = min(limit - given[i], max(1, budget * loads[i] // whole), surplus)
            given[i] = given[i] + addition
            surplus = surplus - addition
    return np.array([limit] + given)


def ragged(own_key, number_of, total, bound, slope):
    if number_of == 2:
        one = jax.random.randint(own_key, (), max(1, total - bound), min(bound, total - 1) + 1)
        return jnp.stack([one, total - one])
    tallies = jnp.asarray(profile(number_of, total, bound, slope), jnp.int32)
    pairs = (number_of - 1) // 2
    source_of, taker = tallies[1:1 + 2 * pairs:2], tallies[2:2 + 2 * pairs:2]
    slack = jnp.minimum(source_of - 1, bound - taker)
    moved = jax.random.randint(jax.random.fold_in(own_key, 1), (pairs,), 0, 1 << 20) % (slack + 1)
    tallies = tallies.at[1:1 + 2 * pairs:2].set(source_of - moved).at[2:2 + 2 * pairs:2].set(taker + moved)
    return tallies[jax.random.permutation(jax.random.fold_in(own_key, 2), number_of)]


def bell_draw(stream_key, extent, spread, limit, shards=(), held_as=jnp.bfloat16):
    level = block_scale(stream_key, extent, shards, -0.22, 0.18) if shards else 1.0
    drawn = jax.random.normal(stream_key, extent, jnp.float32) * spread * level
    return jnp.minimum(jnp.maximum(drawn, -limit), limit).astype(held_as)


def setup_inputs(seed: int = 0) -> dict:
    arg_keys = jax.random.split(jax.random.key(seed), 12)
    return {
        "tokens": bell_draw(arg_keys[0], (SEQS, LEN, D), 1.0, 6.0, ((0, 4), (1, 8))),
        "first_values": bell_draw(arg_keys[1], (SEQS, LEN, D), 1.0, 6.0, ((0, 4), (1, 8))),
        "docs": jax.vmap(lambda own: jnp.searchsorted(jnp.cumsum(ragged(own, DOCS, LEN, DOC_MOST, 2)), jnp.arange(LEN), side="right"))(jax.random.split(arg_keys[2], SEQS)).reshape((SEQS, LEN)).astype(jnp.int32),
        "cotangent": bell_draw(arg_keys[3], (SEQS, LEN, D), 1.0, 6.0, ((0, 4), (1, 8))),
        "w_qkv": bell_draw(arg_keys[4], (D, 3 * D), D ** -0.5, 0.1875),
        "w_out": bell_draw(arg_keys[5], (D, D), (max(D // 256, 4)) ** -0.5, 3.0),
        "w_gate": bell_draw(arg_keys[6], (D, FF), D ** -0.5, 0.1875),
        "w_up": bell_draw(arg_keys[7], (D, FF), D ** -0.5, 0.1875),
        "w_down": bell_draw(arg_keys[8], (FF, D), FF ** -0.5, 0.109375),
        "gain_attn": jnp.clip(1.0 + 0.1 * jax.random.normal(arg_keys[9], (D,), jnp.float32), 0.5, 1.5),
        "gain_ffn": jnp.clip(1.0 + 0.1 * jax.random.normal(arg_keys[10], (D,), jnp.float32), 0.5, 1.5),
    }


@jax.custom_vjp
def low(v):
    return lax.optimization_barrier(v.astype(jnp.bfloat16)).astype(jnp.float32)

@jax.custom_vjp
def low_back(v):
    return v

def low_keep(v):
    return (low(v), None)

def low_pass(kept, grad):
    return (grad,)

def back_keep(v):
    return (v, None)

def back_low(kept, grad):
    return (low(grad),)
low.defvjp(low_keep, low_pass)
low_back.defvjp(back_keep, back_low)
epsilon = 1e-06
score_scale = 0.125

def product(left_side, right_side):
    return jnp.dot(left_side, right_side, precision=lax.Precision.HIGHEST, preferred_element_type=jnp.float32)

def norm_scale(values):
    return lax.rsqrt(lax.optimization_barrier(jnp.mean(values * values, axis=-1, keepdims=True)) + epsilon)

def rope_tables(positions, half_dim):
    inverse = 10000.0 ** (-jnp.arange(half_dim, dtype=jnp.float32) / half_dim)
    angles = positions.astype(jnp.float32)[:, None] * inverse[None, :]
    angles = jnp.concatenate([angles, angles], axis=-1)
    return (jnp.cos(angles), jnp.sin(angles))

def rotate(values, cosine, sines):
    half_dim = values.shape[-1] // 2
    turned = jnp.concatenate([-values[..., half_dim:], values[..., :half_dim]], axis=-1)
    return values * cosine + turned * sines

def attention(queries, keys_rot, mixed_values, doc_row):
    length = queries.shape[0]
    block_rows = min(512, length)
    count_blocks = length // block_rows
    positions = jnp.arange(length, dtype=jnp.int32)

    def one_block(block_args):
        part_queries, part_docs, part_positions = block_args
        scores = jnp.einsum('qhd,khd->hqk', part_queries, keys_rot, precision=lax.Precision.HIGHEST) * score_scale
        scores = low_back(scores)
        allowed = (positions[None, :] <= part_positions[:, None]) & (doc_row[None, :] == part_docs[:, None])
        scores = jnp.where(allowed[None], scores, -1e+30)
        running_top = lax.optimization_barrier(jnp.max(scores, axis=-1, keepdims=True))
        weights = jnp.exp(scores - running_top)
        weights = weights / lax.optimization_barrier(jnp.sum(weights, axis=-1, keepdims=True))
        return jnp.einsum('hqk,khd->qhd', low(weights), mixed_values, precision=lax.Precision.HIGHEST)
    blocks = lax.map(jax.checkpoint(one_block), (queries.reshape(count_blocks, block_rows, HEADS, HEAD_DIM), doc_row.reshape(count_blocks, block_rows), positions.reshape(count_blocks, block_rows)))
    return blocks.reshape(length, HEADS * HEAD_DIM)

def layer(inputs, first_values, w_qkv, w_out, w_gate, w_up, w_down, gain_attn, gain_ffn, doc_row):
    length, model_width = inputs.shape
    head_shape = (length, HEADS, HEAD_DIM)
    normed = low(inputs * norm_scale(inputs) * gain_attn)
    projected = low_back(product(normed, w_qkv))
    cosine, sines = rope_tables(jnp.arange(length, dtype=jnp.int32), HEAD_DIM // 2)
    cosine = cosine[:, None, :]
    sines = sines[:, None, :]
    queries = low(rotate(projected[:, :model_width].reshape(head_shape), cosine, sines))
    keys_rot = low(rotate(projected[:, model_width:2 * model_width].reshape(head_shape), cosine, sines))
    mixed_values = low(0.5 * projected[:, 2 * model_width:] + 0.5 * first_values).reshape(head_shape)
    attended = low(low_back(attention(queries, keys_rot, mixed_values, doc_row)))
    middle = inputs + low_back(product(attended, w_out))
    normed_ffn = low(middle * norm_scale(middle) * gain_ffn)
    gate = low_back(product(normed_ffn, w_gate))
    upward = low_back(product(normed_ffn, w_up))
    hidden = low(jax.nn.silu(gate) * upward)
    return middle + low_back(product(hidden, w_down))

def reference(tokens, first_values, docs, cotangent, w_qkv, w_out, w_gate, w_up, w_down, gain_attn, gain_ffn):
    params = (w_qkv.astype(jnp.float32), w_out.astype(jnp.float32), w_gate.astype(jnp.float32), w_up.astype(jnp.float32), w_down.astype(jnp.float32), gain_attn.astype(jnp.float32), gain_ffn.astype(jnp.float32))

    def one_row(totals, row_data):
        row_tokens, row_first, row_docs, row_cot = row_data

        def forward(inputs, first_row, weight_qkv, weight_out, weight_gate, weight_up, weight_down, gain_one, gain_two):
            return layer(inputs, first_row, weight_qkv, weight_out, weight_gate, weight_up, weight_down, gain_one, gain_two, row_docs)
        output, pullback = jax.vjp(forward, row_tokens.astype(jnp.float32), row_first.astype(jnp.float32), *params)
        grads = pullback(row_cot.astype(jnp.float32))
        totals = tuple((running + fresh for running, fresh in zip(totals, grads[2:])))
        return (totals, (output.astype(jnp.bfloat16), grads[0].astype(jnp.bfloat16), grads[1].astype(jnp.bfloat16)))
    zeros = tuple((jnp.zeros(weight.shape, jnp.float32) for weight in params))
    totals, outputs = lax.scan(one_row, zeros, (tokens, first_values, docs, cotangent))
    return (outputs[0], outputs[1], outputs[2], totals[0], totals[1], totals[2], totals[3], totals[4], totals[5], totals[6])
```

```python
import functools

import jax
import jax.numpy as jnp
from jax import lax
from jax.experimental import pallas as pl
from jax.experimental.pallas import tpu as pltpu
from jax.sharding import PartitionSpec as P

HEAD_DIM = 64
LANES = 128
AXES = ("dp", "blk")
epsilon = 1e-06
score_scale = 0.125
bf16 = jnp.bfloat16
f32 = jnp.float32

NN = (((1,), (0,)), ((), ()))
NT = (((1,), (1,)), ((), ()))
TN = (((0,), (0,)), ((), ()))


def mm(a, b, dims):
    return lax.dot_general(a, b, dims, preferred_element_type=f32)


def sds(shape, dtype):
    return jax.ShapeDtypeStruct(shape, dtype)


def cost(flops, nbytes, trans=0):
    return pl.CostEstimate(flops=int(flops), bytes_accessed=int(nbytes), transcendentals=int(trans))


def whole(shape):
    return pl.BlockSpec(shape, lambda *_: (0,) * len(shape))


def lane_half(shape):
    lane = lax.broadcasted_iota(jnp.int32, shape, len(shape) - 1)
    return (lane & (HEAD_DIM - 1)) < HEAD_DIM // 2


def turn(values):
    half = HEAD_DIM // 2
    return jnp.where(
        lane_half(values.shape),
        pltpu.roll(values, LANES - half, 1),
        pltpu.roll(values, half, 1),
    )


def head_mask(shape, head):
    lane = lax.broadcasted_iota(jnp.int32, shape, 1)
    return lane < HEAD_DIM if head == 0 else lane >= HEAD_DIM


def qkv_body(nq, x_ref, gain_ref, w_ref, first_ref, cos_ref, sin_ref, normed_ref, q_ref, kv_ref):
    step = pl.program_id(0)

    @pl.when(step == 0)
    def _():
        inputs = x_ref[...].astype(f32)
        factor = lax.rsqrt(jnp.mean(inputs * inputs, axis=-1, keepdims=True) + epsilon)
        normed_ref[...] = (inputs * factor * gain_ref[...]).astype(bf16)

    projected = mm(normed_ref[...], w_ref[...], NN)
    width = projected.shape[1]

    def rotated():
        parts = []
        for i in range(width // LANES):
            part = projected[:, i * LANES : (i + 1) * LANES]
            parts.append((part * cos_ref[...] + turn(part) * sin_ref[...]).astype(bf16))
        return jnp.concatenate(parts, axis=1)

    @pl.when(step < nq)
    def _():
        q_ref[...] = rotated()

    @pl.when((step >= nq) & (step < 2 * nq))
    def _():
        kv_ref[...] = rotated()

    @pl.when(step >= 2 * nq)
    def _():
        kv_ref[...] = (0.5 * projected + 0.5 * first_ref[...].astype(f32)).astype(bf16)


def project(x, gain, w_qkv, first, cosine, sines):
    rows, width = x.shape
    bn = 512
    nq = width // bn
    return pl.pallas_call(
        functools.partial(qkv_body, nq),
        grid=(3 * nq,),
        in_specs=[
            whole((rows, width)),
            whole((1, width)),
            pl.BlockSpec((width, bn), lambda j: (0, j)),
            pl.BlockSpec((rows, bn), lambda j: (0, jnp.maximum(j - 2 * nq, 0))),
            whole((rows, LANES)),
            whole((rows, LANES)),
        ],
        out_specs=[
            whole((rows, width)),
            pl.BlockSpec((rows, bn), lambda j: (0, jnp.minimum(j, nq - 1))),
            pl.BlockSpec((rows, bn), lambda j: (0, jnp.maximum(j - nq, 0))),
        ],
        out_shape=[sds((rows, width), bf16), sds((rows, width), bf16), sds((rows, 2 * width), bf16)],
        cost_estimate=cost(6 * rows * width * width, 6 * width * width + 12 * rows * width),
        name="project",
    )(x, gain, w_qkv, first, cosine, sines)


def set_bias(bias_ref, kpos_ref, qpos_ref, qstart_ref):
    keys, qpos = kpos_ref[...], qpos_ref[...]
    allowed = (keys <= qpos) & (keys >= qstart_ref[...])
    bias_ref[...] = jnp.where(allowed, 0.0, -1e30)


def attend_body(slots, *refs):
    q_ref = refs[0]
    k_refs = refs[1 : 1 + slots]
    v_refs = refs[1 + slots : 1 + 2 * slots]
    kpos_ref, qpos_ref, qstart_ref, out_ref, lse_ref, bias_ref = refs[1 + 2 * slots :]

    @pl.when(pl.program_id(0) == 0)
    def _():
        set_bias(bias_ref, kpos_ref, qpos_ref, qstart_ref)

    queries = q_ref[...] * jnp.asarray(score_scale, bf16)
    keys = jnp.concatenate([r[...] for r in k_refs], axis=0)
    values = jnp.concatenate([r[...] for r in v_refs], axis=0)
    values_t = jnp.transpose(values)
    outs = []
    for head in range(2):
        own = jnp.where(head_mask(queries.shape, head), queries, jnp.zeros_like(queries))
        scores = mm(keys, own, NT) + bias_ref[...]
        top = jnp.max(scores, axis=0, keepdims=True)
        weights = jnp.exp(scores - top)
        total = jnp.sum(weights, axis=0, keepdims=True)
        probs = (weights * (1.0 / total)).astype(bf16)
        outs.append(mm(values_t[head * HEAD_DIM : (head + 1) * HEAD_DIM], probs, NN))
        lse_ref[0, head : head + 1, :] = top + jnp.log(total)
    out_ref[...] = jnp.transpose(jnp.concatenate(outs, axis=0)).astype(bf16)


def attend(q, kvs, kpos, qpos, qstart):
    rows, width = q.shape
    slots = len(kvs)
    pairs = width // LANES
    keys = slots * rows
    col = pl.BlockSpec((rows, LANES), lambda i: (0, i))
    col_v = pl.BlockSpec((rows, LANES), lambda i: (0, pairs + i))
    return pl.pallas_call(
        functools.partial(attend_body, slots),
        grid=(pairs,),
        in_specs=[col]
        + [col] * slots
        + [col_v] * slots
        + [whole((keys, 1)), whole((1, rows)), whole((1, rows))],
        out_specs=[col, pl.BlockSpec((1, 2, rows), lambda i: (i, 0, 0))],
        out_shape=[sds((rows, width), bf16), sds((pairs, 2, rows), f32)],
        scratch_shapes=[pltpu.VMEM((keys, rows), f32)],
        cost_estimate=cost(
            8 * pairs * rows * keys * LANES, 2 * rows * width * (2 + 2 * slots), 2 * pairs * rows * keys
        ),
        name="attend",
    )(q, *kvs, *kvs, kpos, qpos, qstart)


def attend_back_body(slots, *refs):
    q_ref, grad_ref = refs[:2]
    k_refs = refs[2 : 2 + slots]
    v_refs = refs[2 + slots : 2 + 2 * slots]
    lse_ref, kpos_ref, qpos_ref, qstart_ref, cos_ref, sin_ref = refs[2 + 2 * slots : 8 + 2 * slots]
    gq_ref, gk_ref, gv_ref = refs[8 + 2 * slots : 11 + 2 * slots]
    other_k = refs[11 + 2 * slots : 10 + 3 * slots]
    other_v = refs[10 + 3 * slots : 9 + 4 * slots]
    bias_ref = refs[-1]

    @pl.when(pl.program_id(0) == 0)
    def _():
        set_bias(bias_ref, kpos_ref, qpos_ref, qstart_ref)

    queries = q_ref[...] * jnp.asarray(score_scale, bf16)
    grads = grad_ref[...]
    keys = jnp.concatenate([r[...] for r in k_refs], axis=0)
    values = jnp.concatenate([r[...] for r in v_refs], axis=0)
    keys_t = jnp.transpose(keys)
    grad_values = grad_keys = None
    grad_q = []
    for head in range(2):
        mask = head_mask(queries.shape, head)
        own_q = jnp.where(mask, queries, jnp.zeros_like(queries))
        own_g = jnp.where(mask, grads, jnp.zeros_like(grads))
        scores = mm(keys, own_q, NT) + bias_ref[...]
        probs = jnp.exp(scores - lse_ref[0, head : head + 1, :])
        grad_probs = mm(values, own_g, NT)
        delta = jnp.sum(probs * grad_probs, axis=0, keepdims=True)
        grad_scores = (probs * (grad_probs - delta)).astype(bf16)
        part_v = mm(probs.astype(bf16), own_g, NN)
        part_k = mm(grad_scores, own_q, NN)
        grad_values = part_v if grad_values is None else grad_values + part_v
        grad_keys = part_k if grad_keys is None else grad_keys + part_k
        grad_q.append(mm(keys_t[head * HEAD_DIM : (head + 1) * HEAD_DIM], grad_scores, NN))
    grad_q = jnp.transpose(jnp.concatenate(grad_q, axis=0)) * score_scale
    gq_ref[...] = (grad_q * cos_ref[...] - turn(grad_q) * sin_ref[...]).astype(bf16)
    rows = q_ref.shape[0]
    gk_ref[...] = grad_keys[:rows]
    gv_ref[...] = grad_values[:rows]
    for slot in range(1, slots):
        other_k[slot - 1][...] = grad_keys[slot * rows : (slot + 1) * rows].astype(bf16)
        other_v[slot - 1][...] = grad_values[slot * rows : (slot + 1) * rows].astype(bf16)


def attend_back(q, grad, kvs, lse, kpos, qpos, qstart, cosine, sines):
    rows, width = q.shape
    slots = len(kvs)
    pairs = width // LANES
    keys = slots * rows
    col = pl.BlockSpec((rows, LANES), lambda i: (0, i))
    col_v = pl.BlockSpec((rows, LANES), lambda i: (0, pairs + i))
    outs = pl.pallas_call(
        functools.partial(attend_back_body, slots),
        grid=(pairs,),
        in_specs=[col, col]
        + [col] * slots
        + [col_v] * slots
        + [pl.BlockSpec((1, 2, rows), lambda i: (i, 0, 0))]
        + [whole((keys, 1)), whole((1, rows)), whole((1, rows))]
        + [whole((rows, LANES))] * 2,
        out_specs=[col] * (3 + 2 * (slots - 1)),
        out_shape=[sds((rows, width), bf16)]
        + [sds((rows, width), f32)] * 2
        + [sds((rows, width), bf16)] * (2 * (slots - 1)),
        scratch_shapes=[pltpu.VMEM((keys, rows), f32)],
        cost_estimate=cost(
            20 * pairs * rows * keys * LANES, 2 * rows * width * (7 + 4 * slots), 2 * pairs * rows * keys
        ),
        name="attend_back",
    )(q, grad, *kvs, *kvs, lse, kpos, qpos, qstart, cosine, sines)
    gq, gk, gv = outs[:3]
    return gq, gk, gv, outs[3 : 2 + slots], outs[2 + slots :]


def ffn_body(
    steps,
    ff,
    x_ref,
    att_ref,
    wout_ref,
    gain_ref,
    cot_ref,
    wg_ref,
    wu_ref,
    wd_ref,
    nffn_ref,
    hidden_ref,
    acts_ref,
    out_ref,
    gmid_ref,
    gbranch_ref,
    gatt_ref,
    mid_s,
    acc_s,
    gacc_s,
    hid_s,
    gg_s,
    gu_s,
):
    step = pl.program_id(0)
    block = wg_ref.shape[1]

    @pl.when(step == 0)
    def _():
        middle = x_ref[...].astype(f32) + mm(att_ref[...], wout_ref[...], NN)
        mid_s[...] = middle
        factor = lax.rsqrt(jnp.mean(middle * middle, axis=-1, keepdims=True) + epsilon)
        nffn_ref[...] = (middle * factor * gain_ref[...]).astype(bf16)
        acc_s[...] = middle
        gacc_s[...] = jnp.zeros_like(gacc_s)

    normed = nffn_ref[...]
    wd = wd_ref[...]
    gate = mm(normed, wg_ref[...], NN)
    upward = mm(normed, wu_ref[...], NN)
    grad_hidden = mm(cot_ref[...], wd, NT)
    sig = 1.0 / (1.0 + jnp.exp(-gate))
    silu = gate * sig
    hidden = (silu * upward).astype(bf16)
    grad_gate = (grad_hidden * upward * (sig * (1.0 + gate * (1.0 - sig)))).astype(bf16)
    grad_up = (grad_hidden * silu).astype(bf16)
    acc_s[...] += mm(hidden, wd, NN)
    gacc_s[...] += mm(grad_gate, wg_ref[...], NT) + mm(grad_up, wu_ref[...], NT)
    at = pl.ds(pl.multiple_of(step * block, block), block)
    hid_s[:, at] = hidden
    gg_s[:, at] = grad_gate
    gu_s[:, at] = grad_up

    @pl.when(step == steps - 1)
    def _():
        quarter = ff // 4
        for i in range(4):
            cut = slice(i * quarter, (i + 1) * quarter)
            hidden_ref[i] = hid_s[:, cut]
            acts_ref[i] = jnp.concatenate([gg_s[:, cut], gu_s[:, cut]], axis=1)
        out_ref[...] = acc_s[...].astype(bf16)
        middle = mid_s[...]
        factor = lax.rsqrt(jnp.mean(middle * middle, axis=-1, keepdims=True) + epsilon)
        scaled = gacc_s[...] * gain_ref[...]
        inner = jnp.mean(scaled * middle, axis=-1, keepdims=True)
        grad_middle = cot_ref[...].astype(f32) + factor * (
            scaled - middle * (factor * factor * inner)
        )
        gmid_ref[...] = grad_middle
        branch = grad_middle.astype(bf16)
        gbranch_ref[...] = branch
        gatt_ref[...] = mm(branch, wout_ref[...], NT).astype(bf16)


def feed_forward(x, attended, w_out, gain, cot, w_gate, w_up, w_down):
    rows, width = x.shape
    ff = w_gate.shape[1]
    block = 256
    steps = ff // block
    quarter = ff // 4
    full = whole((rows, width))
    return pl.pallas_call(
        functools.partial(ffn_body, steps, ff),
        grid=(steps,),
        in_specs=[
            full,
            full,
            whole((width, width)),
            whole((1, width)),
            full,
            pl.BlockSpec((width, block), lambda j: (0, j)),
            pl.BlockSpec((width, block), lambda j: (0, j)),
            pl.BlockSpec((block, width), lambda j: (j, 0)),
        ],
        out_specs=[full, whole((4, rows, quarter)), whole((4, rows, 2 * quarter)), full, full, full, full],
        out_shape=[
            sds((rows, width), bf16),
            sds((4, rows, quarter), bf16),
            sds((4, rows, 2 * quarter), bf16),
            sds((rows, width), bf16),
            sds((rows, width), f32),
            sds((rows, width), bf16),
            sds((rows, width), bf16),
        ],
        scratch_shapes=[pltpu.VMEM((rows, width), f32)] * 3 + [pltpu.VMEM((rows, ff), bf16)] * 3,
        cost_estimate=cost(
            12 * rows * width * ff + 4 * rows * width * width,
            6 * width * ff + 2 * width * width + 20 * rows * width,
            rows * ff,
        ),
        name="feed_forward",
    )(x, attended, w_out, gain, cot, w_gate, w_up, w_down)


def grad_pack_body(received, *refs):
    gq_ref, gk_ref, gv_ref = refs[:3]
    other_k = refs[3 : 3 + received]
    other_v = refs[3 + received : 3 + 2 * received]
    cos_ref, sin_ref, packed_ref, first_ref = refs[3 + 2 * received :]
    grad_k, grad_v = gk_ref[...], gv_ref[...]
    for r in other_k:
        grad_k = grad_k + r[...].astype(f32)
    for r in other_v:
        grad_v = grad_v + r[...].astype(f32)
    grad_k = (grad_k * cos_ref[...] - turn(grad_k) * sin_ref[...]).astype(bf16)
    grad_v = (0.5 * grad_v).astype(bf16)
    first_ref[...] = grad_v
    packed_ref[0] = jnp.concatenate([gq_ref[...], grad_k, grad_v], axis=1)


def grad_pack(gq, gk, gv, other_k, other_v, cosine, sines):
    rows, width = gq.shape
    pairs = width // LANES
    received = len(other_k)
    col = pl.BlockSpec((rows, LANES), lambda i: (0, i))
    return pl.pallas_call(
        functools.partial(grad_pack_body, received),
        grid=(pairs,),
        in_specs=[col] * (3 + 2 * received) + [whole((rows, LANES))] * 2,
        out_specs=[pl.BlockSpec((1, rows, 3 * LANES), lambda i: (i, 0, 0)), col],
        out_shape=[sds((pairs, rows, 3 * LANES), bf16), sds((rows, width), bf16)],
        cost_estimate=cost(20 * rows * width, 2 * rows * width * 12),
        name="grad_pack",
    )(gq, gk, gv, *other_k, *other_v, cosine, sines)


def grad_inputs_body(pairs, packed_ref, wq_ref, wk_ref, wv_ref, x_ref, gain_ref, gmid_ref, out_ref, acc_s):
    step = pl.program_id(0)

    @pl.when(step == 0)
    def _():
        acc_s[...] = jnp.zeros_like(acc_s)

    weights = jnp.concatenate([wq_ref[...], wk_ref[...], wv_ref[...]], axis=1)
    acc_s[...] += mm(packed_ref[0], weights, NT)

    @pl.when(step == pairs - 1)
    def _():
        inputs = x_ref[...].astype(f32)
        factor = lax.rsqrt(jnp.mean(inputs * inputs, axis=-1, keepdims=True) + epsilon)
        scaled = acc_s[...] * gain_ref[...]
        inner = jnp.mean(scaled * inputs, axis=-1, keepdims=True)
        grads = gmid_ref[...] + factor * (scaled - inputs * (factor * factor * inner))
        out_ref[...] = grads.astype(bf16)


def grad_inputs(packed, w_qkv, x, gain, grad_middle):
    rows, width = x.shape
    pairs = width // LANES
    full = whole((rows, width))
    return pl.pallas_call(
        functools.partial(grad_inputs_body, pairs),
        grid=(pairs,),
        in_specs=[
            pl.BlockSpec((1, rows, 3 * LANES), lambda i: (i, 0, 0)),
            pl.BlockSpec((width, LANES), lambda i: (0, i)),
            pl.BlockSpec((width, LANES), lambda i: (0, pairs + i)),
            pl.BlockSpec((width, LANES), lambda i: (0, 2 * pairs + i)),
            full,
            whole((1, width)),
            full,
        ],
        out_specs=full,
        out_shape=sds((rows, width), bf16),
        scratch_shapes=[pltpu.VMEM((rows, width), f32)],
        cost_estimate=cost(6 * rows * width * width, 6 * width * width + 16 * rows * width),
        name="grad_inputs",
    )(packed, w_qkv, w_qkv, w_qkv, x, gain, grad_middle)


def outer_body(count, *refs):
    total = None
    for left, right in zip(refs[:count], refs[count : 2 * count]):
        part = mm(left[...], right[...], TN)
        total = part if total is None else total + part
    refs[-1][...] = total.astype(bf16)


def outer(lefts, rights):
    rows, height = lefts[0].shape
    width = rights[0].shape[1]
    count = len(lefts)
    block = 256 if height % 256 == 0 else height
    return pl.pallas_call(
        functools.partial(outer_body, count),
        grid=(height // block,),
        in_specs=[pl.BlockSpec((rows, block), lambda i: (0, i))] * count
        + [whole((rows, width))] * count,
        out_specs=pl.BlockSpec((block, width), lambda i: (i, 0)),
        out_shape=sds((height, width), bf16),
        cost_estimate=cost(
            2 * count * rows * height * width, 2 * (count * rows * (height + width) + height * width)
        ),
        name="outer",
    )(*lefts, *rights)


def build(ndp, nblk):
    n = ndp * nblk
    nbits = n.bit_length() - 1
    blk_bits = nblk.bit_length() - 1
    if (1 << nbits) != n or (1 << blk_bits) != nblk:
        raise ValueError("mesh sizes")
    low_e, high_e = blk_bits, nbits - 1

    def send(value, target):
        pairs = [(i, target(i)) for i in range(n)]
        pairs = [p for p in pairs if p[0] != p[1]]
        return lax.ppermute(value, AXES, pairs)

    def flip(value, bit):
        return send(value, lambda i: i ^ (1 << bit))

    def pick(value, index, axis=0):
        return lax.dynamic_index_in_dim(value, index, axis, keepdims=False)

    def shards(
        tokens, first_values, docs, cotangent, w_qkv, w_out, w_gate, w_up, w_down, gain_attn, gain_ffn
    ):
        seqs, length, width = tokens.shape
        ff = w_gate.shape[1]
        rows = seqs * length
        group = nblk // seqs
        blk = lax.axis_index("blk")
        index = lax.axis_index("dp") * nblk + blk
        seq, member = blk // group, blk % group

        def bit(t):
            return (index >> t) & 1

        def shift_seq(i, s):
            base, b = i - i % nblk, i % nblk
            return base + ((b // group + s) % seqs) * group + b % group

        def shift_member(i, s):
            base, b = i - i % nblk, i % nblk
            return base + (b // group) * group + (b % group + s) % group

        def to_sequence(value):
            parts = [pick(value, seq)]
            for s in range(1, seqs):
                out = pick(value, (seq + s) % seqs)
                parts.append(send(out, lambda i, s=s: shift_seq(i, s)))
            return jnp.concatenate(parts, axis=0)

        def from_sequence(value):
            blocks = value.reshape(seqs, length, width)
            result = jnp.zeros((seqs, length, width), value.dtype)
            for s in range(seqs):
                part = blocks[s]
                if s:
                    part = send(part, lambda i, s=s: shift_seq(i, -s))
                result = lax.dynamic_update_index_in_dim(result, part, (seq + s) % seqs, 0)
            return result

        x = to_sequence(tokens)
        first = to_sequence(first_values)
        cot = to_sequence(cotangent)

        docs_all = lax.all_gather(docs, "blk", axis=1, tiled=True)
        docs_row = pick(docs_all, seq)
        starts = jnp.sum((docs_row[None, :] < docs_row[:, None]).astype(jnp.int32), axis=1)
        starts = starts.reshape(nblk, length)
        base = jnp.arange(length, dtype=jnp.int32)
        blocks = [((seq - s) % seqs) * group + member for s in range(seqs)]
        qpos = jnp.concatenate([b * length + base for b in blocks])
        qstart = jnp.concatenate([pick(starts, b) for b in blocks])
        kpos = jnp.concatenate(
            [
                (((seq - s) % seqs) * group + (member - g) % group) * length + base
                for g in range(group)
                for s in range(seqs)
            ]
        )
        half = HEAD_DIM // 2
        inverse = 10000.0 ** (-jnp.arange(half, dtype=f32) / half)
        angles = qpos.astype(f32)[:, None] * inverse[None, :]
        cos_half, sin_half = jnp.cos(angles), jnp.sin(angles)
        cosine = jnp.concatenate([cos_half] * 4, axis=1)
        sines = jnp.concatenate([-sin_half, sin_half] * 2, axis=1)
        qpos, qstart, kpos = qpos[None, :], qstart[None, :], kpos[:, None]
        gain_a, gain_f = gain_attn[None, :], gain_ffn[None, :]

        normed, q, kv = project(x, gain_a, w_qkv, first, cosine, sines)
        kvs = [kv] + [send(kv, lambda i, g=g: shift_member(i, g)) for g in range(1, group)]
        attended, lse = attend(q, kvs, kpos, qpos, qstart)
        nffn, hidden4, acts4, out, grad_mid, grad_branch, grad_att = feed_forward(
            x, attended, w_out, gain_f, cot, w_gate, w_up, w_down
        )
        output = from_sequence(out)

        def share(value, e):
            edge = flip(value, e)
            return [value, edge, flip(value, 0), flip(edge, 0)]

        def share_quarters(value4, e):
            value = value4.reshape((2, 2) + value4.shape[1:])
            mine, theirs = pick(value, bit(e)), pick(value, 1 - bit(e))
            edge = flip(theirs, e)
            c = bit(0)
            return [
                pick(mine, c),
                pick(edge, c),
                flip(pick(mine, 1 - c), 0),
                flip(pick(edge, 1 - c), 0),
            ]

        def stage(value, device_bit, axis, last):
            b = bit(device_bit)
            got = flip(pick(value, 1 - b, axis), device_bit)
            total = pick(value, b, axis).astype(f32) + got.astype(f32)
            return total.astype(bf16)

        def reduce_columns(part, e):
            per = part.shape[0] // n
            value = part.reshape((2,) * nbits + (per, part.shape[1]))
            left = list(range(nbits - 1, -1, -1))
            order = [t for t in range(nbits - 1, blk_bits - 1, -1) if t != e]
            order += list(range(1, blk_bits))
            for t in order:
                axis = left.index(t)
                value = stage(value, t, axis, t == order[-1])
                left.pop(axis)
            b, c = bit(e), bit(0)
            keep, got = pick(value, b), flip(pick(value, 1 - b), e)
            low = jnp.where(b == 0, keep, got)
            high = jnp.where(b == 0, got, keep)
            both = jnp.stack([low, high])
            keep, got = pick(both, c, 1), flip(pick(both, 1 - c, 1), 0)
            low = jnp.where(c == 0, keep, got)
            high = jnp.where(c == 0, got, keep)
            return jnp.stack([low, high], axis=1).reshape(4, per, part.shape[1]).astype(f32)

        def reduce_rows(part):
            per = 4 * part.shape[0] // n
            value = part.reshape((2,) * (nbits - 2) + (per, part.shape[1]))
            left = list(range(nbits - 3, -1, -1))
            second = nbits - 2
            order = [(second, 0)]
            order += [(t, t) for t in range(nbits - 3, blk_bits - 1, -1)]
            order += [(t, t) for t in range(1, min(blk_bits, nbits - 2))]
            for device_bit, chunk_bit in order:
                axis = left.index(chunk_bit)
                value = stage(value, device_bit, axis, device_bit == order[-1][0])
                left.pop(axis)

            def swap(i):
                a, b = (i >> second) & 1, i & 1
                return i if a == b else i ^ (1 << second) ^ 1

            got = send(value, swap)
            return jnp.where(bit(second) == bit(0), value, got).astype(f32)

        down_part = outer(share_quarters(hidden4, high_e), share(cot, high_e))
        grad_down = reduce_rows(down_part)

        acts_part = outer(share(nffn, low_e), share_quarters(acts4, low_e))
        acts_done = reduce_columns(acts_part, low_e)
        quarter = ff // 4
        per = width // n

        def spread(value):
            return jnp.transpose(value, (1, 0, 2)).reshape(per, -1)

        grad_gate = spread(acts_done[:, :, :quarter])
        grad_up = spread(acts_done[:, :, quarter:])

        branch4 = jnp.transpose(grad_branch.reshape(rows, 4, width // 4), (1, 0, 2))
        out_part = outer(share(attended, high_e), share_quarters(branch4, high_e))
        grad_out = spread(reduce_columns(out_part, high_e))

        gq, gk, gv, other_k, other_v = attend_back(
            q, grad_att, kvs, lse, kpos, qpos, qstart, cosine, sines
        )
        got_k = [send(v, lambda i, g=g: shift_member(i, -g)) for g, v in enumerate(other_k, 1)]
        got_v = [send(v, lambda i, g=g: shift_member(i, -g)) for g, v in enumerate(other_v, 1)]
        packed, grad_first = grad_pack(gq, gk, gv, got_k, got_v, cosine, sines)
        grad_first_values = from_sequence(grad_first)
        grad_x = grad_inputs(packed, w_qkv, x, gain_a, grad_mid)
        grad_tokens = from_sequence(grad_x)

        pairs = width // LANES
        eighths = packed.reshape(2, 4, pairs // 8, rows, 3 * LANES)
        eighths = jnp.transpose(eighths, (0, 1, 3, 2, 4)).reshape(2, 4, rows, -1)
        done = []
        for color, e in enumerate((low_e, high_e)):
            part = outer(share(normed, e), share_quarters(eighths[color], e))
            done.append(reduce_columns(part, e))
        grad_qkv = jnp.concatenate(done, axis=0).reshape(8, per, pairs // 8, 3, LANES)
        grad_qkv = jnp.transpose(grad_qkv, (1, 3, 0, 2, 4)).reshape(per, 3 * width)

        def own(value):
            return lax.dynamic_slice_in_dim(value, index * per, per, 0)

        grad_gain_attn = jnp.sum(grad_qkv * own(w_qkv).astype(f32), axis=1) / own(gain_attn)
        grad_gain_ffn = (
            jnp.sum(
                grad_gate * own(w_gate).astype(f32) + grad_up * own(w_up).astype(f32), axis=1
            )
            / own(gain_ffn)
        )
        return (
            output,
            grad_tokens,
            grad_first_values,
            grad_qkv,
            grad_out,
            grad_gate,
            grad_up,
            grad_down,
            grad_gain_attn,
            grad_gain_ffn,
        )

    return shards


def solution(mesh):
    seq = P("dp", "blk", None)
    rows = P(AXES, None)
    vec = P(AXES)
    in_specs = (seq, seq, P("dp", "blk"), seq) + (P(),) * 7
    out_specs = (seq, seq, seq, rows, rows, rows, rows, rows, vec, vec)
    return jax.shard_map(
        build(mesh.shape["dp"], mesh.shape["blk"]),
        mesh=mesh,
        in_specs=in_specs,
        out_specs=out_specs,
        check_vma=False,
    )
```

```python
import functools

import jax
import jax.numpy as jnp
from jax import lax
from jax.experimental import pallas as pl
from jax.experimental.pallas import tpu as pltpu
from jax.sharding import PartitionSpec as P

HEAD_DIM = 64
LANES = 128
AXES = ("dp", "blk")
epsilon = 1e-06
score_scale = 0.125
cost_share = 0.3
bf16 = jnp.bfloat16
f32 = jnp.float32

NN = (((1,), (0,)), ((), ()))
NT = (((1,), (1,)), ((), ()))
TN = (((0,), (0,)), ((), ()))


def mm(a, b, dims):
    return lax.dot_general(a, b, dims, preferred_element_type=f32)


def sds(shape, dtype):
    return jax.ShapeDtypeStruct(shape, dtype)


def cost(flops, nbytes, trans=0):
    return pl.CostEstimate(
        flops=int(flops * cost_share), bytes_accessed=int(nbytes * cost_share), transcendentals=0
    )


def whole(shape):
    return pl.BlockSpec(shape, lambda *_: (0,) * len(shape))


def scalar():
    return pl.BlockSpec(memory_space=pltpu.SMEM)


def tie(*values):
    return lax.optimization_barrier(values)


def lane_half(shape):
    lane = lax.broadcasted_iota(jnp.int32, shape, len(shape) - 1)
    return (lane & (HEAD_DIM - 1)) < HEAD_DIM // 2


def turn(values):
    half = HEAD_DIM // 2
    return jnp.where(
        lane_half(values.shape),
        pltpu.roll(values, LANES - half, 1),
        pltpu.roll(values, half, 1),
    )


def head_mask(shape, head):
    lane = lax.broadcasted_iota(jnp.int32, shape, 1)
    return lane < HEAD_DIM if head == 0 else lane >= HEAD_DIM


def rotate_all(projected, cosine, sines):
    parts = []
    for i in range(projected.shape[1] // LANES):
        part = projected[:, i * LANES : (i + 1) * LANES]
        parts.append((part * cosine + turn(part) * sines).astype(bf16))
    return jnp.concatenate(parts, axis=1)


def query_key_body(nq, x_ref, gain_ref, w_ref, cos_ref, sin_ref, normed_ref, q_ref, k_ref):
    step = pl.program_id(0)

    @pl.when(step == 0)
    def _():
        inputs = x_ref[...].astype(f32)
        factor = lax.rsqrt(jnp.mean(inputs * inputs, axis=-1, keepdims=True) + epsilon)
        normed_ref[...] = (inputs * factor * gain_ref[...]).astype(bf16)

    rotated = rotate_all(mm(normed_ref[...], w_ref[...], NN), cos_ref[...], sin_ref[...])

    @pl.when(step < nq)
    def _():
        q_ref[...] = rotated

    @pl.when(step >= nq)
    def _():
        k_ref[...] = rotated


def query_key(x, gain, w_qkv, cosine, sines):
    rows, width = x.shape
    bn = 512
    nq = width // bn
    return pl.pallas_call(
        functools.partial(query_key_body, nq),
        grid=(2 * nq,),
        in_specs=[
            whole((rows, width)),
            whole((1, width)),
            pl.BlockSpec((width, bn), lambda j: (0, j)),
            whole((rows, LANES)),
            whole((rows, LANES)),
        ],
        out_specs=[
            whole((rows, width)),
            pl.BlockSpec((rows, bn), lambda j: (0, jnp.minimum(j, nq - 1))),
            pl.BlockSpec((rows, bn), lambda j: (0, jnp.maximum(j - nq, 0))),
        ],
        out_shape=[sds((rows, width), bf16)] * 3,
        cost_estimate=cost(4 * rows * width * width, 4 * width * width + 8 * rows * width),
        name="query_key",
    )(x, gain, w_qkv, cosine, sines)


def value_mix_body(normed_ref, w_ref, first_ref, out_ref):
    projected = mm(normed_ref[...], w_ref[...], NN)
    out_ref[...] = (0.5 * projected + 0.5 * first_ref[...].astype(f32)).astype(bf16)


def value_mix(normed, w_qkv, first):
    rows, width = normed.shape
    bn = 512
    nq = width // bn
    col = pl.BlockSpec((rows, bn), lambda j: (0, j))
    return pl.pallas_call(
        value_mix_body,
        grid=(nq,),
        in_specs=[whole((rows, width)), pl.BlockSpec((width, bn), lambda j: (0, 2 * nq + j)), col],
        out_specs=col,
        out_shape=sds((rows, width), bf16),
        cost_estimate=cost(2 * rows * width * width, 2 * width * width + 6 * rows * width),
        name="value_mix",
    )(normed, w_qkv, first)


def set_bias(bias_ref, kpos_ref, qpos_ref, qstart_ref):
    keys, qpos = kpos_ref[...], qpos_ref[...]
    allowed = (keys <= qpos) & (keys >= qstart_ref[...])
    bias_ref[...] = jnp.where(allowed, 0.0, -1e30)


def attend_body(slots, *refs):
    q_ref = refs[0]
    k_refs = refs[1 : 1 + slots]
    v_refs = refs[1 + slots : 1 + 2 * slots]
    kpos_ref, qpos_ref, qstart_ref, out_ref, lse_ref, bias_ref = refs[1 + 2 * slots :]

    @pl.when(pl.program_id(0) == 0)
    def _():
        set_bias(bias_ref, kpos_ref, qpos_ref, qstart_ref)

    queries = q_ref[...] * jnp.asarray(score_scale, bf16)
    keys = jnp.concatenate([r[...] for r in k_refs], axis=0)
    values = jnp.concatenate([r[...] for r in v_refs], axis=0)
    values_t = jnp.transpose(values)
    outs = []
    for head in range(2):
        own = jnp.where(head_mask(queries.shape, head), queries, jnp.zeros_like(queries))
        scores = mm(keys, own, NT) + bias_ref[...]
        top = jnp.max(scores, axis=0, keepdims=True)
        weights = jnp.exp(scores - top)
        total = jnp.sum(weights, axis=0, keepdims=True)
        probs = (weights * (1.0 / total)).astype(bf16)
        outs.append(mm(values_t[head * HEAD_DIM : (head + 1) * HEAD_DIM], probs, NN))
        lse_ref[0, head : head + 1, :] = top + jnp.log(total)
    out_ref[...] = jnp.transpose(jnp.concatenate(outs, axis=0)).astype(bf16)


def attend(q, ks, vs, kpos, qpos, qstart):
    rows, width = q.shape
    slots = len(ks)
    pairs = width // LANES
    keys = slots * rows
    col = pl.BlockSpec((rows, LANES), lambda i: (0, i))
    return pl.pallas_call(
        functools.partial(attend_body, slots),
        grid=(pairs,),
        in_specs=[col]
        + [col] * slots
        + [col] * slots
        + [whole((keys, 1)), whole((1, rows)), whole((1, rows))],
        out_specs=[col, pl.BlockSpec((1, 2, rows), lambda i: (i, 0, 0))],
        out_shape=[sds((rows, width), bf16), sds((pairs, 2, rows), f32)],
        scratch_shapes=[pltpu.VMEM((keys, rows), f32)],
        cost_estimate=cost(
            8 * pairs * rows * keys * LANES, 2 * rows * width * (2 + 2 * slots), 2 * pairs * rows * keys
        ),
        name="attend",
    )(q, *ks, *vs, kpos, qpos, qstart)


def attend_back_body(slots, *refs):
    q_ref, grad_ref = refs[:2]
    k_refs = refs[2 : 2 + slots]
    v_refs = refs[2 + slots : 2 + 2 * slots]
    lse_ref, kpos_ref, qpos_ref, qstart_ref, cos_ref, sin_ref = refs[2 + 2 * slots : 8 + 2 * slots]
    gq_ref, gk_ref, gv_ref = refs[8 + 2 * slots : 11 + 2 * slots]
    other_k = refs[11 + 2 * slots : 10 + 3 * slots]
    other_v = refs[10 + 3 * slots : 9 + 4 * slots]
    bias_ref = refs[-1]

    @pl.when(pl.program_id(0) == 0)
    def _():
        set_bias(bias_ref, kpos_ref, qpos_ref, qstart_ref)

    queries = q_ref[...] * jnp.asarray(score_scale, bf16)
    grads = grad_ref[...]
    keys = jnp.concatenate([r[...] for r in k_refs], axis=0)
    values = jnp.concatenate([r[...] for r in v_refs], axis=0)
    keys_t = jnp.transpose(keys)
    grad_values = grad_keys = None
    grad_q = []
    for head in range(2):
        mask = head_mask(queries.shape, head)
        own_q = jnp.where(mask, queries, jnp.zeros_like(queries))
        own_g = jnp.where(mask, grads, jnp.zeros_like(grads))
        scores = mm(keys, own_q, NT) + bias_ref[...]
        probs = jnp.exp(scores - lse_ref[0, head : head + 1, :])
        grad_probs = mm(values, own_g, NT)
        delta = jnp.sum(probs * grad_probs, axis=0, keepdims=True)
        grad_scores = (probs * (grad_probs - delta)).astype(bf16)
        part_v = mm(probs.astype(bf16), own_g, NN)
        part_k = mm(grad_scores, own_q, NN)
        grad_values = part_v if grad_values is None else grad_values + part_v
        grad_keys = part_k if grad_keys is None else grad_keys + part_k
        grad_q.append(mm(keys_t[head * HEAD_DIM : (head + 1) * HEAD_DIM], grad_scores, NN))
    grad_q = jnp.transpose(jnp.concatenate(grad_q, axis=0)) * score_scale
    gq_ref[...] = (grad_q * cos_ref[...] - turn(grad_q) * sin_ref[...]).astype(bf16)
    rows = q_ref.shape[0]
    gk_ref[...] = grad_keys[:rows]
    gv_ref[...] = grad_values[:rows]
    for slot in range(1, slots):
        other_k[slot - 1][...] = grad_keys[slot * rows : (slot + 1) * rows].astype(bf16)
        other_v[slot - 1][...] = grad_values[slot * rows : (slot + 1) * rows].astype(bf16)


def attend_back(q, grad, ks, vs, lse, kpos, qpos, qstart, cosine, sines):
    rows, width = q.shape
    slots = len(ks)
    pairs = width // LANES
    keys = slots * rows
    col = pl.BlockSpec((rows, LANES), lambda i: (0, i))
    outs = pl.pallas_call(
        functools.partial(attend_back_body, slots),
        grid=(pairs,),
        in_specs=[col, col]
        + [col] * slots
        + [col] * slots
        + [pl.BlockSpec((1, 2, rows), lambda i: (i, 0, 0))]
        + [whole((keys, 1)), whole((1, rows)), whole((1, rows))]
        + [whole((rows, LANES))] * 2,
        out_specs=[col] * (3 + 2 * (slots - 1)),
        out_shape=[sds((rows, width), bf16)]
        + [sds((rows, width), f32)] * 2
        + [sds((rows, width), bf16)] * (2 * (slots - 1)),
        scratch_shapes=[pltpu.VMEM((keys, rows), f32)],
        cost_estimate=cost(
            20 * pairs * rows * keys * LANES, 2 * rows * width * (7 + 4 * slots), 2 * pairs * rows * keys
        ),
        name="attend_back",
    )(q, grad, *ks, *vs, lse, kpos, qpos, qstart, cosine, sines)
    gq, gk, gv = outs[:3]
    return gq, gk, gv, outs[3 : 2 + slots], outs[2 + slots :]


def middle_body(x_ref, att_ref, wout_ref, gain_ref, mid_ref, nffn_ref):
    middle = x_ref[...].astype(f32) + mm(att_ref[...], wout_ref[...], NN)
    mid_ref[...] = middle
    factor = lax.rsqrt(jnp.mean(middle * middle, axis=-1, keepdims=True) + epsilon)
    nffn_ref[...] = (middle * factor * gain_ref[...]).astype(bf16)


def middle_norm(x, attended, w_out, gain):
    rows, width = x.shape
    return pl.pallas_call(
        middle_body,
        out_shape=[sds((rows, width), f32), sds((rows, width), bf16)],
        cost_estimate=cost(2 * rows * width * width, 2 * width * width + 10 * rows * width),
        name="middle_norm",
    )(x, attended, w_out, gain)


def store_half(edge, keep_ref, send_ref, half, offset, value):
    at = pl.ds(pl.multiple_of(offset * LANES, LANES), LANES)

    @pl.when(half == edge)
    def _():
        keep_ref[:, at] = value

    @pl.when(half != edge)
    def _():
        send_ref[:, at] = value


def ffn_acts_body(
    sizes,
    edge_ref,
    nffn_ref,
    cot_ref,
    wg_ref,
    wu_ref,
    wd_ref,
    hid_ref,
    gg_ref,
    gu_ref,
    hk_ref,
    hs_ref,
    ak_ref,
    as_ref,
    bk_ref,
    bs_ref,
):
    step = pl.program_id(0)
    block = wg_ref.shape[1]
    normed = nffn_ref[...]
    gate = mm(normed, wg_ref[...], NN)
    upward = mm(normed, wu_ref[...], NN)
    grad_hidden = mm(cot_ref[...], wd_ref[...], NT)
    sig = 1.0 / (1.0 + jnp.exp(-gate))
    silu = gate * sig
    hidden = (silu * upward).astype(bf16)
    grad_gate = (grad_hidden * upward * (sig * (1.0 + gate * (1.0 - sig)))).astype(bf16)
    grad_up = (grad_hidden * silu).astype(bf16)
    hid_ref[...] = hidden
    gg_ref[...] = grad_gate
    gu_ref[...] = grad_up
    per = block // LANES
    total, hid_half, a_half, b_half = sizes
    low_edge, high_edge = edge_ref[0], edge_ref[1]
    for i in range(per):
        at = slice(i * LANES, (i + 1) * LANES)
        lane_block = step * per + i
        store_half(
            high_edge, hk_ref, hs_ref, lane_block // hid_half, lane_block % hid_half, hidden[:, at]
        )
        for first, value in ((0, grad_gate), (total, grad_up)):
            place = lane_block + first
            piece = value[:, at]

            @pl.when(place < 2 * a_half)
            def _(place=place, piece=piece):
                store_half(low_edge, ak_ref, as_ref, place // a_half, place % a_half, piece)

            @pl.when(place >= 2 * a_half)
            def _(place=place, piece=piece):
                rest = place - 2 * a_half
                store_half(low_edge, bk_ref, bs_ref, rest // b_half, rest % b_half, piece)


def half_blocks(ff):
    total = ff // LANES
    a_half = (total + 1) // 2 + (total // 2) % 2
    return total, total // 2, a_half, total - a_half


def ffn_acts(edges, nffn, cot, w_gate, w_up, w_down):
    rows, width = nffn.shape
    ff = w_gate.shape[1]
    block = 256
    sizes = half_blocks(ff)
    _, hid_half, a_half, b_half = sizes
    full = whole((rows, width))
    col = pl.BlockSpec((rows, block), lambda j: (0, j))
    widths = [hid_half * LANES] * 2 + [a_half * LANES] * 2 + [b_half * LANES] * 2
    return pl.pallas_call(
        functools.partial(ffn_acts_body, sizes),
        grid=(ff // block,),
        in_specs=[
            scalar(),
            full,
            full,
            pl.BlockSpec((width, block), lambda j: (0, j)),
            pl.BlockSpec((width, block), lambda j: (0, j)),
            pl.BlockSpec((block, width), lambda j: (j, 0)),
        ],
        out_specs=[col] * 3 + [whole((rows, w)) for w in widths],
        out_shape=[sds((rows, ff), bf16)] * 3 + [sds((rows, w), bf16) for w in widths],
        cost_estimate=cost(6 * rows * width * ff, 6 * width * ff + 12 * rows * ff),
        name="ffn_acts",
    )(edges, nffn, cot, w_gate, w_up, w_down)


def ffn_back_body(
    steps,
    seqs,
    edge_ref,
    hid_ref,
    gg_ref,
    gu_ref,
    wg_ref,
    wu_ref,
    wd_ref,
    mid_ref,
    cot_ref,
    wout_ref,
    gain_ref,
    *refs,
):
    out_refs = refs[:seqs]
    gmid_ref, keep_ref, send_ref, gatt_ref, acc_s, gacc_s = refs[seqs:]
    step = pl.program_id(0)

    @pl.when(step == 0)
    def _():
        acc_s[...] = mid_ref[...]
        gacc_s[...] = jnp.zeros_like(gacc_s)

    acc_s[...] += mm(hid_ref[...], wd_ref[...], NN)
    gacc_s[...] += mm(gg_ref[...], wg_ref[...], NT) + mm(gu_ref[...], wu_ref[...], NT)

    @pl.when(step == steps - 1)
    def _():
        length = out_refs[0].shape[0]
        for s in range(seqs):
            out_refs[s][...] = acc_s[s * length : (s + 1) * length].astype(bf16)
        middle = mid_ref[...]
        factor = lax.rsqrt(jnp.mean(middle * middle, axis=-1, keepdims=True) + epsilon)
        scaled = gacc_s[...] * gain_ref[...]
        inner = jnp.mean(scaled * middle, axis=-1, keepdims=True)
        grad_middle = cot_ref[...].astype(f32) + factor * (
            scaled - middle * (factor * factor * inner)
        )
        gmid_ref[...] = grad_middle
        branch = grad_middle.astype(bf16)
        half = branch.shape[1] // 2

        @pl.when(edge_ref[0] == 0)
        def _():
            keep_ref[...] = branch[:, :half]
            send_ref[...] = branch[:, half:]

        @pl.when(edge_ref[0] != 0)
        def _():
            keep_ref[...] = branch[:, half:]
            send_ref[...] = branch[:, :half]

        gatt_ref[...] = mm(branch, wout_ref[...], NT).astype(bf16)


def ffn_back(seqs, edges, hidden, gg, gu, w_gate, w_up, w_down, middle, cot, w_out, gain):
    rows, width = cot.shape
    ff = w_gate.shape[1]
    block = 256
    steps = ff // block
    full = whole((rows, width))
    col = pl.BlockSpec((rows, block), lambda j: (0, j))
    part = whole((rows // seqs, width))
    half = whole((rows, width // 2))
    outs = pl.pallas_call(
        functools.partial(ffn_back_body, steps, seqs),
        grid=(steps,),
        in_specs=[
            scalar(),
            col,
            col,
            col,
            pl.BlockSpec((width, block), lambda j: (0, j)),
            pl.BlockSpec((width, block), lambda j: (0, j)),
            pl.BlockSpec((block, width), lambda j: (j, 0)),
            full,
            full,
            whole((width, width)),
            whole((1, width)),
        ],
        out_specs=[part] * seqs + [full, half, half, full],
        out_shape=[sds((rows // seqs, width), bf16)] * seqs
        + [
            sds((rows, width), f32),
            sds((rows, width // 2), bf16),
            sds((rows, width // 2), bf16),
            sds((rows, width), bf16),
        ],
        scratch_shapes=[pltpu.VMEM((rows, width), f32)] * 2,
        cost_estimate=cost(
            6 * rows * width * ff + 2 * rows * width * width,
            6 * width * ff + 2 * width * width + 6 * rows * ff + 20 * rows * width,
        ),
        name="ffn_back",
    )(edges, hidden, gg, gu, w_gate, w_up, w_down, middle, cot, w_out, gain)
    return outs[:seqs], outs[seqs:]


def grad_pack_body(seqs, received, pairs, edge_ref, *refs):
    gq_ref, gk_ref, gv_ref = refs[:3]
    other_k = refs[3 : 3 + received]
    other_v = refs[3 + received : 3 + 2 * received]
    cos_ref, sin_ref, packed_ref = refs[3 + 2 * received : 6 + 2 * received]
    first_refs = refs[6 + 2 * received : 6 + 2 * received + seqs]
    xk_ref, xs_ref, yk_ref, ys_ref = refs[6 + 2 * received + seqs :]
    step = pl.program_id(0)
    grad_k, grad_v = gk_ref[...], gv_ref[...]
    for r in other_k:
        grad_k = grad_k + r[...].astype(f32)
    for r in other_v:
        grad_v = grad_v + r[...].astype(f32)
    grad_k = (grad_k * cos_ref[...] - turn(grad_k) * sin_ref[...]).astype(bf16)
    grad_v = (0.5 * grad_v).astype(bf16)
    length = first_refs[0].shape[0]
    for s in range(seqs):
        first_refs[s][...] = grad_v[s * length : (s + 1) * length]
    packed = jnp.concatenate([gq_ref[...], grad_k, grad_v], axis=1)
    packed_ref[0] = packed
    quarter = pairs // 4
    part = step // quarter
    at = pl.ds(pl.multiple_of((step % quarter) * packed.shape[1], LANES), packed.shape[1])
    low_edge, high_edge = edge_ref[0], edge_ref[1]
    for color, edge, keep_ref, send_ref in (
        (0, low_edge, xk_ref, xs_ref),
        (1, high_edge, yk_ref, ys_ref),
    ):

        @pl.when(part == 2 * color + edge)
        def _():
            keep_ref[:, at] = packed

        @pl.when(part == 2 * color + 1 - edge)
        def _():
            send_ref[:, at] = packed


def grad_pack(seqs, edges, gq, gk, gv, other_k, other_v, cosine, sines):
    rows, width = gq.shape
    pairs = width // LANES
    received = len(other_k)
    col = pl.BlockSpec((rows, LANES), lambda i: (0, i))
    part = pl.BlockSpec((rows // seqs, LANES), lambda i: (0, i))
    quarter = (rows, pairs // 4 * 3 * LANES)
    outs = pl.pallas_call(
        functools.partial(grad_pack_body, seqs, received, pairs),
        grid=(pairs,),
        in_specs=[scalar()] + [col] * (3 + 2 * received) + [whole((rows, LANES))] * 2,
        out_specs=[pl.BlockSpec((1, rows, 3 * LANES), lambda i: (i, 0, 0))]
        + [part] * seqs
        + [whole(quarter)] * 4,
        out_shape=[sds((pairs, rows, 3 * LANES), bf16)]
        + [sds((rows // seqs, width), bf16)] * seqs
        + [sds(quarter, bf16)] * 4,
        cost_estimate=cost(20 * rows * width, 2 * rows * width * 12),
        name="grad_pack",
    )(edges, gq, gk, gv, *other_k, *other_v, cosine, sines)
    return outs[0], outs[1 : 1 + seqs], outs[1 + seqs :]


def grad_inputs_body(pairs, seqs, packed_ref, wq_ref, wk_ref, wv_ref, x_ref, gain_ref, gmid_ref, *refs):
    out_refs, acc_s = refs[:seqs], refs[seqs]
    step = pl.program_id(0)

    @pl.when(step == 0)
    def _():
        acc_s[...] = jnp.zeros_like(acc_s)

    weights = jnp.concatenate([wq_ref[...], wk_ref[...], wv_ref[...]], axis=1)
    acc_s[...] += mm(packed_ref[0], weights, NT)

    @pl.when(step == pairs - 1)
    def _():
        inputs = x_ref[...].astype(f32)
        factor = lax.rsqrt(jnp.mean(inputs * inputs, axis=-1, keepdims=True) + epsilon)
        scaled = acc_s[...] * gain_ref[...]
        inner = jnp.mean(scaled * inputs, axis=-1, keepdims=True)
        grads = gmid_ref[...] + factor * (scaled - inputs * (factor * factor * inner))
        grads = grads.astype(bf16)
        length = out_refs[0].shape[0]
        for s in range(seqs):
            out_refs[s][...] = grads[s * length : (s + 1) * length]


def grad_inputs(seqs, packed, w_qkv, x, gain, grad_middle):
    rows, width = x.shape
    pairs = width // LANES
    full = whole((rows, width))
    return pl.pallas_call(
        functools.partial(grad_inputs_body, pairs, seqs),
        grid=(pairs,),
        in_specs=[
            pl.BlockSpec((1, rows, 3 * LANES), lambda i: (i, 0, 0)),
            pl.BlockSpec((width, LANES), lambda i: (0, i)),
            pl.BlockSpec((width, LANES), lambda i: (0, pairs + i)),
            pl.BlockSpec((width, LANES), lambda i: (0, 2 * pairs + i)),
            full,
            whole((1, width)),
            full,
        ],
        out_specs=[whole((rows // seqs, width))] * seqs,
        out_shape=[sds((rows // seqs, width), bf16)] * seqs,
        scratch_shapes=[pltpu.VMEM((rows, width), f32)],
        cost_estimate=cost(6 * rows * width * width, 6 * width * width + 16 * rows * width),
        name="grad_inputs",
    )(packed, w_qkv, w_qkv, w_qkv, x, gain, grad_middle)


def place_body(seqs, shift_ref, *refs):
    out_ref = refs[seqs]
    for j in range(seqs):
        for s in range(seqs):

            @pl.when(lax.rem(shift_ref[0] + s, seqs) == j)
            def _(j=j, s=s):
                out_ref[j] = refs[s][...]


def place(parts, seq):
    seqs = len(parts)
    length, width = parts[0].shape
    return pl.pallas_call(
        functools.partial(place_body, seqs),
        in_specs=[scalar()] + [pl.BlockSpec(memory_space=pltpu.VMEM)] * seqs,
        out_specs=pl.BlockSpec(memory_space=pltpu.VMEM),
        out_shape=sds((seqs, length, width), parts[0].dtype),
        cost_estimate=cost(0, 4 * seqs * length * width),
        name="place",
    )(seq[None], *parts)


def outer_body(counts, per, core_ref, *refs):
    keep_ref, send_ref = refs[-2:]
    column = at = 0
    core = core_ref[0]
    for count in counts:
        lefts, rights = refs[at : at + count], refs[at + count : at + 2 * count]
        at += 2 * count
        total = None
        for left, right in zip(lefts, rights):
            part = mm(left[...], right[...], TN)
            total = part if total is None else total + part
        wide = total.shape[1]
        cut = slice(column, column + wide)
        column += wide
        total = total.astype(bf16)
        for i in range(total.shape[0] // (2 * per)):
            even = total[2 * i * per : (2 * i + 1) * per]
            odd = total[(2 * i + 1) * per : (2 * i + 2) * per]

            @pl.when(core == 0)
            def _(i=i, even=even, odd=odd, cut=cut):
                keep_ref[i, :, cut] = even
                send_ref[i, :, cut] = odd

            @pl.when(core != 0)
            def _(i=i, even=even, odd=odd, cut=cut):
                keep_ref[i, :, cut] = odd
                send_ref[i, :, cut] = even


def outer(core, per, *groups):
    rows, height = groups[0][0][0].shape
    width = sum(rights[0].shape[1] for _, rights in groups)
    block = 256 if height % 256 == 0 else height
    specs, args, flops = [], [], 0
    for lefts, rights in groups:
        wide = rights[0].shape[1]
        specs += [pl.BlockSpec((rows, block), lambda i: (0, i))] * len(lefts)
        specs += [whole((rows, wide))] * len(rights)
        args += [*lefts, *rights]
        flops += 2 * len(lefts) * rows * height * wide
    out_spec = pl.BlockSpec((block // (2 * per), per, width), lambda i: (i, 0, 0))
    return pl.pallas_call(
        functools.partial(outer_body, [len(lefts) for lefts, _ in groups], per),
        grid=(height // block,),
        in_specs=[scalar()] + specs,
        out_specs=[out_spec] * 2,
        out_shape=[sds((height // (2 * per), per, width), bf16)] * 2,
        cost_estimate=cost(flops, 2 * (sum(a.size for a in args) + height * width)),
        name="outer",
    )(core[None], *args)


def build(ndp, nblk):
    n = ndp * nblk
    nbits = n.bit_length() - 1
    blk_bits = nblk.bit_length() - 1
    if (1 << nbits) != n or (1 << blk_bits) != nblk:
        raise ValueError("mesh sizes")
    low_e, high_e = blk_bits, nbits - 1

    def send(value, target):
        pairs = [(i, target(i)) for i in range(n)]
        return lax.ppermute(value, AXES, pairs)

    def flip(value, bit):
        return send(value, lambda i: i ^ (1 << bit))

    def pick(value, index, axis=0):
        return lax.dynamic_index_in_dim(value, index, axis, keepdims=False)

    def shards(
        tokens, first_values, docs, cotangent, w_qkv, w_out, w_gate, w_up, w_down, gain_attn, gain_ffn
    ):
        seqs, length, width = tokens.shape
        ff = w_gate.shape[1]
        rows = seqs * length
        group = nblk // seqs
        blk = lax.axis_index("blk")
        index = lax.axis_index("dp") * nblk + blk
        seq, member = blk // group, blk % group

        def bit(t):
            return (index >> t) & 1

        core = bit(0)
        edges = jnp.stack([bit(low_e), bit(high_e)])

        def shift_seq(i, s):
            base, b = i - i % nblk, i % nblk
            return base + ((b // group + s) % seqs) * group + b % group

        def shift_member(i, s):
            base, b = i - i % nblk, i % nblk
            return base + (b // group) * group + (b % group + s) % group

        def to_sequence(value):
            parts = [pick(value, seq)]
            for s in range(1, seqs):
                out = pick(value, (seq + s) % seqs)
                parts.append(send(out, lambda i, s=s: shift_seq(i, s)))
            return parts

        def from_sequence(blocks):
            return [
                part if s == 0 else send(part, lambda i, s=s: shift_seq(i, -s))
                for s, part in enumerate(blocks)
            ]

        def others(value):
            return [send(value, lambda i, g=g: shift_member(i, g)) for g in range(1, group)]

        marks = jnp.pad(docs[:, None, :].astype(bf16), ((0, 0), (0, 7), (0, width - length)))
        token_parts = to_sequence(jnp.concatenate([tokens, marks], axis=1))
        first_parts = to_sequence(first_values)
        cot_parts = to_sequence(cotangent)
        x = jnp.concatenate([p[:length] for p in token_parts], axis=0)
        qdocs = jnp.concatenate([p[length, :length] for p in token_parts]).astype(jnp.int32)[None]

        base = jnp.arange(length, dtype=jnp.int32)
        qpos = jnp.concatenate(
            [(((seq - s) % seqs) * group + member) * length + base for s in range(seqs)]
        )
        kpos = jnp.concatenate(
            [
                (((seq - s) % seqs) * group + (member - g) % group) * length + base
                for g in range(group)
                for s in range(seqs)
            ]
        )
        half = HEAD_DIM // 2
        inverse = 10000.0 ** (-jnp.arange(half, dtype=f32) / half)
        angles = qpos.astype(f32)[:, None] * inverse[None, :]
        cos_half, sin_half = jnp.cos(angles), jnp.sin(angles)
        cosine = jnp.concatenate([cos_half] * 4, axis=1)
        sines = jnp.concatenate([-sin_half, sin_half] * 2, axis=1)
        qpos, kpos = qpos[None, :], kpos[:, None]
        gain_a, gain_f = gain_attn[None, :], gain_ffn[None, :]

        x, cosine, sines, qpos, kpos = tie(x, cosine, sines, qpos, kpos)
        normed, q, k = query_key(x, gain_a, w_qkv, cosine, sines)
        other_docs = others(qdocs)
        ks = [k] + others(k)
        normed_x = flip(normed, low_e)
        normed_y = flip(normed, high_e)
        all_docs = jnp.concatenate([qdocs] + other_docs, axis=1)
        qstart = jnp.sum((all_docs[0][:, None] < qdocs).astype(jnp.int32), axis=0, keepdims=True)
        first = jnp.concatenate(first_parts, axis=0)
        ks, first, qstart = tie(ks, first, qstart)
        v = value_mix(normed, w_qkv, first)
        vs = [v] + others(v)
        attended, lse = attend(q, ks, vs, kpos, qpos, qstart)
        attended, normed_x, normed_y, cot_parts = tie(attended, normed_x, normed_y, cot_parts)
        cot = jnp.concatenate(cot_parts, axis=0)
        attended_x = flip(attended, low_e)
        cot_y = flip(cot, high_e)
        middle, nffn = middle_norm(x, attended, w_out, gain_f)
        nffn_x = flip(nffn, low_e)
        hidden, gg, gu, hk, hs, ak, a_s, bk, bs = ffn_acts(edges, nffn, cot, w_gate, w_up, w_down)
        hidden, gg, gu, hs, a_s, bs, attended_x, cot_y = tie(
            hidden, gg, gu, hs, a_s, bs, attended_x, cot_y
        )
        h_y = flip(hs, high_e)
        a_x = flip(a_s, low_e)
        out_blocks, (grad_mid, gbk, gbs, grad_att) = ffn_back(
            seqs, edges, hidden, gg, gu, w_gate, w_up, w_down, middle, cot, w_out, gain_f
        )
        out_blocks, gbs, grad_att, nffn_x = tie(out_blocks, gbs, grad_att, nffn_x)
        out_parts = from_sequence(out_blocks)
        gq, gk, gv, other_k, other_v = attend_back(
            q, grad_att, ks, vs, lse, kpos, qpos, qstart, cosine, sines
        )
        gq, gk, gv, other_k, other_v, out_parts, h_y = tie(
            gq, gk, gv, other_k, other_v, out_parts, h_y
        )
        b_x = flip(bs, low_e)
        gb_x = flip(gbs, low_e)
        got_k = [send(v, lambda i, g=g: shift_member(i, -g)) for g, v in enumerate(other_k, 1)]
        got_v = [send(v, lambda i, g=g: shift_member(i, -g)) for g, v in enumerate(other_v, 1)]
        per_down = ff // n
        per = width // n
        dk, ds = outer(core, per_down, ([hk, h_y], [cot, cot_y]))
        dk, ds, got_k, got_v = tie(dk, ds, got_k, got_v)
        d_c = flip(ds, 0)
        packed, first_blocks, (qxk, qxs, qyk, qys) = grad_pack(
            seqs, edges, gq, gk, gv, got_k, got_v, cosine, sines
        )
        q_x = flip(qxs, low_e)
        q_y = flip(qys, high_e)

        def reduce_rows(keep, got, top, skip):
            dims = (2,) * top + keep.shape[1:]
            value = keep.reshape(dims).astype(f32) + got.reshape(dims).astype(f32)
            left = list(range(top, 0, -1))
            order = [t for t in left if t >= blk_bits and t != skip]
            order += list(range(1, min(blk_bits, top + 1)))
            for t in order:
                axis = left.index(t)
                b = bit(t)
                other = flip(pick(value, 1 - b, axis).astype(bf16), t)
                value = pick(value, b, axis) + other.astype(f32)
                left.pop(axis)
            return value

        def reduce_columns(keep, got, e):
            value = reduce_rows(keep, got, nbits - 1, e)
            b = bit(e)
            mine = pick(value, b)
            other = flip(pick(value, 1 - b).astype(bf16), e).astype(f32)
            return jnp.stack([jnp.where(b == 0, mine, other), jnp.where(b == 0, other, mine)])

        ak2, as2 = outer(core, per, ([nffn, nffn_x], [ak, a_x]))
        a_c = flip(as2, 0)
        grad_down = reduce_rows(dk, d_c, nbits - 2, -1)
        a_done = reduce_columns(ak2, a_c, low_e)
        bk2, bs2 = outer(
            core, per, ([nffn, nffn_x], [bk, b_x]), ([attended, attended_x], [gbk, gb_x])
        )
        b_c = flip(bs2, 0)
        b_done = reduce_columns(bk2, b_c, low_e)
        grad_x = grad_inputs(seqs, packed, w_qkv, x, gain_a, grad_mid)
        qxk2, qxs2 = outer(core, per, ([normed, normed_x], [qxk, q_x]))
        qyk2, qys2 = outer(core, per, ([normed, normed_y], [qyk, q_y]))
        qx_c, qy_c = flip(qxs2, 0), flip(qys2, 0)
        qx_done = reduce_columns(qxk2, qx_c, low_e)
        qy_done = reduce_columns(qyk2, qy_c, high_e)
        first_out = from_sequence(first_blocks)
        token_out = from_sequence(grad_x)
        output = place(out_parts, seq)
        grad_first_values = place(first_out, seq)
        grad_tokens = place(token_out, seq)

        _, _, a_half, b_half = half_blocks(ff)
        b_wide = b_half * LANES
        acts = jnp.concatenate(
            [a_done[0], a_done[1], b_done[0, :, :b_wide], b_done[1, :, :b_wide]], axis=1
        )
        grad_gate, grad_up = acts[:, :ff], acts[:, ff:]
        grad_out = jnp.concatenate([b_done[0, :, b_wide:], b_done[1, :, b_wide:]], axis=1)
        pairs = width // LANES
        grad_qkv = jnp.concatenate([qx_done, qy_done], axis=0)
        grad_qkv = grad_qkv.reshape(4, per, pairs // 4, 3, LANES)
        grad_qkv = jnp.transpose(grad_qkv, (1, 3, 0, 2, 4)).reshape(per, 3 * width)

        def own(value):
            return lax.dynamic_slice_in_dim(value, index * per, per, 0)

        grad_gain_attn = jnp.sum(grad_qkv * own(w_qkv).astype(f32), axis=1) / own(gain_attn)
        grad_gain_ffn = (
            jnp.sum(
                grad_gate * own(w_gate).astype(f32) + grad_up * own(w_up).astype(f32), axis=1
            )
            / own(gain_ffn)
        )
        return (
            output,
            grad_tokens,
            grad_first_values,
            grad_qkv,
            grad_out,
            grad_gate,
            grad_up,
            grad_down,
            grad_gain_attn,
            grad_gain_ffn,
        )

    return shards


def solution(mesh):
    seq = P("dp", "blk", None)
    rows = P(AXES, None)
    vec = P(AXES)
    in_specs = (seq, seq, P("dp", "blk"), seq) + (P(),) * 7
    out_specs = (seq, seq, seq, rows, rows, rows, rows, rows, vec, vec)
    return jax.shard_map(
        build(mesh.shape["dp"], mesh.shape["blk"]),
        mesh=mesh,
        in_specs=in_specs,
        out_specs=out_specs,
        check_vma=False,
    )
```

```python
import functools

import jax
import jax.numpy as jnp
from jax import lax
from jax.experimental import pallas as pl
from jax.experimental.pallas import tpu as pltpu
from jax.sharding import PartitionSpec as P

HEAD_DIM = 64
LANES = 128
AXES = ("dp", "blk")
epsilon = 1e-06
score_scale = 0.125
cost_share = 0.3
VMEM_LIMIT = 16 << 20
bf16 = jnp.bfloat16
f32 = jnp.float32

NN = (((1,), (0,)), ((), ()))
NT = (((1,), (1,)), ((), ()))
TN = (((0,), (0,)), ((), ()))


def mm(a, b, dims):
    return lax.dot_general(a, b, dims, preferred_element_type=f32)


def sds(shape, dtype):
    return jax.ShapeDtypeStruct(shape, dtype)


def cost(flops, nbytes, trans=0):
    return pl.CostEstimate(
        flops=int(flops * cost_share), bytes_accessed=int(nbytes * cost_share), transcendentals=0
    )


def whole(shape):
    return pl.BlockSpec(shape, lambda *_: (0,) * len(shape))


def scalar():
    return pl.BlockSpec(memory_space=pltpu.SMEM)


RESIDENT = pl.BlockSpec(memory_space=pltpu.VMEM)


def lanes(step, width):
    return pl.ds(pl.multiple_of(step * width, width), width)


def resident_call(body, ins, outs, name, flops, scratch=(), scalars=1):
    nbytes = sum(a.size * a.dtype.itemsize for a in (*ins, *outs))
    return pl.pallas_call(
        body,
        in_specs=[scalar()] * scalars + [RESIDENT] * (len(ins) - scalars),
        out_specs=[RESIDENT] * len(outs),
        out_shape=list(outs),
        scratch_shapes=list(scratch),
        compiler_params=pltpu.CompilerParams(vmem_limit_bytes=VMEM_LIMIT),
        cost_estimate=cost(flops, nbytes),
        name=name,
    )(*ins)


def tie(*values):
    return lax.optimization_barrier(values)


def lane_half(shape):
    lane = lax.broadcasted_iota(jnp.int32, shape, len(shape) - 1)
    return (lane & (HEAD_DIM - 1)) < HEAD_DIM // 2


def turn(values):
    half = HEAD_DIM // 2
    return jnp.where(
        lane_half(values.shape),
        pltpu.roll(values, LANES - half, 1),
        pltpu.roll(values, half, 1),
    )


def head_mask(shape, head):
    lane = lax.broadcasted_iota(jnp.int32, shape, 1)
    return lane < HEAD_DIM if head == 0 else lane >= HEAD_DIM


def rotate_all(projected, cosine, sines):
    parts = []
    for i in range(projected.shape[1] // LANES):
        part = projected[:, i * LANES : (i + 1) * LANES]
        parts.append((part * cosine + turn(part) * sines).astype(bf16))
    return jnp.concatenate(parts, axis=1)


def query_key_body(x_ref, gain_ref, w_ref, cos_ref, sin_ref, normed_ref, q_ref, k_ref):
    inputs = x_ref[...].astype(f32)
    factor = lax.rsqrt(jnp.mean(inputs * inputs, axis=-1, keepdims=True) + epsilon)
    normed = (inputs * factor * gain_ref[...]).astype(bf16)
    normed_ref[...] = normed
    width = q_ref.shape[1]
    block = 256
    for j in range(2 * width // block):
        at = slice(j * block, (j + 1) * block)
        rotated = rotate_all(mm(normed, w_ref[:, at], NN), cos_ref[...], sin_ref[...])
        if j * block < width:
            q_ref[:, at] = rotated
        else:
            k_ref[:, slice(j * block - width, (j + 1) * block - width)] = rotated


def query_key(x, gain, w_qkv, cosine, sines):
    rows, width = x.shape
    return resident_call(
        query_key_body,
        (x, gain, w_qkv, cosine, sines),
        [sds((rows, width), bf16)] * 3,
        "query_key",
        4 * rows * width * width,
        scalars=0,
    )


def value_mix_body(normed_ref, w_ref, first_ref, out_ref):
    width = out_ref.shape[1]
    block = 256
    for j in range(width // block):
        at = slice(j * block, (j + 1) * block)
        projected = mm(normed_ref[...], w_ref[:, 2 * width + j * block : 2 * width + (j + 1) * block], NN)
        out_ref[:, at] = (0.5 * projected + 0.5 * first_ref[:, at].astype(f32)).astype(bf16)


def value_mix(normed, w_qkv, first):
    rows, width = normed.shape
    return resident_call(
        value_mix_body,
        (normed, w_qkv, first),
        [sds((rows, width), bf16)],
        "value_mix",
        2 * rows * width * width,
        scalars=0,
    )[0]


def set_bias(bias_ref, kpos_ref, qpos_ref, qstart_ref):
    keys, qpos = kpos_ref[...], qpos_ref[...]
    allowed = (keys <= qpos) & (keys >= qstart_ref[...])
    bias_ref[...] = jnp.where(allowed, 0.0, -1e30)


def attend_body(slots, *refs):
    q_ref = refs[0]
    k_refs = refs[1 : 1 + slots]
    v_refs = refs[1 + slots : 1 + 2 * slots]
    kpos_ref, qpos_ref, qstart_ref, out_ref, lse_ref, bias_ref = refs[1 + 2 * slots :]

    @pl.when(pl.program_id(0) == 0)
    def _():
        set_bias(bias_ref, kpos_ref, qpos_ref, qstart_ref)

    queries = q_ref[...] * jnp.asarray(score_scale, bf16)
    keys = jnp.concatenate([r[...] for r in k_refs], axis=0)
    values = jnp.concatenate([r[...] for r in v_refs], axis=0)
    values_t = jnp.transpose(values)
    outs = []
    for head in range(2):
        own = jnp.where(head_mask(queries.shape, head), queries, jnp.zeros_like(queries))
        scores = mm(keys, own, NT) + bias_ref[...]
        top = jnp.max(scores, axis=0, keepdims=True)
        weights = jnp.exp(scores - top)
        total = jnp.sum(weights, axis=0, keepdims=True)
        probs = (weights * (1.0 / total)).astype(bf16)
        outs.append(mm(values_t[head * HEAD_DIM : (head + 1) * HEAD_DIM], probs, NN))
        lse_ref[0, head : head + 1, :] = top + jnp.log(total)
    out_ref[...] = jnp.transpose(jnp.concatenate(outs, axis=0)).astype(bf16)


def attend(q, ks, vs, kpos, qpos, qstart):
    rows, width = q.shape
    slots = len(ks)
    pairs = width // LANES
    keys = slots * rows
    col = pl.BlockSpec((rows, LANES), lambda i: (0, i))
    return pl.pallas_call(
        functools.partial(attend_body, slots),
        grid=(pairs,),
        in_specs=[col]
        + [col] * slots
        + [col] * slots
        + [whole((keys, 1)), whole((1, rows)), whole((1, rows))],
        out_specs=[col, pl.BlockSpec((1, 2, rows), lambda i: (i, 0, 0))],
        out_shape=[sds((rows, width), bf16), sds((pairs, 2, rows), f32)],
        scratch_shapes=[pltpu.VMEM((keys, rows), f32)],
        compiler_params=pltpu.CompilerParams(vmem_limit_bytes=VMEM_LIMIT),
        cost_estimate=cost(
            8 * pairs * rows * keys * LANES, 2 * rows * width * (2 + 2 * slots), 2 * pairs * rows * keys
        ),
        name="attend",
    )(q, *ks, *vs, kpos, qpos, qstart)


def attend_back_body(slots, *refs):
    q_ref, grad_ref = refs[:2]
    k_refs = refs[2 : 2 + slots]
    v_refs = refs[2 + slots : 2 + 2 * slots]
    lse_ref, kpos_ref, qpos_ref, qstart_ref, cos_ref, sin_ref = refs[2 + 2 * slots : 8 + 2 * slots]
    gq_ref, gk_ref, gv_ref = refs[8 + 2 * slots : 11 + 2 * slots]
    other_refs = refs[11 + 2 * slots : 10 + 3 * slots]
    bias_ref = refs[-1]

    @pl.when(pl.program_id(0) == 0)
    def _():
        set_bias(bias_ref, kpos_ref, qpos_ref, qstart_ref)

    queries = q_ref[...] * jnp.asarray(score_scale, bf16)
    grads = grad_ref[...]
    keys = jnp.concatenate([r[...] for r in k_refs], axis=0)
    values = jnp.concatenate([r[...] for r in v_refs], axis=0)
    keys_t = jnp.transpose(keys)
    grad_values = grad_keys = None
    grad_q = []
    for head in range(2):
        mask = head_mask(queries.shape, head)
        own_q = jnp.where(mask, queries, jnp.zeros_like(queries))
        own_g = jnp.where(mask, grads, jnp.zeros_like(grads))
        scores = mm(keys, own_q, NT) + bias_ref[...]
        probs = jnp.exp(scores - lse_ref[0, head : head + 1, :])
        grad_probs = mm(values, own_g, NT)
        delta = jnp.sum(probs * grad_probs, axis=0, keepdims=True)
        grad_scores = (probs * (grad_probs - delta)).astype(bf16)
        part_v = mm(probs.astype(bf16), own_g, NN)
        part_k = mm(grad_scores, own_q, NN)
        grad_values = part_v if grad_values is None else grad_values + part_v
        grad_keys = part_k if grad_keys is None else grad_keys + part_k
        grad_q.append(mm(keys_t[head * HEAD_DIM : (head + 1) * HEAD_DIM], grad_scores, NN))
    grad_q = jnp.transpose(jnp.concatenate(grad_q, axis=0)) * score_scale
    gq_ref[...] = (grad_q * cos_ref[...] - turn(grad_q) * sin_ref[...]).astype(bf16)
    rows = q_ref.shape[0]
    gk_ref[...] = grad_keys[:rows]
    gv_ref[...] = grad_values[:rows]
    for slot in range(1, slots):
        other_refs[slot - 1][0] = grad_keys[slot * rows : (slot + 1) * rows].astype(bf16)
        other_refs[slot - 1][1] = grad_values[slot * rows : (slot + 1) * rows].astype(bf16)


def attend_back(q, grad, ks, vs, lse, kpos, qpos, qstart, cosine, sines):
    rows, width = q.shape
    slots = len(ks)
    pairs = width // LANES
    keys = slots * rows
    col = pl.BlockSpec((rows, LANES), lambda i: (0, i))
    outs = pl.pallas_call(
        functools.partial(attend_back_body, slots),
        grid=(pairs,),
        in_specs=[col, col]
        + [col] * slots
        + [col] * slots
        + [pl.BlockSpec((1, 2, rows), lambda i: (i, 0, 0))]
        + [whole((keys, 1)), whole((1, rows)), whole((1, rows))]
        + [whole((rows, LANES))] * 2,
        out_specs=[col] * 3 + [pl.BlockSpec((2, rows, LANES), lambda i: (0, 0, i))] * (slots - 1),
        out_shape=[sds((rows, width), bf16)]
        + [sds((rows, width), f32)] * 2
        + [sds((2, rows, width), bf16)] * (slots - 1),
        scratch_shapes=[pltpu.VMEM((keys, rows), f32)],
        compiler_params=pltpu.CompilerParams(vmem_limit_bytes=VMEM_LIMIT),
        cost_estimate=cost(
            20 * pairs * rows * keys * LANES, 2 * rows * width * (7 + 4 * slots), 2 * pairs * rows * keys
        ),
        name="attend_back",
    )(q, grad, *ks, *vs, lse, kpos, qpos, qstart, cosine, sines)
    return (*outs[:3], outs[3:])


def middle_body(x_ref, att_ref, wout_ref, gain_ref, mid_ref, nffn_ref):
    middle = x_ref[...].astype(f32) + mm(att_ref[...], wout_ref[...], NN)
    mid_ref[...] = middle
    factor = lax.rsqrt(jnp.mean(middle * middle, axis=-1, keepdims=True) + epsilon)
    nffn_ref[...] = (middle * factor * gain_ref[...]).astype(bf16)


def middle_norm(x, attended, w_out, gain):
    rows, width = x.shape
    return resident_call(
        middle_body,
        (x, attended, w_out, gain),
        [sds((rows, width), f32), sds((rows, width), bf16)],
        "middle_norm",
        2 * rows * width * width,
        scalars=0,
    )


def ffn_acts_body(
    sizes,
    edge_ref,
    nffn_ref,
    cot_ref,
    wg_ref,
    wu_ref,
    wd_ref,
    hid_ref,
    gg_ref,
    gu_ref,
    hk_ref,
    hs_ref,
    ak_ref,
    as_ref,
    bk_ref,
    bs_ref,
):
    total, hid_half, a_half, b_half = sizes
    block = 256
    per = block // LANES
    for step in range(total // per):
        at = slice(step * block, (step + 1) * block)
        gate = mm(nffn_ref[...], wg_ref[:, at], NN)
        upward = mm(nffn_ref[...], wu_ref[:, at], NN)
        grad_hidden = mm(cot_ref[...], wd_ref[at, :], NT)
        sig = 1.0 / (1.0 + jnp.exp(-gate))
        silu = gate * sig
        hid_ref[:, at] = (silu * upward).astype(bf16)
        gg_ref[:, at] = (grad_hidden * upward * (sig * (1.0 + gate * (1.0 - sig)))).astype(bf16)
        gu_ref[:, at] = (grad_hidden * silu).astype(bf16)

    low_edge, high_edge = edge_ref[0], edge_ref[1]

    def halves(edge, keep_ref, send_ref, size, places):
        for half in range(2):
            runs = []
            for offset in range(size):
                source, start = places[half * size + offset]
                if runs and runs[-1][0] is source and runs[-1][2] == start:
                    runs[-1][2] += 1
                else:
                    runs.append([source, start, start + 1, offset])
            for source, start, stop, offset in runs:
                src = slice(start * LANES, stop * LANES)
                dst = slice(offset * LANES, (offset + stop - start) * LANES)

                @pl.when(edge == half)
                def _(source=source, src=src, dst=dst):
                    keep_ref[:, dst] = source[:, src]

                @pl.when(edge != half)
                def _(source=source, src=src, dst=dst):
                    send_ref[:, dst] = source[:, src]

    acts = [(gg_ref, i) for i in range(total)] + [(gu_ref, i) for i in range(total)]
    halves(high_edge, hk_ref, hs_ref, hid_half, [(hid_ref, i) for i in range(total)])
    halves(low_edge, ak_ref, as_ref, a_half, acts[: 2 * a_half])
    halves(low_edge, bk_ref, bs_ref, b_half, acts[2 * a_half :])


def half_blocks(ff):
    total = ff // LANES
    a_half = (total + 1) // 2 + (total // 2) % 2
    return total, total // 2, a_half, total - a_half


def ffn_acts(edges, nffn, cot, w_gate, w_up, w_down):
    rows, width = nffn.shape
    ff = w_gate.shape[1]
    sizes = half_blocks(ff)
    _, hid_half, a_half, b_half = sizes
    widths = [ff] * 3 + [hid_half * LANES] * 2 + [a_half * LANES] * 2 + [b_half * LANES] * 2
    return resident_call(
        functools.partial(ffn_acts_body, sizes),
        (edges, nffn, cot, w_gate, w_up, w_down),
        [sds((rows, w), bf16) for w in widths],
        "ffn_acts",
        6 * rows * width * ff,
    )


def ffn_back_body(
    seqs,
    edge_ref,
    hid_ref,
    gg_ref,
    gu_ref,
    wg_ref,
    wu_ref,
    wd_ref,
    mid_ref,
    cot_ref,
    wout_ref,
    gain_ref,
    *refs,
):
    out_refs = refs[:seqs]
    gmid_ref, keep_ref, send_ref, gatt_ref = refs[seqs:]
    length = out_refs[0].shape[0]
    middle = mid_ref[...]
    grads = mm(gg_ref[...], wg_ref[...], NT) + mm(gu_ref[...], wu_ref[...], NT)
    factor = lax.rsqrt(jnp.mean(middle * middle, axis=-1, keepdims=True) + epsilon)
    scaled = grads * gain_ref[...]
    inner = jnp.mean(scaled * middle, axis=-1, keepdims=True)
    grad_middle = cot_ref[...].astype(f32) + factor * (scaled - middle * (factor * factor * inner))
    gmid_ref[...] = grad_middle
    branch = grad_middle.astype(bf16)
    half = branch.shape[1] // 2

    @pl.when(edge_ref[1] == 0)
    def _():
        keep_ref[...] = branch[:, :half]
        send_ref[...] = branch[:, half:]

    @pl.when(edge_ref[1] != 0)
    def _():
        keep_ref[...] = branch[:, half:]
        send_ref[...] = branch[:, :half]

    gatt_ref[...] = mm(branch, wout_ref[...], NT).astype(bf16)
    out = middle + mm(hid_ref[...], wd_ref[...], NN)
    for s in range(seqs):
        out_refs[s][...] = out[s * length : (s + 1) * length].astype(bf16)


def ffn_back(seqs, edges, hidden, gg, gu, w_gate, w_up, w_down, middle, cot, w_out, gain):
    rows, width = cot.shape
    ff = w_gate.shape[1]
    outs = resident_call(
        functools.partial(ffn_back_body, seqs),
        (edges, hidden, gg, gu, w_gate, w_up, w_down, middle, cot, w_out, gain),
        [sds((rows // seqs, width), bf16)] * seqs
        + [
            sds((rows, width), f32),
            sds((rows, width // 2), bf16),
            sds((rows, width // 2), bf16),
            sds((rows, width), bf16),
        ],
        "ffn_back",
        6 * rows * width * ff + 2 * rows * width * width,
    )
    return outs[:seqs], outs[seqs:]


def grad_pack_body(seqs, received, edge_ref, *refs):
    gq_ref, gk_ref, gv_ref = refs[:3]
    others = refs[3 : 3 + received]
    cos_ref, sin_ref, packed_ref = refs[3 + received : 6 + received]
    first_refs = refs[6 + received : 6 + received + seqs]
    xk_ref, xs_ref, yk_ref, ys_ref = refs[6 + received + seqs :]
    width = gq_ref.shape[1]
    length = first_refs[0].shape[0]
    low_edge, high_edge = edge_ref[0], edge_ref[1]
    pairs = width // LANES
    quarter = pairs // 4
    for pair in range(pairs):
        at = slice(pair * LANES, (pair + 1) * LANES)
        at_v = slice(width + pair * LANES, width + (pair + 1) * LANES)
        grad_k, grad_v = gk_ref[:, at], gv_ref[:, at]
        for r in others:
            grad_k = grad_k + r[0, :, at].astype(f32)
            grad_v = grad_v + r[1, :, at].astype(f32)
        grad_k = (grad_k * cos_ref[...] - turn(grad_k) * sin_ref[...]).astype(bf16)
        grad_v = (0.5 * grad_v).astype(bf16)
        for s in range(seqs):
            first_refs[s][:, at] = grad_v[s * length : (s + 1) * length]
        packed_ref[:, at] = gq_ref[:, at]
        packed_ref[:, at_v] = grad_k
        packed_ref[:, 2 * width + pair * LANES : 2 * width + (pair + 1) * LANES] = grad_v
        packed = jnp.concatenate([gq_ref[:, at], grad_k, grad_v], axis=1)
        color, half = pair // (2 * quarter), pair // quarter % 2
        edge = high_edge if color else low_edge
        keep_ref, send_ref = (yk_ref, ys_ref) if color else (xk_ref, xs_ref)
        dst = slice(pair % quarter * 3 * LANES, (pair % quarter + 1) * 3 * LANES)

        @pl.when(edge == half)
        def _(keep_ref=keep_ref, dst=dst, packed=packed):
            keep_ref[:, dst] = packed

        @pl.when(edge != half)
        def _(send_ref=send_ref, dst=dst, packed=packed):
            send_ref[:, dst] = packed


def grad_pack(seqs, edges, gq, gk, gv, others, cosine, sines):
    rows, width = gq.shape
    outs = resident_call(
        functools.partial(grad_pack_body, seqs, len(others)),
        (edges, gq, gk, gv, *others, cosine, sines),
        [sds((rows, 3 * width), bf16)]
        + [sds((rows // seqs, width), bf16)] * seqs
        + [sds((rows, 3 * width // 4), bf16)] * 4,
        "grad_pack",
        20 * rows * width,
    )
    return outs[0], outs[1 : 1 + seqs], outs[1 + seqs :]


def grad_inputs_body(seqs, packed_ref, w_ref, x_ref, gain_ref, gmid_ref, *refs):
    given, out_refs = refs[: 2 * seqs], refs[2 * seqs :]
    grads = mm(packed_ref[...], w_ref[...], NT)
    inputs = x_ref[...].astype(f32)
    factor = lax.rsqrt(jnp.mean(inputs * inputs, axis=-1, keepdims=True) + epsilon)
    scaled = grads * gain_ref[...]
    inner = jnp.mean(scaled * inputs, axis=-1, keepdims=True)
    grads = gmid_ref[...] + factor * (scaled - inputs * (factor * factor * inner))
    grads = grads.astype(bf16)
    length = out_refs[0].shape[1]
    for s in range(seqs):
        out_refs[s][0] = given[s][...]
        out_refs[s][1] = grads[s * length : (s + 1) * length]
        out_refs[s][2] = given[seqs + s][...]


def grad_inputs(seqs, packed, w_qkv, x, gain, grad_middle, out_blocks, first_blocks):
    rows, width = x.shape
    return resident_call(
        functools.partial(grad_inputs_body, seqs),
        (packed, w_qkv, x, gain, grad_middle, *out_blocks, *first_blocks),
        [sds((3, rows // seqs, width), bf16)] * seqs,
        "grad_inputs",
        6 * rows * width * width,
        scalars=0,
    )


def place_body(seqs, shift_ref, *refs):
    for i, out_ref in enumerate(refs[seqs:]):
        for j in range(seqs):
            for s in range(seqs):

                @pl.when(lax.rem(shift_ref[0] + s, seqs) == j)
                def _(i=i, j=j, s=s, out_ref=out_ref):
                    out_ref[j] = refs[s][i]


def place(parts, seq):
    seqs = len(parts)
    count, length, width = parts[0].shape
    part = pl.BlockSpec((count, length, width // 4), lambda i: (0, 0, i))
    return pl.pallas_call(
        functools.partial(place_body, seqs),
        grid=(4,),
        in_specs=[scalar()] + [part] * seqs,
        out_specs=[pl.BlockSpec((seqs, length, width // 4), lambda i: (0, 0, i))] * count,
        out_shape=[sds((seqs, length, width), bf16)] * count,
        compiler_params=pltpu.CompilerParams(vmem_limit_bytes=VMEM_LIMIT),
        cost_estimate=cost(0, 4 * seqs * count * length * width),
        name="place",
    )(seq[None], *parts)


def outer_body(counts, per, core_ref, *refs):
    keep_ref, send_ref = refs[-2:]
    column = at = 0
    core = core_ref[0]
    for count in counts:
        lefts, rights = refs[at : at + count], refs[at + count : at + 2 * count]
        at += 2 * count
        total = None
        for left, right in zip(lefts, rights):
            part = mm(left[...], right[...], TN)
            total = part if total is None else total + part
        wide = total.shape[1]
        cut = slice(column, column + wide)
        column += wide
        total = total.astype(bf16)
        for i in range(total.shape[0] // (2 * per)):
            even = total[2 * i * per : (2 * i + 1) * per]
            odd = total[(2 * i + 1) * per : (2 * i + 2) * per]

            @pl.when(core == 0)
            def _(i=i, even=even, odd=odd, cut=cut):
                keep_ref[i, :, cut] = even
                send_ref[i, :, cut] = odd

            @pl.when(core != 0)
            def _(i=i, even=even, odd=odd, cut=cut):
                keep_ref[i, :, cut] = odd
                send_ref[i, :, cut] = even


def outer(core, per, *groups):
    rows, height = groups[0][0][0].shape
    width = sum(rights[0].shape[1] for _, rights in groups)
    block = 256 if height % 256 == 0 else height
    specs, args, flops = [], [], 0
    for lefts, rights in groups:
        wide = rights[0].shape[1]
        specs += [pl.BlockSpec((rows, block), lambda i: (0, i))] * len(lefts)
        specs += [whole((rows, wide))] * len(rights)
        args += [*lefts, *rights]
        flops += 2 * len(lefts) * rows * height * wide
    out_spec = pl.BlockSpec((block // (2 * per), per, width), lambda i: (i, 0, 0))
    return pl.pallas_call(
        functools.partial(outer_body, [len(lefts) for lefts, _ in groups], per),
        grid=(height // block,),
        in_specs=[scalar()] + specs,
        out_specs=[out_spec] * 2,
        out_shape=[sds((height // (2 * per), per, width), bf16)] * 2,
        compiler_params=pltpu.CompilerParams(vmem_limit_bytes=VMEM_LIMIT),
        cost_estimate=cost(flops, 2 * (sum(a.size for a in args) + height * width)),
        name="outer",
    )(core[None], *args)


def build(ndp, nblk):
    n = ndp * nblk
    nbits = n.bit_length() - 1
    blk_bits = nblk.bit_length() - 1
    if (1 << nbits) != n or (1 << blk_bits) != nblk:
        raise ValueError("mesh sizes")
    low_e, high_e = blk_bits, nbits - 1

    def send(value, target):
        pairs = [(i, target(i)) for i in range(n)]
        return lax.ppermute(value, AXES, pairs)

    def flip(value, bit):
        return send(value, lambda i: i ^ (1 << bit))

    def pick(value, index, axis=0):
        return lax.dynamic_index_in_dim(value, index, axis, keepdims=False)

    def shards(
        tokens, first_values, docs, cotangent, w_qkv, w_out, w_gate, w_up, w_down, gain_attn, gain_ffn
    ):
        seqs, length, width = tokens.shape
        ff = w_gate.shape[1]
        rows = seqs * length
        group = nblk // seqs
        blk = lax.axis_index("blk")
        index = lax.axis_index("dp") * nblk + blk
        seq, member = blk // group, blk % group

        def bit(t):
            return (index >> t) & 1

        core = bit(0)
        edges = jnp.stack([bit(low_e), bit(high_e)])

        def shift_seq(i, s):
            base, b = i - i % nblk, i % nblk
            return base + ((b // group + s) % seqs) * group + b % group

        def shift_member(i, s):
            base, b = i - i % nblk, i % nblk
            return base + (b // group) * group + (b % group + s) % group

        def to_sequence(value):
            parts = [pick(value, seq)]
            for s in range(1, seqs):
                out = pick(value, (seq + s) % seqs)
                parts.append(send(out, lambda i, s=s: shift_seq(i, s)))
            return parts

        def from_sequence(blocks):
            return [
                part if s == 0 else send(part, lambda i, s=s: shift_seq(i, -s))
                for s, part in enumerate(blocks)
            ]

        def others(value):
            return [send(value, lambda i, g=g: shift_member(i, g)) for g in range(1, group)]

        marks = jnp.pad(docs[:, None, :].astype(bf16), ((0, 0), (0, 7), (0, width - length)))
        parts = to_sequence(jnp.concatenate([tokens, marks, first_values], axis=1))

        base = jnp.arange(length, dtype=jnp.int32)
        qpos = jnp.concatenate(
            [(((seq - s) % seqs) * group + member) * length + base for s in range(seqs)]
        )
        kpos = jnp.concatenate(
            [
                (((seq - s) % seqs) * group + (member - g) % group) * length + base
                for g in range(group)
                for s in range(seqs)
            ]
        )
        half = HEAD_DIM // 2
        inverse = 10000.0 ** (-jnp.arange(half, dtype=f32) / half)
        angles = qpos.astype(f32)[:, None] * inverse[None, :]
        cos_half, sin_half = jnp.cos(angles), jnp.sin(angles)
        cosine = jnp.concatenate([cos_half] * 4, axis=1)
        sines = jnp.concatenate([-sin_half, sin_half] * 2, axis=1)
        qpos, kpos = qpos[None, :], kpos[:, None]
        gain_a, gain_f = gain_attn[None, :], gain_ffn[None, :]

        cosine, sines, qpos, kpos, parts, cotangent = tie(
            cosine, sines, qpos, kpos, parts, cotangent
        )
        x = jnp.concatenate([p[:length] for p in parts], axis=0)
        first = jnp.concatenate([p[-length:] for p in parts], axis=0)
        qdocs = jnp.concatenate([p[length, :length] for p in parts]).astype(jnp.int32)[None]
        normed, q, k = query_key(x, gain_a, w_qkv, cosine, sines)
        other_docs = others(qdocs)
        ks = [k] + others(k)
        cot_parts = to_sequence(cotangent)
        all_docs = jnp.concatenate([qdocs] + other_docs, axis=1)
        qstart = jnp.sum((all_docs[0][:, None] < qdocs).astype(jnp.int32), axis=0, keepdims=True)
        v = value_mix(normed, w_qkv, first)
        normed_x = flip(normed, low_e)
        normed_y = flip(normed, high_e)
        vs = [v] + others(v)
        attended, lse = attend(q, ks, vs, kpos, qpos, qstart)
        attended, normed_x, normed_y, cot_parts = tie(attended, normed_x, normed_y, cot_parts)
        cot = jnp.concatenate(cot_parts, axis=0)
        attended_y = flip(attended, high_e)
        cot_y = flip(cot, high_e)
        middle, nffn = middle_norm(x, attended, w_out, gain_f)
        nffn_x = flip(nffn, low_e)
        hidden, gg, gu, hk, hs, ak, a_s, bk, bs = ffn_acts(edges, nffn, cot, w_gate, w_up, w_down)
        hidden, gg, gu, hs, a_s, bs, nffn_x, cot_y = tie(
            hidden, gg, gu, hs, a_s, bs, nffn_x, cot_y
        )
        h_y = flip(hs, high_e)
        a_x = flip(a_s, low_e)
        out_blocks, (grad_mid, gbk, gbs, grad_att) = ffn_back(
            seqs, edges, hidden, gg, gu, w_gate, w_up, w_down, middle, cot, w_out, gain_f
        )
        gbs, bs, grad_att = tie(gbs, bs, grad_att)
        b_x = flip(bs, low_e)
        gb_y = flip(gbs, high_e)
        gq, gk, gv, other_kv = attend_back(
            q, grad_att, ks, vs, lse, kpos, qpos, qstart, cosine, sines
        )
        gq, gk, gv, other_kv, h_y, a_x = tie(gq, gk, gv, other_kv, h_y, a_x)
        got_kv = [send(v, lambda i, g=g: shift_member(i, -g)) for g, v in enumerate(other_kv, 1)]
        per_down = ff // n
        per = width // n
        dk, ds = outer(core, per_down, ([hk, h_y], [cot, cot_y]))
        dk, ds, got_kv = tie(dk, ds, got_kv)
        d_c = flip(ds, 0)
        packed, first_blocks, (qxk, qxs, qyk, qys) = grad_pack(
            seqs, edges, gq, gk, gv, got_kv, cosine, sines
        )
        packed, first_blocks, qxs, qys, d_c = tie(packed, first_blocks, qxs, qys, d_c)
        q_x = flip(qxs, low_e)
        q_y = flip(qys, high_e)
        blocks = grad_inputs(seqs, packed, w_qkv, x, gain_a, grad_mid, out_blocks, first_blocks)

        class Rows:
            def __init__(self, keep, got, top, skip):
                dims = (2,) * top + keep.shape[1:]
                self.terms = [keep.reshape(dims), got.reshape(dims)]
                self.left = list(range(top, 0, -1))
                self.order = [t for t in self.left if t >= blk_bits and t != skip]
                self.order += list(range(1, min(blk_bits, top + 1)))
                self.skip, self.swapped = skip, False

            def total(self, terms):
                return functools.reduce(lambda a, b: a + b, [t.astype(f32) for t in terms])

            def go(self):
                t = self.order.pop(0)
                axis, b = self.left.index(t), bit(t)
                out = self.total([pick(v, 1 - b, axis) for v in self.terms]).astype(bf16)
                self.terms = [pick(v, b, axis) for v in self.terms] + [flip(out, t)]
                self.left.pop(axis)

            def next(self):
                if self.order:
                    self.go()
                elif self.skip >= 0 and not self.swapped:
                    value, b = self.total(self.terms), bit(self.skip)
                    self.swapped = True
                    out = flip(pick(value, 1 - b).astype(bf16), self.skip)
                    self.terms = [pick(value, b), out]
                else:
                    return False
                return True

            def halves(self):
                mine, other = self.terms[0], self.terms[1].astype(f32)
                b = bit(self.skip)
                return jnp.stack([jnp.where(b == 0, mine, other), jnp.where(b == 0, other, mine)])

        def settle(values, *reductions):
            last = [r.terms[-1] for r in reductions]
            values, last = tie(values, last)
            for r, got in zip(reductions, last):
                r.terms[-1] = got
            return values

        ak2, as2 = outer(core, per, ([nffn, nffn_x], [ak, a_x]))
        blocks, ak2, as2, b_x, gb_y, attended_y = tie(blocks, ak2, as2, b_x, gb_y, attended_y)
        a_c = flip(as2, 0)
        down = Rows(dk, d_c, nbits - 2, -1)
        down.next()
        moved = from_sequence(blocks)
        bk2, bs2 = outer(core, per, ([nffn, nffn_x], [bk, b_x]))
        bk2, bs2, a_c, q_x, q_y = tie(bk2, bs2, a_c, q_x, q_y)
        b_c = flip(bs2, 0)
        part_a = Rows(ak2, a_c, nbits - 1, low_e)
        part_a.next()
        qyk2, qys2 = outer(
            core, per, ([normed, normed_y], [qyk, q_y]), ([attended, attended_y], [gbk, gb_y])
        )
        qyk2, qys2, b_c, moved[1::2] = tie(qyk2, qys2, b_c, moved[1::2])
        qy_c = flip(qys2, 0)
        part_b = Rows(bk2, b_c, nbits - 1, low_e)
        qxk2, qxs2 = outer(core, per, ([normed, normed_x], [qxk, q_x]))
        qxk2, qxs2, qy_c, moved = settle((qxk2, qxs2, qy_c, moved), down)
        qx_c = flip(qxs2, 0)
        part_y = Rows(qyk2, qy_c, nbits - 1, high_e)
        part_b.next()
        down.next()
        part_y.next()
        (qx_c,) = settle((qx_c,), part_a, down)
        part_x = Rows(qxk2, qx_c, nbits - 1, low_e)
        part_a.next()
        part_x.next()
        down.next()
        settle((), part_a, part_b, part_y, down)
        everything = (part_a, part_b, part_y, part_x, down)
        while True:
            busy = [part for part in everything if part.next()]
            if not busy:
                break
            settle((), *busy)
        grad_down = down.total(down.terms)
        a_done, b_done, qx_done, qy_done = (
            part.halves() for part in (part_a, part_b, part_x, part_y)
        )
        output, grad_tokens, grad_first_values = place(moved, seq)

        acts = jnp.concatenate([a_done[0], a_done[1], b_done[0], b_done[1]], axis=1)
        grad_gate, grad_up = acts[:, :ff], acts[:, ff:]
        q_wide = 3 * width // 4
        grad_out = jnp.concatenate([qy_done[0, :, q_wide:], qy_done[1, :, q_wide:]], axis=1)
        qy_done = qy_done[:, :, :q_wide]
        pairs = width // LANES
        grad_qkv = jnp.concatenate([qx_done, qy_done], axis=0)
        grad_qkv = grad_qkv.reshape(4, per, pairs // 4, 3, LANES)
        grad_qkv = jnp.transpose(grad_qkv, (1, 3, 0, 2, 4)).reshape(per, 3 * width)

        def own(value):
            return lax.dynamic_slice_in_dim(value, index * per, per, 0)

        grad_gain_attn = jnp.sum(grad_qkv * own(w_qkv).astype(f32), axis=1) / own(gain_attn)
        grad_gain_ffn = (
            jnp.sum(
                grad_gate * own(w_gate).astype(f32) + grad_up * own(w_up).astype(f32), axis=1
            )
            / own(gain_ffn)
        )
        return (
            output,
            grad_tokens,
            grad_first_values,
            grad_qkv,
            grad_out,
            grad_gate,
            grad_up,
            grad_down,
            grad_gain_attn,
            grad_gain_ffn,
        )

    return shards


def solution(mesh):
    seq = P("dp", "blk", None)
    rows = P(AXES, None)
    vec = P(AXES)
    in_specs = (seq, seq, P("dp", "blk"), seq) + (P(),) * 7
    out_specs = (seq, seq, seq, rows, rows, rows, rows, rows, vec, vec)
    return jax.shard_map(
        build(mesh.shape["dp"], mesh.shape["blk"]),
        mesh=mesh,
        in_specs=in_specs,
        out_specs=out_specs,
        check_vma=False,
    )
```

```python
import functools

import jax
import jax.numpy as jnp
from jax import lax
from jax.experimental import pallas as pl
from jax.experimental.pallas import tpu as pltpu
from jax.sharding import PartitionSpec as P

HEAD_DIM = 64
LANES = 128
AXES = ("dp", "blk")
epsilon = 1e-06
score_scale = 0.125
cost_share = 1.0
VMEM_LIMIT = 16 << 20
bf16 = jnp.bfloat16
f32 = jnp.float32

NN = (((1,), (0,)), ((), ()))
NT = (((1,), (1,)), ((), ()))
TN = (((0,), (0,)), ((), ()))


def mm(a, b, dims):
    return lax.dot_general(a, b, dims, preferred_element_type=f32)


def sds(shape, dtype):
    return jax.ShapeDtypeStruct(shape, dtype)


def cost(flops, nbytes, trans=0):
    return pl.CostEstimate(
        flops=int(flops * cost_share), bytes_accessed=int(nbytes * cost_share), transcendentals=0
    )


def whole(shape):
    return pl.BlockSpec(shape, lambda *_: (0,) * len(shape))


def scalar():
    return pl.BlockSpec(memory_space=pltpu.SMEM)


RESIDENT = pl.BlockSpec(memory_space=pltpu.VMEM)


def lanes(step, width):
    return pl.ds(pl.multiple_of(step * width, width), width)


def resident_call(body, ins, outs, name, flops, scratch=(), scalars=1):
    nbytes = sum(a.size * a.dtype.itemsize for a in (*ins, *outs))
    return pl.pallas_call(
        body,
        in_specs=[scalar()] * scalars + [RESIDENT] * (len(ins) - scalars),
        out_specs=[RESIDENT] * len(outs),
        out_shape=list(outs),
        scratch_shapes=list(scratch),
        compiler_params=pltpu.CompilerParams(vmem_limit_bytes=VMEM_LIMIT),
        cost_estimate=cost(flops, nbytes),
        name=name,
    )(*ins)


def tie(*values):
    return lax.optimization_barrier(values)


def lane_half(shape):
    lane = lax.broadcasted_iota(jnp.int32, shape, len(shape) - 1)
    return (lane & (HEAD_DIM - 1)) < HEAD_DIM // 2


def turn(values):
    half = HEAD_DIM // 2
    return jnp.where(
        lane_half(values.shape),
        pltpu.roll(values, LANES - half, 1),
        pltpu.roll(values, half, 1),
    )


def head_mask(shape, head):
    lane = lax.broadcasted_iota(jnp.int32, shape, 1)
    return lane < HEAD_DIM if head == 0 else lane >= HEAD_DIM


def rotate_all(projected, cosine, sines):
    parts = []
    for i in range(projected.shape[1] // LANES):
        part = projected[:, i * LANES : (i + 1) * LANES]
        parts.append((part * cosine + turn(part) * sines).astype(bf16))
    return jnp.concatenate(parts, axis=1)


def query_key_body(x_ref, gain_ref, w_ref, cos_ref, sin_ref, normed_ref, q_ref, k_ref):
    inputs = x_ref[...].astype(f32)
    factor = lax.rsqrt(jnp.mean(inputs * inputs, axis=-1, keepdims=True) + epsilon)
    normed = (inputs * factor * gain_ref[...]).astype(bf16)
    normed_ref[...] = normed
    width = q_ref.shape[1]
    block = 256
    for j in range(2 * width // block):
        at = slice(j * block, (j + 1) * block)
        rotated = rotate_all(mm(normed, w_ref[:, at], NN), cos_ref[...], sin_ref[...])
        if j * block < width:
            q_ref[:, at] = rotated
        else:
            k_ref[:, slice(j * block - width, (j + 1) * block - width)] = rotated


def query_key(x, gain, w_qkv, cosine, sines):
    rows, width = x.shape
    return resident_call(
        query_key_body,
        (x, gain, w_qkv, cosine, sines),
        [sds((rows, width), bf16)] * 3,
        "query_key",
        4 * rows * width * width,
        scalars=0,
    )


def value_mix_body(normed_ref, w_ref, first_ref, out_ref):
    width = out_ref.shape[1]
    block = 256
    for j in range(width // block):
        at = slice(j * block, (j + 1) * block)
        projected = mm(normed_ref[...], w_ref[:, 2 * width + j * block : 2 * width + (j + 1) * block], NN)
        out_ref[:, at] = (0.5 * projected + 0.5 * first_ref[:, at].astype(f32)).astype(bf16)


def value_mix(normed, w_qkv, first):
    rows, width = normed.shape
    return resident_call(
        value_mix_body,
        (normed, w_qkv, first),
        [sds((rows, width), bf16)],
        "value_mix",
        2 * rows * width * width,
        scalars=0,
    )[0]


def set_bias(bias_ref, kpos_ref, qpos_ref, qstart_ref):
    keys, qpos = kpos_ref[...], qpos_ref[...]
    allowed = (keys <= qpos) & (keys >= qstart_ref[...])
    bias_ref[...] = jnp.where(allowed, 0.0, -1e30)


def attend_body(slots, *refs):
    q_ref = refs[0]
    k_refs = refs[1 : 1 + slots]
    v_refs = refs[1 + slots : 1 + 2 * slots]
    kpos_ref, qpos_ref, qstart_ref, out_ref, lse_ref, bias_ref = refs[1 + 2 * slots :]

    @pl.when(pl.program_id(0) == 0)
    def _():
        set_bias(bias_ref, kpos_ref, qpos_ref, qstart_ref)

    queries = q_ref[...] * jnp.asarray(score_scale, bf16)
    keys = jnp.concatenate([r[...] for r in k_refs], axis=0)
    values = jnp.concatenate([r[...] for r in v_refs], axis=0)
    values_t = jnp.transpose(values)
    outs = []
    for head in range(2):
        own = jnp.where(head_mask(queries.shape, head), queries, jnp.zeros_like(queries))
        scores = mm(keys, own, NT) + bias_ref[...]
        top = jnp.max(scores, axis=0, keepdims=True)
        weights = jnp.exp(scores - top)
        total = jnp.sum(weights, axis=0, keepdims=True)
        probs = (weights * (1.0 / total)).astype(bf16)
        outs.append(mm(values_t[head * HEAD_DIM : (head + 1) * HEAD_DIM], probs, NN))
        lse_ref[0, head : head + 1, :] = top + jnp.log(total)
    out_ref[...] = jnp.transpose(jnp.concatenate(outs, axis=0)).astype(bf16)


def attend(q, ks, vs, kpos, qpos, qstart):
    rows, width = q.shape
    slots = len(ks)
    pairs = width // LANES
    keys = slots * rows
    col = pl.BlockSpec((rows, LANES), lambda i: (0, i))
    return pl.pallas_call(
        functools.partial(attend_body, slots),
        grid=(pairs,),
        in_specs=[col]
        + [col] * slots
        + [col] * slots
        + [whole((keys, 1)), whole((1, rows)), whole((1, rows))],
        out_specs=[col, pl.BlockSpec((1, 2, rows), lambda i: (i, 0, 0))],
        out_shape=[sds((rows, width), bf16), sds((pairs, 2, rows), f32)],
        scratch_shapes=[pltpu.VMEM((keys, rows), f32)],
        cost_estimate=cost(
            8 * pairs * rows * keys * LANES, 2 * rows * width * (2 + 2 * slots), 2 * pairs * rows * keys
        ),
        name="attend",
    )(q, *ks, *vs, kpos, qpos, qstart)


def attend_back_body(slots, *refs):
    q_ref, grad_ref = refs[:2]
    k_refs = refs[2 : 2 + slots]
    v_refs = refs[2 + slots : 2 + 2 * slots]
    lse_ref, kpos_ref, qpos_ref, qstart_ref, cos_ref, sin_ref = refs[2 + 2 * slots : 8 + 2 * slots]
    gq_ref, gk_ref, gv_ref = refs[8 + 2 * slots : 11 + 2 * slots]
    other_refs = refs[11 + 2 * slots : 10 + 3 * slots]
    bias_ref = refs[-1]

    @pl.when(pl.program_id(0) == 0)
    def _():
        set_bias(bias_ref, kpos_ref, qpos_ref, qstart_ref)

    queries = q_ref[...] * jnp.asarray(score_scale, bf16)
    grads = grad_ref[...]
    keys = jnp.concatenate([r[...] for r in k_refs], axis=0)
    values = jnp.concatenate([r[...] for r in v_refs], axis=0)
    keys_t = jnp.transpose(keys)
    grad_values = grad_keys = None
    grad_q = []
    for head in range(2):
        mask = head_mask(queries.shape, head)
        own_q = jnp.where(mask, queries, jnp.zeros_like(queries))
        own_g = jnp.where(mask, grads, jnp.zeros_like(grads))
        scores = mm(keys, own_q, NT) + bias_ref[...]
        probs = jnp.exp(scores - lse_ref[0, head : head + 1, :])
        grad_probs = mm(values, own_g, NT)
        delta = jnp.sum(probs * grad_probs, axis=0, keepdims=True)
        grad_scores = (probs * (grad_probs - delta)).astype(bf16)
        part_v = mm(probs.astype(bf16), own_g, NN)
        part_k = mm(grad_scores, own_q, NN)
        grad_values = part_v if grad_values is None else grad_values + part_v
        grad_keys = part_k if grad_keys is None else grad_keys + part_k
        grad_q.append(mm(keys_t[head * HEAD_DIM : (head + 1) * HEAD_DIM], grad_scores, NN))
    grad_q = jnp.transpose(jnp.concatenate(grad_q, axis=0)) * score_scale
    gq_ref[...] = (grad_q * cos_ref[...] - turn(grad_q) * sin_ref[...]).astype(bf16)
    rows = q_ref.shape[0]
    gk_ref[...] = grad_keys[:rows]
    gv_ref[...] = grad_values[:rows]
    for slot in range(1, slots):
        other_refs[slot - 1][0] = grad_keys[slot * rows : (slot + 1) * rows].astype(bf16)
        other_refs[slot - 1][1] = grad_values[slot * rows : (slot + 1) * rows].astype(bf16)


def attend_back(q, grad, ks, vs, lse, kpos, qpos, qstart, cosine, sines):
    rows, width = q.shape
    slots = len(ks)
    pairs = width // LANES
    keys = slots * rows
    col = pl.BlockSpec((rows, LANES), lambda i: (0, i))
    outs = pl.pallas_call(
        functools.partial(attend_back_body, slots),
        grid=(pairs,),
        in_specs=[col, col]
        + [col] * slots
        + [col] * slots
        + [pl.BlockSpec((1, 2, rows), lambda i: (i, 0, 0))]
        + [whole((keys, 1)), whole((1, rows)), whole((1, rows))]
        + [whole((rows, LANES))] * 2,
        out_specs=[col] * 3 + [pl.BlockSpec((2, rows, LANES), lambda i: (0, 0, i))] * (slots - 1),
        out_shape=[sds((rows, width), bf16)]
        + [sds((rows, width), f32)] * 2
        + [sds((2, rows, width), bf16)] * (slots - 1),
        scratch_shapes=[pltpu.VMEM((keys, rows), f32)],
        cost_estimate=cost(
            20 * pairs * rows * keys * LANES, 2 * rows * width * (7 + 4 * slots), 2 * pairs * rows * keys
        ),
        name="attend_back",
    )(q, grad, *ks, *vs, lse, kpos, qpos, qstart, cosine, sines)
    return (*outs[:3], outs[3:])


def middle_body(x_ref, att_ref, wout_ref, gain_ref, mid_ref, nffn_ref):
    middle = x_ref[...].astype(f32) + mm(att_ref[...], wout_ref[...], NN)
    mid_ref[...] = middle
    factor = lax.rsqrt(jnp.mean(middle * middle, axis=-1, keepdims=True) + epsilon)
    nffn_ref[...] = (middle * factor * gain_ref[...]).astype(bf16)


def middle_norm(x, attended, w_out, gain):
    rows, width = x.shape
    return resident_call(
        middle_body,
        (x, attended, w_out, gain),
        [sds((rows, width), f32), sds((rows, width), bf16)],
        "middle_norm",
        2 * rows * width * width,
        scalars=0,
    )


def ffn_acts_body(
    sizes,
    edge_ref,
    nffn_ref,
    cot_ref,
    wg_ref,
    wu_ref,
    wd_ref,
    hid_ref,
    gg_ref,
    gu_ref,
    hk_ref,
    hs_ref,
    ak_ref,
    as_ref,
    bk_ref,
    bs_ref,
):
    total, hid_half, a_half, b_half = sizes
    block = 256
    per = block // LANES
    for step in range(total // per):
        at = slice(step * block, (step + 1) * block)
        gate = mm(nffn_ref[...], wg_ref[:, at], NN)
        upward = mm(nffn_ref[...], wu_ref[:, at], NN)
        grad_hidden = mm(cot_ref[...], wd_ref[at, :], NT)
        sig = 1.0 / (1.0 + jnp.exp(-gate))
        silu = gate * sig
        hid_ref[:, at] = (silu * upward).astype(bf16)
        gg_ref[:, at] = (grad_hidden * upward * (sig * (1.0 + gate * (1.0 - sig)))).astype(bf16)
        gu_ref[:, at] = (grad_hidden * silu).astype(bf16)

    low_edge, high_edge = edge_ref[0], edge_ref[1]

    def halves(edge, keep_ref, send_ref, size, places):
        for half in range(2):
            runs = []
            for offset in range(size):
                source, start = places[half * size + offset]
                if runs and runs[-1][0] is source and runs[-1][2] == start:
                    runs[-1][2] += 1
                else:
                    runs.append([source, start, start + 1, offset])
            for source, start, stop, offset in runs:
                src = slice(start * LANES, stop * LANES)
                dst = slice(offset * LANES, (offset + stop - start) * LANES)

                @pl.when(edge == half)
                def _(source=source, src=src, dst=dst):
                    keep_ref[:, dst] = source[:, src]

                @pl.when(edge != half)
                def _(source=source, src=src, dst=dst):
                    send_ref[:, dst] = source[:, src]

    acts = [(gg_ref, i) for i in range(total)] + [(gu_ref, i) for i in range(total)]
    halves(high_edge, hk_ref, hs_ref, hid_half, [(hid_ref, i) for i in range(total)])
    halves(low_edge, ak_ref, as_ref, a_half, acts[: 2 * a_half])
    halves(low_edge, bk_ref, bs_ref, b_half, acts[2 * a_half :])


def half_blocks(ff):
    total = ff // LANES
    a_half = (total + 1) // 2 + (total // 2) % 2
    return total, total // 2, a_half, total - a_half


def ffn_acts(edges, nffn, cot, w_gate, w_up, w_down):
    rows, width = nffn.shape
    ff = w_gate.shape[1]
    sizes = half_blocks(ff)
    _, hid_half, a_half, b_half = sizes
    widths = [ff] * 3 + [hid_half * LANES] * 2 + [a_half * LANES] * 2 + [b_half * LANES] * 2
    return resident_call(
        functools.partial(ffn_acts_body, sizes),
        (edges, nffn, cot, w_gate, w_up, w_down),
        [sds((rows, w), bf16) for w in widths],
        "ffn_acts",
        6 * rows * width * ff,
    )


def ffn_back_body(
    seqs,
    edge_ref,
    hid_ref,
    gg_ref,
    gu_ref,
    wg_ref,
    wu_ref,
    wd_ref,
    mid_ref,
    cot_ref,
    wout_ref,
    gain_ref,
    *refs,
):
    out_refs = refs[:seqs]
    gmid_ref, keep_ref, send_ref, gatt_ref = refs[seqs:]
    length = out_refs[0].shape[0]
    middle = mid_ref[...]
    grads = mm(gg_ref[...], wg_ref[...], NT) + mm(gu_ref[...], wu_ref[...], NT)
    factor = lax.rsqrt(jnp.mean(middle * middle, axis=-1, keepdims=True) + epsilon)
    scaled = grads * gain_ref[...]
    inner = jnp.mean(scaled * middle, axis=-1, keepdims=True)
    grad_middle = cot_ref[...].astype(f32) + factor * (scaled - middle * (factor * factor * inner))
    gmid_ref[...] = grad_middle
    branch = grad_middle.astype(bf16)
    half = branch.shape[1] // 2

    @pl.when(edge_ref[1] == 0)
    def _():
        keep_ref[...] = branch[:, :half]
        send_ref[...] = branch[:, half:]

    @pl.when(edge_ref[1] != 0)
    def _():
        keep_ref[...] = branch[:, half:]
        send_ref[...] = branch[:, :half]

    gatt_ref[...] = mm(branch, wout_ref[...], NT).astype(bf16)
    out = middle + mm(hid_ref[...], wd_ref[...], NN)
    for s in range(seqs):
        out_refs[s][...] = out[s * length : (s + 1) * length].astype(bf16)


def ffn_back(seqs, edges, hidden, gg, gu, w_gate, w_up, w_down, middle, cot, w_out, gain):
    rows, width = cot.shape
    ff = w_gate.shape[1]
    outs = resident_call(
        functools.partial(ffn_back_body, seqs),
        (edges, hidden, gg, gu, w_gate, w_up, w_down, middle, cot, w_out, gain),
        [sds((rows // seqs, width), bf16)] * seqs
        + [
            sds((rows, width), f32),
            sds((rows, width // 2), bf16),
            sds((rows, width // 2), bf16),
            sds((rows, width), bf16),
        ],
        "ffn_back",
        6 * rows * width * ff + 2 * rows * width * width,
    )
    return outs[:seqs], outs[seqs:]


def grad_pack_body(seqs, received, edge_ref, *refs):
    gq_ref, gk_ref, gv_ref = refs[:3]
    others = refs[3 : 3 + received]
    cos_ref, sin_ref, packed_ref = refs[3 + received : 6 + received]
    first_refs = refs[6 + received : 6 + received + seqs]
    xk_ref, xs_ref, yk_ref, ys_ref = refs[6 + received + seqs :]
    width = gq_ref.shape[1]
    length = first_refs[0].shape[0]
    low_edge, high_edge = edge_ref[0], edge_ref[1]
    pairs = width // LANES
    quarter = pairs // 4
    for pair in range(pairs):
        at = slice(pair * LANES, (pair + 1) * LANES)
        at_v = slice(width + pair * LANES, width + (pair + 1) * LANES)
        grad_k, grad_v = gk_ref[:, at], gv_ref[:, at]
        for r in others:
            grad_k = grad_k + r[0, :, at].astype(f32)
            grad_v = grad_v + r[1, :, at].astype(f32)
        grad_k = (grad_k * cos_ref[...] - turn(grad_k) * sin_ref[...]).astype(bf16)
        grad_v = (0.5 * grad_v).astype(bf16)
        for s in range(seqs):
            first_refs[s][:, at] = grad_v[s * length : (s + 1) * length]
        packed_ref[:, at] = gq_ref[:, at]
        packed_ref[:, at_v] = grad_k
        packed_ref[:, 2 * width + pair * LANES : 2 * width + (pair + 1) * LANES] = grad_v
        packed = jnp.concatenate([gq_ref[:, at], grad_k, grad_v], axis=1)
        color, half = pair // (2 * quarter), pair // quarter % 2
        edge = high_edge if color else low_edge
        keep_ref, send_ref = (yk_ref, ys_ref) if color else (xk_ref, xs_ref)
        dst = slice(pair % quarter * 3 * LANES, (pair % quarter + 1) * 3 * LANES)

        @pl.when(edge == half)
        def _(keep_ref=keep_ref, dst=dst, packed=packed):
            keep_ref[:, dst] = packed

        @pl.when(edge != half)
        def _(send_ref=send_ref, dst=dst, packed=packed):
            send_ref[:, dst] = packed


def grad_pack(seqs, edges, gq, gk, gv, others, cosine, sines):
    rows, width = gq.shape
    outs = resident_call(
        functools.partial(grad_pack_body, seqs, len(others)),
        (edges, gq, gk, gv, *others, cosine, sines),
        [sds((rows, 3 * width), bf16)]
        + [sds((rows // seqs, width), bf16)] * seqs
        + [sds((rows, 3 * width // 4), bf16)] * 4,
        "grad_pack",
        20 * rows * width,
    )
    return outs[0], outs[1 : 1 + seqs], outs[1 + seqs :]


def grad_inputs_body(seqs, packed_ref, w_ref, x_ref, gain_ref, gmid_ref, *refs):
    first_refs, out_refs = refs[:seqs], refs[seqs:]
    grads = mm(packed_ref[...], w_ref[...], NT)
    inputs = x_ref[...].astype(f32)
    factor = lax.rsqrt(jnp.mean(inputs * inputs, axis=-1, keepdims=True) + epsilon)
    scaled = grads * gain_ref[...]
    inner = jnp.mean(scaled * inputs, axis=-1, keepdims=True)
    grads = gmid_ref[...] + factor * (scaled - inputs * (factor * factor * inner))
    grads = grads.astype(bf16)
    length = out_refs[0].shape[1]
    for s in range(seqs):
        out_refs[s][0] = grads[s * length : (s + 1) * length]
        out_refs[s][1] = first_refs[s][...]


def grad_inputs(seqs, packed, w_qkv, x, gain, grad_middle, first_blocks):
    rows, width = x.shape
    return resident_call(
        functools.partial(grad_inputs_body, seqs),
        (packed, w_qkv, x, gain, grad_middle, *first_blocks),
        [sds((2, rows // seqs, width), bf16)] * seqs,
        "grad_inputs",
        6 * rows * width * width,
        scalars=0,
    )


def place_body(seqs, shift_ref, *refs):
    for i, out_ref in enumerate(refs[seqs:]):
        for j in range(seqs):
            for s in range(seqs):

                @pl.when(lax.rem(shift_ref[0] + s, seqs) == j)
                def _(i=i, j=j, s=s, out_ref=out_ref):
                    out_ref[j] = refs[s][i]


def place(parts, seq):
    seqs = len(parts)
    count, length, width = parts[0].shape
    part = pl.BlockSpec((count, length, width // 4), lambda i: (0, 0, i))
    return pl.pallas_call(
        functools.partial(place_body, seqs),
        grid=(4,),
        in_specs=[scalar()] + [part] * seqs,
        out_specs=[pl.BlockSpec((seqs, length, width // 4), lambda i: (0, 0, i))] * count,
        out_shape=[sds((seqs, length, width), bf16)] * count,
        compiler_params=pltpu.CompilerParams(vmem_limit_bytes=VMEM_LIMIT),
        cost_estimate=cost(0, 4 * seqs * count * length * width),
        name="place",
    )(seq[None], *parts)


def outer_body(counts, per, core_ref, *refs):
    keep_ref, send_ref = refs[-2:]
    column = at = 0
    core = core_ref[0]
    for count in counts:
        lefts, rights = refs[at : at + count], refs[at + count : at + 2 * count]
        at += 2 * count
        total = None
        for left, right in zip(lefts, rights):
            part = mm(left[...], right[...], TN)
            total = part if total is None else total + part
        wide = total.shape[1]
        cut = slice(column, column + wide)
        column += wide
        total = total.astype(bf16)
        for i in range(total.shape[0] // (2 * per)):
            even = total[2 * i * per : (2 * i + 1) * per]
            odd = total[(2 * i + 1) * per : (2 * i + 2) * per]

            @pl.when(core == 0)
            def _(i=i, even=even, odd=odd, cut=cut):
                keep_ref[i, :, cut] = even
                send_ref[i, :, cut] = odd

            @pl.when(core != 0)
            def _(i=i, even=even, odd=odd, cut=cut):
                keep_ref[i, :, cut] = odd
                send_ref[i, :, cut] = even


def outer(core, per, *groups):
    rows, height = groups[0][0][0].shape
    width = sum(rights[0].shape[1] for _, rights in groups)
    block = 256 if height % 256 == 0 else height
    specs, args, flops = [], [], 0
    for lefts, rights in groups:
        wide = rights[0].shape[1]
        specs += [pl.BlockSpec((rows, block), lambda i: (0, i))] * len(lefts)
        specs += [whole((rows, wide))] * len(rights)
        args += [*lefts, *rights]
        flops += 2 * len(lefts) * rows * height * wide
    out_spec = pl.BlockSpec((block // (2 * per), per, width), lambda i: (i, 0, 0))
    return pl.pallas_call(
        functools.partial(outer_body, [len(lefts) for lefts, _ in groups], per),
        grid=(height // block,),
        in_specs=[scalar()] + specs,
        out_specs=[out_spec] * 2,
        out_shape=[sds((height // (2 * per), per, width), bf16)] * 2,
        cost_estimate=cost(flops, 2 * (sum(a.size for a in args) + height * width)),
        name="outer",
    )(core[None], *args)


def build(ndp, nblk):
    n = ndp * nblk
    nbits = n.bit_length() - 1
    blk_bits = nblk.bit_length() - 1
    if (1 << nbits) != n or (1 << blk_bits) != nblk:
        raise ValueError("mesh sizes")
    low_e, high_e = blk_bits, nbits - 1

    def send(value, target):
        pairs = [(i, target(i)) for i in range(n)]
        return lax.ppermute(value, AXES, pairs)

    def flip(value, bit):
        return send(value, lambda i: i ^ (1 << bit))

    def pick(value, index, axis=0):
        return lax.dynamic_index_in_dim(value, index, axis, keepdims=False)

    def shards(
        tokens, first_values, docs, cotangent, w_qkv, w_out, w_gate, w_up, w_down, gain_attn, gain_ffn
    ):
        seqs, length, width = tokens.shape
        ff = w_gate.shape[1]
        rows = seqs * length
        group = nblk // seqs
        blk = lax.axis_index("blk")
        index = lax.axis_index("dp") * nblk + blk
        seq, member = blk // group, blk % group

        def bit(t):
            return (index >> t) & 1

        core = bit(0)
        edges = jnp.stack([bit(low_e), bit(high_e)])

        def shift_seq(i, s):
            base, b = i - i % nblk, i % nblk
            return base + ((b // group + s) % seqs) * group + b % group

        def shift_member(i, s):
            base, b = i - i % nblk, i % nblk
            return base + (b // group) * group + (b % group + s) % group

        def to_sequence(value):
            parts = [pick(value, seq)]
            for s in range(1, seqs):
                out = pick(value, (seq + s) % seqs)
                parts.append(send(out, lambda i, s=s: shift_seq(i, s)))
            return parts

        def from_sequence(blocks):
            return [
                part if s == 0 else send(part, lambda i, s=s: shift_seq(i, -s))
                for s, part in enumerate(blocks)
            ]

        def others(value):
            return [send(value, lambda i, g=g: shift_member(i, g)) for g in range(1, group)]

        marks = jnp.pad(docs[:, None, :].astype(bf16), ((0, 0), (0, 7), (0, width - length)))
        parts = to_sequence(jnp.concatenate([tokens, marks, first_values], axis=1))

        base = jnp.arange(length, dtype=jnp.int32)
        qpos = jnp.concatenate(
            [(((seq - s) % seqs) * group + member) * length + base for s in range(seqs)]
        )
        kpos = jnp.concatenate(
            [
                (((seq - s) % seqs) * group + (member - g) % group) * length + base
                for g in range(group)
                for s in range(seqs)
            ]
        )
        half = HEAD_DIM // 2
        inverse = 10000.0 ** (-jnp.arange(half, dtype=f32) / half)
        angles = qpos.astype(f32)[:, None] * inverse[None, :]
        cos_half, sin_half = jnp.cos(angles), jnp.sin(angles)
        cosine = jnp.concatenate([cos_half] * 4, axis=1)
        sines = jnp.concatenate([-sin_half, sin_half] * 2, axis=1)
        qpos, kpos = qpos[None, :], kpos[:, None]
        gain_a, gain_f = gain_attn[None, :], gain_ffn[None, :]

        cosine, sines, qpos, kpos, parts, cotangent = tie(
            cosine, sines, qpos, kpos, parts, cotangent
        )
        x = jnp.concatenate([p[:length] for p in parts], axis=0)
        first = jnp.concatenate([p[-length:] for p in parts], axis=0)
        qdocs = jnp.concatenate([p[length, :length] for p in parts]).astype(jnp.int32)[None]
        normed, q, k = query_key(x, gain_a, w_qkv, cosine, sines)
        other_docs = others(qdocs)
        ks = [k] + others(k)
        cot_parts = to_sequence(cotangent)
        all_docs = jnp.concatenate([qdocs] + other_docs, axis=1)
        qstart = jnp.sum((all_docs[0][:, None] < qdocs).astype(jnp.int32), axis=0, keepdims=True)
        v = value_mix(normed, w_qkv, first)
        normed_x = flip(normed, low_e)
        normed_y = flip(normed, high_e)
        vs = [v] + others(v)
        attended, lse = attend(q, ks, vs, kpos, qpos, qstart)
        attended, normed_x, normed_y, cot_parts = tie(attended, normed_x, normed_y, cot_parts)
        cot = jnp.concatenate(cot_parts, axis=0)
        attended_y = flip(attended, high_e)
        cot_y = flip(cot, high_e)
        middle, nffn = middle_norm(x, attended, w_out, gain_f)
        nffn_x = flip(nffn, low_e)
        hidden, gg, gu, hk, hs, ak, a_s, bk, bs = ffn_acts(edges, nffn, cot, w_gate, w_up, w_down)
        hidden, gg, gu, hs, a_s, bs, nffn_x, cot_y, attended_y = tie(
            hidden, gg, gu, hs, a_s, bs, nffn_x, cot_y, attended_y
        )
        h_y = flip(hs, high_e)
        a_x = flip(a_s, low_e)
        out_blocks, (grad_mid, gbk, gbs, grad_att) = ffn_back(
            seqs, edges, hidden, gg, gu, w_gate, w_up, w_down, middle, cot, w_out, gain_f
        )
        gbs, bs, grad_att = tie(gbs, bs, grad_att)
        out_parts = from_sequence(out_blocks)
        b_x = flip(bs, low_e)
        gb_y = flip(gbs, high_e)
        gq, gk, gv, other_kv = attend_back(
            q, grad_att, ks, vs, lse, kpos, qpos, qstart, cosine, sines
        )
        gq, gk, gv, other_kv, h_y, a_x, out_parts = tie(
            gq, gk, gv, other_kv, h_y, a_x, out_parts
        )
        got_kv = [send(v, lambda i, g=g: shift_member(i, -g)) for g, v in enumerate(other_kv, 1)]
        per_down = ff // n
        per = width // n

        class Rows:
            def __init__(self, keep, got, top, skip):
                dims = (2,) * top + keep.shape[1:]
                self.terms = [keep.reshape(dims), got.reshape(dims)]
                self.left = list(range(top, 0, -1))
                self.order = [t for t in self.left if t >= blk_bits and t != skip]
                self.order += list(range(1, min(blk_bits, top + 1)))
                self.skip, self.swapped = skip, False

            def total(self, terms):
                return functools.reduce(lambda a, b: a + b, [t.astype(f32) for t in terms])

            def go(self):
                t = self.order.pop(0)
                axis, b = self.left.index(t), bit(t)
                out = self.total([pick(v, 1 - b, axis) for v in self.terms]).astype(bf16)
                self.terms = [pick(v, b, axis) for v in self.terms] + [flip(out, t)]
                self.left.pop(axis)

            def next(self):
                if self.order:
                    self.go()
                elif self.skip >= 0 and not self.swapped:
                    value, b = self.total(self.terms), bit(self.skip)
                    self.swapped = True
                    out = flip(pick(value, 1 - b).astype(bf16), self.skip)
                    self.terms = [pick(value, b), out]
                else:
                    return False
                return True

            def halves(self):
                mine, other = self.terms[0], self.terms[1].astype(f32)
                b = bit(self.skip)
                return jnp.stack([jnp.where(b == 0, mine, other), jnp.where(b == 0, other, mine)])

        def settle(values, *reductions):
            last = [r.terms[-1] for r in reductions]
            values, last = tie(values, last)
            for r, got in zip(reductions, last):
                r.terms[-1] = got
            return values

        ak2, as2 = outer(core, per, ([nffn, nffn_x], [ak, a_x]))
        ak2, as2, got_kv = tie(ak2, as2, got_kv)
        a_c = flip(as2, 0)
        packed, first_blocks, (qxk, qxs, qyk, qys) = grad_pack(
            seqs, edges, gq, gk, gv, got_kv, cosine, sines
        )
        packed, first_blocks, qxs, qys, a_c, hk, h_y = tie(
            packed, first_blocks, qxs, qys, a_c, hk, h_y
        )
        part_a = Rows(ak2, a_c, nbits - 1, low_e)
        part_a.next()
        q_x = flip(qxs, low_e)
        q_y = flip(qys, high_e)
        dk, ds = outer(core, per_down, ([hk, h_y], [cot, cot_y]))
        blocks = grad_inputs(seqs, packed, w_qkv, x, gain_a, grad_mid, first_blocks)
        blocks, dk, ds, bk, b_x, gb_y = tie(blocks, dk, ds, bk, b_x, gb_y)
        d_c = flip(ds, 0)
        moved = from_sequence(blocks)
        bk2, bs2 = outer(core, per, ([nffn, nffn_x], [bk, b_x]))
        bk2, bs2, d_c, q_x, q_y = tie(bk2, bs2, d_c, q_x, q_y)
        b_c = flip(bs2, 0)
        down = Rows(dk, d_c, nbits - 2, -1)
        down.next()
        qyk2, qys2 = outer(
            core, per, ([normed, normed_y], [qyk, q_y]), ([attended, attended_y], [gbk, gb_y])
        )
        qyk2, qys2, b_c, moved[1::2] = settle((qyk2, qys2, b_c, moved[1::2]), part_a)
        qy_c = flip(qys2, 0)
        part_b = Rows(bk2, b_c, nbits - 1, low_e)
        part_b.next()
        part_a.next()
        qxk2, qxs2 = outer(core, per, ([normed, normed_x], [qxk, q_x]))
        qxk2, qxs2, qy_c = settle((qxk2, qxs2, qy_c), part_a, down)
        qx_c = flip(qxs2, 0)
        part_y = Rows(qyk2, qy_c, nbits - 1, high_e)
        part_y.next()
        part_a.next()
        down.next()
        (qx_c,) = settle((qx_c,), part_a, part_b, down)
        part_x = Rows(qxk2, qx_c, nbits - 1, low_e)
        part_x.next()
        part_b.next()
        down.next()
        part_a.next()
        (moved,) = settle((moved,), part_a, part_b, part_y, down)
        everything = (part_a, part_b, part_y, part_x, down)
        while True:
            busy = [part for part in everything if part.next()]
            if not busy:
                break
            settle((), *busy)
        grad_down = down.total(down.terms)
        a_done, b_done, qx_done, qy_done = (
            part.halves() for part in (part_a, part_b, part_x, part_y)
        )
        (output,) = place([part[None] for part in out_parts], seq)
        grad_tokens, grad_first_values = place(moved, seq)

        acts = jnp.concatenate([a_done[0], a_done[1], b_done[0], b_done[1]], axis=1)
        grad_gate, grad_up = acts[:, :ff], acts[:, ff:]
        q_wide = 3 * width // 4
        grad_out = jnp.concatenate([qy_done[0, :, q_wide:], qy_done[1, :, q_wide:]], axis=1)
        qy_done = qy_done[:, :, :q_wide]
        pairs = width // LANES
        grad_qkv = jnp.concatenate([qx_done, qy_done], axis=0)
        grad_qkv = grad_qkv.reshape(4, per, pairs // 4, 3, LANES)
        grad_qkv = jnp.transpose(grad_qkv, (1, 3, 0, 2, 4)).reshape(per, 3 * width)

        def own(value):
            return lax.dynamic_slice_in_dim(value, index * per, per, 0)

        grad_gain_attn = jnp.sum(grad_qkv * own(w_qkv).astype(f32), axis=1) / own(gain_attn)
        grad_gain_ffn = (
            jnp.sum(
                grad_gate * own(w_gate).astype(f32) + grad_up * own(w_up).astype(f32), axis=1
            )
            / own(gain_ffn)
        )
        return (
            output,
            grad_tokens,
            grad_first_values,
            grad_qkv,
            grad_out,
            grad_gate,
            grad_up,
            grad_down,
            grad_gain_attn,
            grad_gain_ffn,
        )

    return shards


def solution(mesh):
    seq = P("dp", "blk", None)
    rows = P(AXES, None)
    vec = P(AXES)
    in_specs = (seq, seq, P("dp", "blk"), seq) + (P(),) * 7
    out_specs = (seq, seq, seq, rows, rows, rows, rows, rows, vec, vec)
    return jax.shard_map(
        build(mesh.shape["dp"], mesh.shape["blk"]),
        mesh=mesh,
        in_specs=in_specs,
        out_specs=out_specs,
        check_vma=False,
    )
```

```python
import functools

import jax
import jax.numpy as jnp
from jax import lax
from jax.experimental import pallas as pl
from jax.experimental.pallas import tpu as pltpu
from jax.sharding import PartitionSpec as P

HEAD_DIM = 64
LANES = 128
AXES = ("dp", "blk")
epsilon = 1e-06
score_scale = 0.125
cost_share = 3.0
VMEM_LIMIT = 16 << 20
bf16 = jnp.bfloat16
f32 = jnp.float32

NN = (((1,), (0,)), ((), ()))
NT = (((1,), (1,)), ((), ()))
TN = (((0,), (0,)), ((), ()))


def mm(a, b, dims):
    return lax.dot_general(a, b, dims, preferred_element_type=f32)


def sds(shape, dtype):
    return jax.ShapeDtypeStruct(shape, dtype)


def cost(flops, nbytes, trans=0):
    return pl.CostEstimate(
        flops=int(flops * cost_share), bytes_accessed=int(nbytes * cost_share), transcendentals=0
    )


def whole(shape):
    return pl.BlockSpec(shape, lambda *_: (0,) * len(shape))


def scalar():
    return pl.BlockSpec(memory_space=pltpu.SMEM)


RESIDENT = pl.BlockSpec(memory_space=pltpu.VMEM)


def lanes(step, width):
    return pl.ds(pl.multiple_of(step * width, width), width)


def resident_call(body, ins, outs, name, flops, scratch=(), scalars=1):
    nbytes = sum(a.size * a.dtype.itemsize for a in (*ins, *outs))
    return pl.pallas_call(
        body,
        in_specs=[scalar()] * scalars + [RESIDENT] * (len(ins) - scalars),
        out_specs=[RESIDENT] * len(outs),
        out_shape=list(outs),
        scratch_shapes=list(scratch),
        compiler_params=pltpu.CompilerParams(vmem_limit_bytes=VMEM_LIMIT),
        cost_estimate=cost(flops, nbytes),
        name=name,
    )(*ins)


def tie(*values):
    return lax.optimization_barrier(values)


def lane_half(shape):
    lane = lax.broadcasted_iota(jnp.int32, shape, len(shape) - 1)
    return (lane & (HEAD_DIM - 1)) < HEAD_DIM // 2


def turn(values):
    half = HEAD_DIM // 2
    return jnp.where(
        lane_half(values.shape),
        pltpu.roll(values, LANES - half, 1),
        pltpu.roll(values, half, 1),
    )


def head_mask(shape, head):
    lane = lax.broadcasted_iota(jnp.int32, shape, 1)
    return lane < HEAD_DIM if head == 0 else lane >= HEAD_DIM


def rotate_all(projected, cosine, sines):
    parts = []
    for i in range(projected.shape[1] // LANES):
        part = projected[:, i * LANES : (i + 1) * LANES]
        parts.append((part * cosine + turn(part) * sines).astype(bf16))
    return jnp.concatenate(parts, axis=1)


def query_key_body(x_ref, gain_ref, w_ref, cos_ref, sin_ref, normed_ref, q_ref, k_ref):
    inputs = x_ref[...].astype(f32)
    factor = lax.rsqrt(jnp.mean(inputs * inputs, axis=-1, keepdims=True) + epsilon)
    normed = (inputs * factor * gain_ref[...]).astype(bf16)
    normed_ref[...] = normed
    width = q_ref.shape[1]
    block = 256
    for j in range(2 * width // block):
        at = slice(j * block, (j + 1) * block)
        rotated = rotate_all(mm(normed, w_ref[:, at], NN), cos_ref[...], sin_ref[...])
        if j * block < width:
            q_ref[:, at] = rotated
        else:
            k_ref[:, slice(j * block - width, (j + 1) * block - width)] = rotated


def query_key(x, gain, w_qkv, cosine, sines):
    rows, width = x.shape
    return resident_call(
        query_key_body,
        (x, gain, w_qkv, cosine, sines),
        [sds((rows, width), bf16)] * 3,
        "query_key",
        4 * rows * width * width,
        scalars=0,
    )


def value_mix_body(normed_ref, w_ref, first_ref, out_ref):
    width = out_ref.shape[1]
    block = 256
    for j in range(width // block):
        at = slice(j * block, (j + 1) * block)
        projected = mm(normed_ref[...], w_ref[:, 2 * width + j * block : 2 * width + (j + 1) * block], NN)
        out_ref[:, at] = (0.5 * projected + 0.5 * first_ref[:, at].astype(f32)).astype(bf16)


def value_mix(normed, w_qkv, first):
    rows, width = normed.shape
    return resident_call(
        value_mix_body,
        (normed, w_qkv, first),
        [sds((rows, width), bf16)],
        "value_mix",
        2 * rows * width * width,
        scalars=0,
    )[0]


def set_bias(bias_ref, kpos_ref, qpos_ref, qstart_ref):
    keys, qpos = kpos_ref[...], qpos_ref[...]
    allowed = (keys <= qpos) & (keys >= qstart_ref[...])
    bias_ref[...] = jnp.where(allowed, 0.0, -1e30)


def attend_body(slots, *refs):
    q_ref = refs[0]
    k_refs = refs[1 : 1 + slots]
    v_refs = refs[1 + slots : 1 + 2 * slots]
    kpos_ref, qpos_ref, qstart_ref, out_ref, lse_ref, bias_ref = refs[1 + 2 * slots :]

    @pl.when(pl.program_id(0) == 0)
    def _():
        set_bias(bias_ref, kpos_ref, qpos_ref, qstart_ref)

    queries = q_ref[...] * jnp.asarray(score_scale, bf16)
    keys = jnp.concatenate([r[...] for r in k_refs], axis=0)
    values = jnp.concatenate([r[...] for r in v_refs], axis=0)
    values_t = jnp.transpose(values)
    outs = []
    for head in range(2):
        own = jnp.where(head_mask(queries.shape, head), queries, jnp.zeros_like(queries))
        scores = mm(keys, own, NT) + bias_ref[...]
        top = jnp.max(scores, axis=0, keepdims=True)
        weights = jnp.exp(scores - top)
        total = jnp.sum(weights, axis=0, keepdims=True)
        probs = (weights * (1.0 / total)).astype(bf16)
        outs.append(mm(values_t[head * HEAD_DIM : (head + 1) * HEAD_DIM], probs, NN))
        lse_ref[0, head : head + 1, :] = top + jnp.log(total)
    out_ref[...] = jnp.transpose(jnp.concatenate(outs, axis=0)).astype(bf16)


def attend(q, ks, vs, kpos, qpos, qstart):
    rows, width = q.shape
    slots = len(ks)
    pairs = width // LANES
    keys = slots * rows
    col = pl.BlockSpec((rows, LANES), lambda i: (0, i))
    return pl.pallas_call(
        functools.partial(attend_body, slots),
        grid=(pairs,),
        in_specs=[col]
        + [col] * slots
        + [col] * slots
        + [whole((keys, 1)), whole((1, rows)), whole((1, rows))],
        out_specs=[col, pl.BlockSpec((1, 2, rows), lambda i: (i, 0, 0))],
        out_shape=[sds((rows, width), bf16), sds((pairs, 2, rows), f32)],
        scratch_shapes=[pltpu.VMEM((keys, rows), f32)],
        cost_estimate=cost(
            8 * pairs * rows * keys * LANES, 2 * rows * width * (2 + 2 * slots), 2 * pairs * rows * keys
        ),
        name="attend",
    )(q, *ks, *vs, kpos, qpos, qstart)


def attend_back_body(slots, *refs):
    q_ref, grad_ref = refs[:2]
    k_refs = refs[2 : 2 + slots]
    v_refs = refs[2 + slots : 2 + 2 * slots]
    lse_ref, kpos_ref, qpos_ref, qstart_ref, cos_ref, sin_ref = refs[2 + 2 * slots : 8 + 2 * slots]
    gq_ref, gk_ref, gv_ref = refs[8 + 2 * slots : 11 + 2 * slots]
    other_refs = refs[11 + 2 * slots : 10 + 3 * slots]
    bias_ref = refs[-1]

    @pl.when(pl.program_id(0) == 0)
    def _():
        set_bias(bias_ref, kpos_ref, qpos_ref, qstart_ref)

    queries = q_ref[...] * jnp.asarray(score_scale, bf16)
    grads = grad_ref[...]
    keys = jnp.concatenate([r[...] for r in k_refs], axis=0)
    values = jnp.concatenate([r[...] for r in v_refs], axis=0)
    keys_t = jnp.transpose(keys)
    grad_values = grad_keys = None
    grad_q = []
    for head in range(2):
        mask = head_mask(queries.shape, head)
        own_q = jnp.where(mask, queries, jnp.zeros_like(queries))
        own_g = jnp.where(mask, grads, jnp.zeros_like(grads))
        scores = mm(keys, own_q, NT) + bias_ref[...]
        probs = jnp.exp(scores - lse_ref[0, head : head + 1, :])
        grad_probs = mm(values, own_g, NT)
        delta = jnp.sum(probs * grad_probs, axis=0, keepdims=True)
        grad_scores = (probs * (grad_probs - delta)).astype(bf16)
        part_v = mm(probs.astype(bf16), own_g, NN)
        part_k = mm(grad_scores, own_q, NN)
        grad_values = part_v if grad_values is None else grad_values + part_v
        grad_keys = part_k if grad_keys is None else grad_keys + part_k
        grad_q.append(mm(keys_t[head * HEAD_DIM : (head + 1) * HEAD_DIM], grad_scores, NN))
    grad_q = jnp.transpose(jnp.concatenate(grad_q, axis=0)) * score_scale
    gq_ref[...] = (grad_q * cos_ref[...] - turn(grad_q) * sin_ref[...]).astype(bf16)
    rows = q_ref.shape[0]
    gk_ref[...] = grad_keys[:rows]
    gv_ref[...] = grad_values[:rows]
    for slot in range(1, slots):
        other_refs[slot - 1][0] = grad_keys[slot * rows : (slot + 1) * rows].astype(bf16)
        other_refs[slot - 1][1] = grad_values[slot * rows : (slot + 1) * rows].astype(bf16)


def attend_back(q, grad, ks, vs, lse, kpos, qpos, qstart, cosine, sines):
    rows, width = q.shape
    slots = len(ks)
    pairs = width // LANES
    keys = slots * rows
    col = pl.BlockSpec((rows, LANES), lambda i: (0, i))
    outs = pl.pallas_call(
        functools.partial(attend_back_body, slots),
        grid=(pairs,),
        in_specs=[col, col]
        + [col] * slots
        + [col] * slots
        + [pl.BlockSpec((1, 2, rows), lambda i: (i, 0, 0))]
        + [whole((keys, 1)), whole((1, rows)), whole((1, rows))]
        + [whole((rows, LANES))] * 2,
        out_specs=[col] * 3 + [pl.BlockSpec((2, rows, LANES), lambda i: (0, 0, i))] * (slots - 1),
        out_shape=[sds((rows, width), bf16)]
        + [sds((rows, width), f32)] * 2
        + [sds((2, rows, width), bf16)] * (slots - 1),
        scratch_shapes=[pltpu.VMEM((keys, rows), f32)],
        cost_estimate=cost(
            20 * pairs * rows * keys * LANES, 2 * rows * width * (7 + 4 * slots), 2 * pairs * rows * keys
        ),
        name="attend_back",
    )(q, grad, *ks, *vs, lse, kpos, qpos, qstart, cosine, sines)
    return (*outs[:3], outs[3:])


def middle_body(x_ref, att_ref, wout_ref, gain_ref, mid_ref, nffn_ref):
    middle = x_ref[...].astype(f32) + mm(att_ref[...], wout_ref[...], NN)
    mid_ref[...] = middle
    factor = lax.rsqrt(jnp.mean(middle * middle, axis=-1, keepdims=True) + epsilon)
    nffn_ref[...] = (middle * factor * gain_ref[...]).astype(bf16)


def middle_norm(x, attended, w_out, gain):
    rows, width = x.shape
    return resident_call(
        middle_body,
        (x, attended, w_out, gain),
        [sds((rows, width), f32), sds((rows, width), bf16)],
        "middle_norm",
        2 * rows * width * width,
        scalars=0,
    )


def ffn_acts_body(
    sizes,
    edge_ref,
    nffn_ref,
    cot_ref,
    wg_ref,
    wu_ref,
    wd_ref,
    hid_ref,
    gg_ref,
    gu_ref,
    hk_ref,
    hs_ref,
    ak_ref,
    as_ref,
    bk_ref,
    bs_ref,
):
    total, hid_half, a_half, b_half = sizes
    block = 256
    per = block // LANES
    for step in range(total // per):
        at = slice(step * block, (step + 1) * block)
        gate = mm(nffn_ref[...], wg_ref[:, at], NN)
        upward = mm(nffn_ref[...], wu_ref[:, at], NN)
        grad_hidden = mm(cot_ref[...], wd_ref[at, :], NT)
        sig = 1.0 / (1.0 + jnp.exp(-gate))
        silu = gate * sig
        hid_ref[:, at] = (silu * upward).astype(bf16)
        gg_ref[:, at] = (grad_hidden * upward * (sig * (1.0 + gate * (1.0 - sig)))).astype(bf16)
        gu_ref[:, at] = (grad_hidden * silu).astype(bf16)

    low_edge, high_edge = edge_ref[0], edge_ref[1]

    def halves(edge, keep_ref, send_ref, size, places):
        for half in range(2):
            runs = []
            for offset in range(size):
                source, start = places[half * size + offset]
                if runs and runs[-1][0] is source and runs[-1][2] == start:
                    runs[-1][2] += 1
                else:
                    runs.append([source, start, start + 1, offset])
            for source, start, stop, offset in runs:
                src = slice(start * LANES, stop * LANES)
                dst = slice(offset * LANES, (offset + stop - start) * LANES)

                @pl.when(edge == half)
                def _(source=source, src=src, dst=dst):
                    keep_ref[:, dst] = source[:, src]

                @pl.when(edge != half)
                def _(source=source, src=src, dst=dst):
                    send_ref[:, dst] = source[:, src]

    acts = [(gg_ref, i) for i in range(total)] + [(gu_ref, i) for i in range(total)]
    halves(high_edge, hk_ref, hs_ref, hid_half, [(hid_ref, i) for i in range(total)])
    halves(low_edge, ak_ref, as_ref, a_half, acts[: 2 * a_half])
    halves(low_edge, bk_ref, bs_ref, b_half, acts[2 * a_half :])


def half_blocks(ff):
    total = ff // LANES
    a_half = (total + 1) // 2 + (total // 2) % 2
    return total, total // 2, a_half, total - a_half


def ffn_acts(edges, nffn, cot, w_gate, w_up, w_down):
    rows, width = nffn.shape
    ff = w_gate.shape[1]
    sizes = half_blocks(ff)
    _, hid_half, a_half, b_half = sizes
    widths = [ff] * 3 + [hid_half * LANES] * 2 + [a_half * LANES] * 2 + [b_half * LANES] * 2
    return resident_call(
        functools.partial(ffn_acts_body, sizes),
        (edges, nffn, cot, w_gate, w_up, w_down),
        [sds((rows, w), bf16) for w in widths],
        "ffn_acts",
        6 * rows * width * ff,
    )


def ffn_back_body(
    seqs,
    edge_ref,
    hid_ref,
    gg_ref,
    gu_ref,
    wg_ref,
    wu_ref,
    wd_ref,
    mid_ref,
    cot_ref,
    wout_ref,
    gain_ref,
    *refs,
):
    out_refs = refs[:seqs]
    gmid_ref, keep_ref, send_ref, gatt_ref = refs[seqs:]
    length = out_refs[0].shape[0]
    middle = mid_ref[...]
    grads = mm(gg_ref[...], wg_ref[...], NT) + mm(gu_ref[...], wu_ref[...], NT)
    factor = lax.rsqrt(jnp.mean(middle * middle, axis=-1, keepdims=True) + epsilon)
    scaled = grads * gain_ref[...]
    inner = jnp.mean(scaled * middle, axis=-1, keepdims=True)
    grad_middle = cot_ref[...].astype(f32) + factor * (scaled - middle * (factor * factor * inner))
    gmid_ref[...] = grad_middle
    branch = grad_middle.astype(bf16)
    half = branch.shape[1] // 2

    @pl.when(edge_ref[1] == 0)
    def _():
        keep_ref[...] = branch[:, :half]
        send_ref[...] = branch[:, half:]

    @pl.when(edge_ref[1] != 0)
    def _():
        keep_ref[...] = branch[:, half:]
        send_ref[...] = branch[:, :half]

    gatt_ref[...] = mm(branch, wout_ref[...], NT).astype(bf16)
    out = middle + mm(hid_ref[...], wd_ref[...], NN)
    for s in range(seqs):
        out_refs[s][...] = out[s * length : (s + 1) * length].astype(bf16)


def ffn_back(seqs, edges, hidden, gg, gu, w_gate, w_up, w_down, middle, cot, w_out, gain):
    rows, width = cot.shape
    ff = w_gate.shape[1]
    outs = resident_call(
        functools.partial(ffn_back_body, seqs),
        (edges, hidden, gg, gu, w_gate, w_up, w_down, middle, cot, w_out, gain),
        [sds((rows // seqs, width), bf16)] * seqs
        + [
            sds((rows, width), f32),
            sds((rows, width // 2), bf16),
            sds((rows, width // 2), bf16),
            sds((rows, width), bf16),
        ],
        "ffn_back",
        6 * rows * width * ff + 2 * rows * width * width,
    )
    return outs[:seqs], outs[seqs:]


def grad_pack_body(seqs, received, edge_ref, *refs):
    gq_ref, gk_ref, gv_ref = refs[:3]
    others = refs[3 : 3 + received]
    cos_ref, sin_ref, packed_ref = refs[3 + received : 6 + received]
    first_refs = refs[6 + received : 6 + received + seqs]
    xk_ref, xs_ref, yk_ref, ys_ref = refs[6 + received + seqs :]
    width = gq_ref.shape[1]
    length = first_refs[0].shape[0]
    low_edge, high_edge = edge_ref[0], edge_ref[1]
    pairs = width // LANES
    quarter = pairs // 4
    for pair in range(pairs):
        at = slice(pair * LANES, (pair + 1) * LANES)
        at_v = slice(width + pair * LANES, width + (pair + 1) * LANES)
        grad_k, grad_v = gk_ref[:, at], gv_ref[:, at]
        for r in others:
            grad_k = grad_k + r[0, :, at].astype(f32)
            grad_v = grad_v + r[1, :, at].astype(f32)
        grad_k = (grad_k * cos_ref[...] - turn(grad_k) * sin_ref[...]).astype(bf16)
        grad_v = (0.5 * grad_v).astype(bf16)
        for s in range(seqs):
            first_refs[s][:, at] = grad_v[s * length : (s + 1) * length]
        packed_ref[:, at] = gq_ref[:, at]
        packed_ref[:, at_v] = grad_k
        packed_ref[:, 2 * width + pair * LANES : 2 * width + (pair + 1) * LANES] = grad_v
        packed = jnp.concatenate([gq_ref[:, at], grad_k, grad_v], axis=1)
        color, half = pair // (2 * quarter), pair // quarter % 2
        edge = high_edge if color else low_edge
        keep_ref, send_ref = (yk_ref, ys_ref) if color else (xk_ref, xs_ref)
        dst = slice(pair % quarter * 3 * LANES, (pair % quarter + 1) * 3 * LANES)

        @pl.when(edge == half)
        def _(keep_ref=keep_ref, dst=dst, packed=packed):
            keep_ref[:, dst] = packed

        @pl.when(edge != half)
        def _(send_ref=send_ref, dst=dst, packed=packed):
            send_ref[:, dst] = packed


def grad_pack(seqs, edges, gq, gk, gv, others, cosine, sines):
    rows, width = gq.shape
    outs = resident_call(
        functools.partial(grad_pack_body, seqs, len(others)),
        (edges, gq, gk, gv, *others, cosine, sines),
        [sds((rows, 3 * width), bf16)]
        + [sds((rows // seqs, width), bf16)] * seqs
        + [sds((rows, 3 * width // 4), bf16)] * 4,
        "grad_pack",
        20 * rows * width,
    )
    return outs[0], outs[1 : 1 + seqs], outs[1 + seqs :]


def grad_inputs_body(seqs, packed_ref, w_ref, x_ref, gain_ref, gmid_ref, *refs):
    first_refs, out_refs = refs[:seqs], refs[seqs:]
    grads = mm(packed_ref[...], w_ref[...], NT)
    inputs = x_ref[...].astype(f32)
    factor = lax.rsqrt(jnp.mean(inputs * inputs, axis=-1, keepdims=True) + epsilon)
    scaled = grads * gain_ref[...]
    inner = jnp.mean(scaled * inputs, axis=-1, keepdims=True)
    grads = gmid_ref[...] + factor * (scaled - inputs * (factor * factor * inner))
    grads = grads.astype(bf16)
    length = out_refs[0].shape[1]
    for s in range(seqs):
        out_refs[s][0] = grads[s * length : (s + 1) * length]
        out_refs[s][1] = first_refs[s][...]


def grad_inputs(seqs, packed, w_qkv, x, gain, grad_middle, first_blocks):
    rows, width = x.shape
    return resident_call(
        functools.partial(grad_inputs_body, seqs),
        (packed, w_qkv, x, gain, grad_middle, *first_blocks),
        [sds((2, rows // seqs, width), bf16)] * seqs,
        "grad_inputs",
        6 * rows * width * width,
        scalars=0,
    )


def place_body(seqs, shift_ref, *refs):
    for i, out_ref in enumerate(refs[seqs:]):
        for j in range(seqs):
            for s in range(seqs):

                @pl.when(lax.rem(shift_ref[0] + s, seqs) == j)
                def _(i=i, j=j, s=s, out_ref=out_ref):
                    out_ref[j] = refs[s][i]


def place(parts, seq):
    seqs = len(parts)
    count, length, width = parts[0].shape
    part = pl.BlockSpec((count, length, width // 4), lambda i: (0, 0, i))
    return pl.pallas_call(
        functools.partial(place_body, seqs),
        grid=(4,),
        in_specs=[scalar()] + [part] * seqs,
        out_specs=[pl.BlockSpec((seqs, length, width // 4), lambda i: (0, 0, i))] * count,
        out_shape=[sds((seqs, length, width), bf16)] * count,
        compiler_params=pltpu.CompilerParams(vmem_limit_bytes=VMEM_LIMIT),
        cost_estimate=cost(0, 4 * seqs * count * length * width),
        name="place",
    )(seq[None], *parts)


def outer_body(counts, per, core_ref, *refs):
    keep_ref, send_ref = refs[-2:]
    column = at = 0
    core = core_ref[0]
    for count in counts:
        lefts, rights = refs[at : at + count], refs[at + count : at + 2 * count]
        at += 2 * count
        total = None
        for left, right in zip(lefts, rights):
            part = mm(left[...], right[...], TN)
            total = part if total is None else total + part
        wide = total.shape[1]
        cut = slice(column, column + wide)
        column += wide
        total = total.astype(bf16)
        for i in range(total.shape[0] // (2 * per)):
            even = total[2 * i * per : (2 * i + 1) * per]
            odd = total[(2 * i + 1) * per : (2 * i + 2) * per]

            @pl.when(core == 0)
            def _(i=i, even=even, odd=odd, cut=cut):
                keep_ref[i, :, cut] = even
                send_ref[i, :, cut] = odd

            @pl.when(core != 0)
            def _(i=i, even=even, odd=odd, cut=cut):
                keep_ref[i, :, cut] = odd
                send_ref[i, :, cut] = even


def outer(core, per, *groups):
    rows, height = groups[0][0][0].shape
    width = sum(rights[0].shape[1] for _, rights in groups)
    block = 256 if height % 256 == 0 else height
    specs, args, flops = [], [], 0
    for lefts, rights in groups:
        wide = rights[0].shape[1]
        specs += [pl.BlockSpec((rows, block), lambda i: (0, i))] * len(lefts)
        specs += [whole((rows, wide))] * len(rights)
        args += [*lefts, *rights]
        flops += 2 * len(lefts) * rows * height * wide
    out_spec = pl.BlockSpec((block // (2 * per), per, width), lambda i: (i, 0, 0))
    return pl.pallas_call(
        functools.partial(outer_body, [len(lefts) for lefts, _ in groups], per),
        grid=(height // block,),
        in_specs=[scalar()] + specs,
        out_specs=[out_spec] * 2,
        out_shape=[sds((height // (2 * per), per, width), bf16)] * 2,
        cost_estimate=cost(flops, 2 * (sum(a.size for a in args) + height * width)),
        name="outer",
    )(core[None], *args)


def build(ndp, nblk):
    n = ndp * nblk
    nbits = n.bit_length() - 1
    blk_bits = nblk.bit_length() - 1
    if (1 << nbits) != n or (1 << blk_bits) != nblk:
        raise ValueError("mesh sizes")
    low_e, high_e = blk_bits, nbits - 1

    def send(value, target):
        pairs = [(i, target(i)) for i in range(n)]
        return lax.ppermute(value, AXES, pairs)

    def flip(value, bit):
        return send(value, lambda i: i ^ (1 << bit))

    def pick(value, index, axis=0):
        return lax.dynamic_index_in_dim(value, index, axis, keepdims=False)

    def shards(
        tokens, first_values, docs, cotangent, w_qkv, w_out, w_gate, w_up, w_down, gain_attn, gain_ffn
    ):
        seqs, length, width = tokens.shape
        ff = w_gate.shape[1]
        rows = seqs * length
        group = nblk // seqs
        blk = lax.axis_index("blk")
        index = lax.axis_index("dp") * nblk + blk
        seq, member = blk // group, blk % group

        def bit(t):
            return (index >> t) & 1

        core = bit(0)
        edges = jnp.stack([bit(low_e), bit(high_e)])

        def shift_seq(i, s):
            base, b = i - i % nblk, i % nblk
            return base + ((b // group + s) % seqs) * group + b % group

        def shift_member(i, s):
            base, b = i - i % nblk, i % nblk
            return base + (b // group) * group + (b % group + s) % group

        def to_sequence(value):
            parts = [pick(value, seq)]
            for s in range(1, seqs):
                out = pick(value, (seq + s) % seqs)
                parts.append(send(out, lambda i, s=s: shift_seq(i, s)))
            return parts

        def from_sequence(blocks):
            return [
                part if s == 0 else send(part, lambda i, s=s: shift_seq(i, -s))
                for s, part in enumerate(blocks)
            ]

        def others(value):
            return [send(value, lambda i, g=g: shift_member(i, g)) for g in range(1, group)]

        marks = jnp.pad(docs[:, None, :].astype(bf16), ((0, 0), (0, 7), (0, width - length)))
        parts = to_sequence(jnp.concatenate([tokens, marks, first_values], axis=1))

        base = jnp.arange(length, dtype=jnp.int32)
        qpos = jnp.concatenate(
            [(((seq - s) % seqs) * group + member) * length + base for s in range(seqs)]
        )
        kpos = jnp.concatenate(
            [
                (((seq - s) % seqs) * group + (member - g) % group) * length + base
                for g in range(group)
                for s in range(seqs)
            ]
        )
        half = HEAD_DIM // 2
        inverse = 10000.0 ** (-jnp.arange(half, dtype=f32) / half)
        angles = qpos.astype(f32)[:, None] * inverse[None, :]
        cos_half, sin_half = jnp.cos(angles), jnp.sin(angles)
        cosine = jnp.concatenate([cos_half] * 4, axis=1)
        sines = jnp.concatenate([-sin_half, sin_half] * 2, axis=1)
        qpos, kpos = qpos[None, :], kpos[:, None]
        gain_a, gain_f = gain_attn[None, :], gain_ffn[None, :]

        cosine, sines, qpos, kpos, parts, cotangent = tie(
            cosine, sines, qpos, kpos, parts, cotangent
        )
        x = jnp.concatenate([p[:length] for p in parts], axis=0)
        first = jnp.concatenate([p[-length:] for p in parts], axis=0)
        qdocs = jnp.concatenate([p[length, :length] for p in parts]).astype(jnp.int32)[None]
        normed, q, k = query_key(x, gain_a, w_qkv, cosine, sines)
        other_docs = others(qdocs)
        ks = [k] + others(k)
        cot_parts = to_sequence(cotangent)
        all_docs = jnp.concatenate([qdocs] + other_docs, axis=1)
        qstart = jnp.sum((all_docs[0][:, None] < qdocs).astype(jnp.int32), axis=0, keepdims=True)
        v = value_mix(normed, w_qkv, first)
        normed_x = flip(normed, low_e)
        normed_y = flip(normed, high_e)
        vs = [v] + others(v)
        attended, lse = attend(q, ks, vs, kpos, qpos, qstart)
        attended, normed_x, normed_y, cot_parts = tie(attended, normed_x, normed_y, cot_parts)
        cot = jnp.concatenate(cot_parts, axis=0)
        attended_y = flip(attended, high_e)
        cot_y = flip(cot, high_e)
        middle, nffn = middle_norm(x, attended, w_out, gain_f)
        nffn_x = flip(nffn, low_e)
        hidden, gg, gu, hk, hs, ak, a_s, bk, bs = ffn_acts(edges, nffn, cot, w_gate, w_up, w_down)
        hidden, gg, gu, hs, a_s, bs, nffn_x, cot_y, attended_y = tie(
            hidden, gg, gu, hs, a_s, bs, nffn_x, cot_y, attended_y
        )
        h_y = flip(hs, high_e)
        a_x = flip(a_s, low_e)
        out_blocks, (grad_mid, gbk, gbs, grad_att) = ffn_back(
            seqs, edges, hidden, gg, gu, w_gate, w_up, w_down, middle, cot, w_out, gain_f
        )
        gbs, bs, grad_att = tie(gbs, bs, grad_att)
        out_parts = from_sequence(out_blocks)
        b_x = flip(bs, low_e)
        gb_y = flip(gbs, high_e)
        gq, gk, gv, other_kv = attend_back(
            q, grad_att, ks, vs, lse, kpos, qpos, qstart, cosine, sines
        )
        gq, gk, gv, other_kv, h_y, a_x, out_parts = tie(
            gq, gk, gv, other_kv, h_y, a_x, out_parts
        )
        got_kv = [send(v, lambda i, g=g: shift_member(i, -g)) for g, v in enumerate(other_kv, 1)]
        per_down = ff // n
        per = width // n

        class Rows:
            def __init__(self, keep, got, top, skip):
                dims = (2,) * top + keep.shape[1:]
                self.terms = [keep.reshape(dims), got.reshape(dims)]
                self.left = list(range(top, 0, -1))
                self.order = [t for t in self.left if t >= blk_bits and t != skip]
                self.order += list(range(1, min(blk_bits, top + 1)))
                self.skip, self.swapped = skip, False

            def total(self, terms):
                return functools.reduce(lambda a, b: a + b, [t.astype(f32) for t in terms])

            def go(self):
                t = self.order.pop(0)
                axis, b = self.left.index(t), bit(t)
                out = self.total([pick(v, 1 - b, axis) for v in self.terms]).astype(bf16)
                self.terms = [pick(v, b, axis) for v in self.terms] + [flip(out, t)]
                self.left.pop(axis)

            def next(self):
                if self.order:
                    self.go()
                elif self.skip >= 0 and not self.swapped:
                    value, b = self.total(self.terms), bit(self.skip)
                    self.swapped = True
                    out = flip(pick(value, 1 - b).astype(bf16), self.skip)
                    self.terms = [pick(value, b), out]
                else:
                    return False
                return True

            def halves(self):
                mine, other = self.terms[0], self.terms[1].astype(f32)
                b = bit(self.skip)
                return jnp.stack([jnp.where(b == 0, mine, other), jnp.where(b == 0, other, mine)])

        def settle(values, *reductions):
            last = [r.terms[-1] for r in reductions]
            values, last = tie(values, last)
            for r, got in zip(reductions, last):
                r.terms[-1] = got
            return values

        ak2, as2 = outer(core, per, ([nffn, nffn_x], [ak, a_x]))
        ak2, as2, got_kv = tie(ak2, as2, got_kv)
        a_c = flip(as2, 0)
        packed, first_blocks, (qxk, qxs, qyk, qys) = grad_pack(
            seqs, edges, gq, gk, gv, got_kv, cosine, sines
        )
        packed, first_blocks, qxs, qys, a_c, hk, h_y = tie(
            packed, first_blocks, qxs, qys, a_c, hk, h_y
        )
        part_a = Rows(ak2, a_c, nbits - 1, low_e)
        part_a.next()
        q_x = flip(qxs, low_e)
        q_y = flip(qys, high_e)
        dk, ds = outer(core, per_down, ([hk, h_y], [cot, cot_y]))
        blocks = grad_inputs(seqs, packed, w_qkv, x, gain_a, grad_mid, first_blocks)
        blocks, dk, ds, bk, b_x, gb_y = settle((blocks, dk, ds, bk, b_x, gb_y), part_a)
        d_c = flip(ds, 0)
        moved = from_sequence(blocks)
        bk2, bs2 = outer(core, per, ([nffn, nffn_x], [bk, b_x]))
        bk2, bs2, d_c, q_x, q_y = tie(bk2, bs2, d_c, q_x, q_y)
        b_c = flip(bs2, 0)
        down = Rows(dk, d_c, nbits - 2, -1)
        down.next()
        qyk2, qys2 = outer(
            core, per, ([normed, normed_y], [qyk, q_y]), ([attended, attended_y], [gbk, gb_y])
        )
        qyk2, qys2, b_c, moved[1::2] = tie(qyk2, qys2, b_c, moved[1::2])
        qy_c = flip(qys2, 0)
        part_b = Rows(bk2, b_c, nbits - 1, low_e)
        part_b.next()
        part_a.next()
        qxk2, qxs2 = outer(core, per, ([normed, normed_x], [qxk, q_x]))
        qxk2, qxs2, qy_c = settle((qxk2, qxs2, qy_c), part_a, down)
        qx_c = flip(qxs2, 0)
        part_y = Rows(qyk2, qy_c, nbits - 1, high_e)
        part_y.next()
        part_a.next()
        down.next()
        (qx_c,) = settle((qx_c,), part_a, part_b, down)
        part_x = Rows(qxk2, qx_c, nbits - 1, low_e)
        part_x.next()
        part_b.next()
        down.next()
        part_a.next()
        (moved,) = settle((moved,), part_a, part_b, part_y, down)
        everything = (part_a, part_b, part_y, part_x, down)
        while True:
            busy = [part for part in everything if part.next()]
            if not busy:
                break
            settle((), *busy)
        grad_down = down.total(down.terms)
        a_done, b_done, qx_done, qy_done = (
            part.halves() for part in (part_a, part_b, part_x, part_y)
        )
        (output,) = place([part[None] for part in out_parts], seq)
        grad_tokens, grad_first_values = place(moved, seq)

        acts = jnp.concatenate([a_done[0], a_done[1], b_done[0], b_done[1]], axis=1)
        grad_gate, grad_up = acts[:, :ff], acts[:, ff:]
        q_wide = 3 * width // 4
        grad_out = jnp.concatenate([qy_done[0, :, q_wide:], qy_done[1, :, q_wide:]], axis=1)
        qy_done = qy_done[:, :, :q_wide]
        pairs = width // LANES
        grad_qkv = jnp.concatenate([qx_done, qy_done], axis=0)
        grad_qkv = grad_qkv.reshape(4, per, pairs // 4, 3, LANES)
        grad_qkv = jnp.transpose(grad_qkv, (1, 3, 0, 2, 4)).reshape(per, 3 * width)

        def own(value):
            return lax.dynamic_slice_in_dim(value, index * per, per, 0)

        grad_gain_attn = jnp.sum(grad_qkv * own(w_qkv).astype(f32), axis=1) / own(gain_attn)
        grad_gain_ffn = (
            jnp.sum(
                grad_gate * own(w_gate).astype(f32) + grad_up * own(w_up).astype(f32), axis=1
            )
            / own(gain_ffn)
        )
        return (
            output,
            grad_tokens,
            grad_first_values,
            grad_qkv,
            grad_out,
            grad_gate,
            grad_up,
            grad_down,
            grad_gain_attn,
            grad_gain_ffn,
        )

    return shards


def solution(mesh):
    seq = P("dp", "blk", None)
    rows = P(AXES, None)
    vec = P(AXES)
    in_specs = (seq, seq, P("dp", "blk"), seq) + (P(),) * 7
    out_specs = (seq, seq, seq, rows, rows, rows, rows, rows, vec, vec)
    return jax.shard_map(
        build(mesh.shape["dp"], mesh.shape["blk"]),
        mesh=mesh,
        in_specs=in_specs,
        out_specs=out_specs,
        check_vma=False,
    )
```

```python
import functools

import jax
import jax.numpy as jnp
from jax import lax
from jax.experimental import pallas as pl
from jax.experimental.pallas import tpu as pltpu
from jax.sharding import PartitionSpec as P

HEAD_DIM = 64
LANES = 128
AXES = ("dp", "blk")
epsilon = 1e-06
score_scale = 0.125
cost_share = 2.0
VMEM_LIMIT = 16 << 20
bf16 = jnp.bfloat16
f32 = jnp.float32

NN = (((1,), (0,)), ((), ()))
NT = (((1,), (1,)), ((), ()))
TN = (((0,), (0,)), ((), ()))


def mm(a, b, dims):
    return lax.dot_general(a, b, dims, preferred_element_type=f32)


def sds(shape, dtype):
    return jax.ShapeDtypeStruct(shape, dtype)


def cost(flops, nbytes, trans=0):
    return pl.CostEstimate(
        flops=int(flops * cost_share), bytes_accessed=int(nbytes * cost_share), transcendentals=0
    )


def whole(shape):
    return pl.BlockSpec(shape, lambda *_: (0,) * len(shape))


def scalar():
    return pl.BlockSpec(memory_space=pltpu.SMEM)


RESIDENT = pl.BlockSpec(memory_space=pltpu.VMEM)


def lanes(step, width):
    return pl.ds(pl.multiple_of(step * width, width), width)


def resident_call(body, ins, outs, name, flops, scratch=(), scalars=1):
    nbytes = sum(a.size * a.dtype.itemsize for a in (*ins, *outs))
    return pl.pallas_call(
        body,
        in_specs=[scalar()] * scalars + [RESIDENT] * (len(ins) - scalars),
        out_specs=[RESIDENT] * len(outs),
        out_shape=list(outs),
        scratch_shapes=list(scratch),
        compiler_params=pltpu.CompilerParams(vmem_limit_bytes=VMEM_LIMIT),
        cost_estimate=cost(flops, nbytes),
        name=name,
    )(*ins)


def tie(*values):
    return lax.optimization_barrier(values)


def lane_half(shape):
    lane = lax.broadcasted_iota(jnp.int32, shape, len(shape) - 1)
    return (lane & (HEAD_DIM - 1)) < HEAD_DIM // 2


def turn(values):
    half = HEAD_DIM // 2
    return jnp.where(
        lane_half(values.shape),
        pltpu.roll(values, LANES - half, 1),
        pltpu.roll(values, half, 1),
    )


def head_mask(shape, head):
    lane = lax.broadcasted_iota(jnp.int32, shape, 1)
    return lane < HEAD_DIM if head == 0 else lane >= HEAD_DIM


def rotate_all(projected, cosine, sines):
    parts = []
    for i in range(projected.shape[1] // LANES):
        part = projected[:, i * LANES : (i + 1) * LANES]
        parts.append((part * cosine + turn(part) * sines).astype(bf16))
    return jnp.concatenate(parts, axis=1)


def query_key_body(x_ref, gain_ref, w_ref, cos_ref, sin_ref, normed_ref, q_ref, k_ref):
    inputs = x_ref[...].astype(f32)
    factor = lax.rsqrt(jnp.mean(inputs * inputs, axis=-1, keepdims=True) + epsilon)
    normed = (inputs * factor * gain_ref[...]).astype(bf16)
    normed_ref[...] = normed
    width = q_ref.shape[1]
    block = 256
    for j in range(2 * width // block):
        at = slice(j * block, (j + 1) * block)
        rotated = rotate_all(mm(normed, w_ref[:, at], NN), cos_ref[...], sin_ref[...])
        if j * block < width:
            q_ref[:, at] = rotated
        else:
            k_ref[:, slice(j * block - width, (j + 1) * block - width)] = rotated


def query_key(x, gain, w_qkv, cosine, sines):
    rows, width = x.shape
    return resident_call(
        query_key_body,
        (x, gain, w_qkv, cosine, sines),
        [sds((rows, width), bf16)] * 3,
        "query_key",
        4 * rows * width * width,
        scalars=0,
    )


def value_mix_body(normed_ref, w_ref, first_ref, out_ref):
    width = out_ref.shape[1]
    block = 256
    for j in range(width // block):
        at = slice(j * block, (j + 1) * block)
        projected = mm(normed_ref[...], w_ref[:, 2 * width + j * block : 2 * width + (j + 1) * block], NN)
        out_ref[:, at] = (0.5 * projected + 0.5 * first_ref[:, at].astype(f32)).astype(bf16)


def value_mix(normed, w_qkv, first):
    rows, width = normed.shape
    return resident_call(
        value_mix_body,
        (normed, w_qkv, first),
        [sds((rows, width), bf16)],
        "value_mix",
        2 * rows * width * width,
        scalars=0,
    )[0]


def set_bias(bias_ref, kpos_ref, qpos_ref, qstart_ref):
    keys, qpos = kpos_ref[...], qpos_ref[...]
    allowed = (keys <= qpos) & (keys >= qstart_ref[...])
    bias_ref[...] = jnp.where(allowed, 0.0, -1e30)


def attend_body(slots, *refs):
    q_ref = refs[0]
    k_refs = refs[1 : 1 + slots]
    v_refs = refs[1 + slots : 1 + 2 * slots]
    kpos_ref, qpos_ref, qstart_ref, out_ref, lse_ref, bias_ref = refs[1 + 2 * slots :]

    @pl.when(pl.program_id(0) == 0)
    def _():
        set_bias(bias_ref, kpos_ref, qpos_ref, qstart_ref)

    queries = q_ref[...] * jnp.asarray(score_scale, bf16)
    keys = jnp.concatenate([r[...] for r in k_refs], axis=0)
    values = jnp.concatenate([r[...] for r in v_refs], axis=0)
    values_t = jnp.transpose(values)
    outs = []
    for head in range(2):
        own = jnp.where(head_mask(queries.shape, head), queries, jnp.zeros_like(queries))
        scores = mm(keys, own, NT) + bias_ref[...]
        top = jnp.max(scores, axis=0, keepdims=True)
        weights = jnp.exp(scores - top)
        total = jnp.sum(weights, axis=0, keepdims=True)
        probs = (weights * (1.0 / total)).astype(bf16)
        outs.append(mm(values_t[head * HEAD_DIM : (head + 1) * HEAD_DIM], probs, NN))
        lse_ref[0, head : head + 1, :] = top + jnp.log(total)
    out_ref[...] = jnp.transpose(jnp.concatenate(outs, axis=0)).astype(bf16)


def attend(q, ks, vs, kpos, qpos, qstart):
    rows, width = q.shape
    slots = len(ks)
    pairs = width // LANES
    keys = slots * rows
    col = pl.BlockSpec((rows, LANES), lambda i: (0, i))
    return pl.pallas_call(
        functools.partial(attend_body, slots),
        grid=(pairs,),
        in_specs=[col]
        + [col] * slots
        + [col] * slots
        + [whole((keys, 1)), whole((1, rows)), whole((1, rows))],
        out_specs=[col, pl.BlockSpec((1, 2, rows), lambda i: (i, 0, 0))],
        out_shape=[sds((rows, width), bf16), sds((pairs, 2, rows), f32)],
        scratch_shapes=[pltpu.VMEM((keys, rows), f32)],
        cost_estimate=cost(
            8 * pairs * rows * keys * LANES, 2 * rows * width * (2 + 2 * slots), 2 * pairs * rows * keys
        ),
        name="attend",
    )(q, *ks, *vs, kpos, qpos, qstart)


def attend_back_body(slots, *refs):
    q_ref, grad_ref = refs[:2]
    k_refs = refs[2 : 2 + slots]
    v_refs = refs[2 + slots : 2 + 2 * slots]
    lse_ref, kpos_ref, qpos_ref, qstart_ref, cos_ref, sin_ref = refs[2 + 2 * slots : 8 + 2 * slots]
    gq_ref, gk_ref, gv_ref = refs[8 + 2 * slots : 11 + 2 * slots]
    other_refs = refs[11 + 2 * slots : 10 + 3 * slots]
    bias_ref = refs[-1]

    @pl.when(pl.program_id(0) == 0)
    def _():
        set_bias(bias_ref, kpos_ref, qpos_ref, qstart_ref)

    queries = q_ref[...] * jnp.asarray(score_scale, bf16)
    grads = grad_ref[...]
    keys = jnp.concatenate([r[...] for r in k_refs], axis=0)
    values = jnp.concatenate([r[...] for r in v_refs], axis=0)
    keys_t = jnp.transpose(keys)
    grad_values = grad_keys = None
    grad_q = []
    for head in range(2):
        mask = head_mask(queries.shape, head)
        own_q = jnp.where(mask, queries, jnp.zeros_like(queries))
        own_g = jnp.where(mask, grads, jnp.zeros_like(grads))
        scores = mm(keys, own_q, NT) + bias_ref[...]
        probs = jnp.exp(scores - lse_ref[0, head : head + 1, :])
        grad_probs = mm(values, own_g, NT)
        delta = jnp.sum(probs * grad_probs, axis=0, keepdims=True)
        grad_scores = (probs * (grad_probs - delta)).astype(bf16)
        part_v = mm(probs.astype(bf16), own_g, NN)
        part_k = mm(grad_scores, own_q, NN)
        grad_values = part_v if grad_values is None else grad_values + part_v
        grad_keys = part_k if grad_keys is None else grad_keys + part_k
        grad_q.append(mm(keys_t[head * HEAD_DIM : (head + 1) * HEAD_DIM], grad_scores, NN))
    grad_q = jnp.transpose(jnp.concatenate(grad_q, axis=0)) * score_scale
    gq_ref[...] = (grad_q * cos_ref[...] - turn(grad_q) * sin_ref[...]).astype(bf16)
    rows = q_ref.shape[0]
    gk_ref[...] = grad_keys[:rows]
    gv_ref[...] = grad_values[:rows]
    for slot in range(1, slots):
        other_refs[slot - 1][0] = grad_keys[slot * rows : (slot + 1) * rows].astype(bf16)
        other_refs[slot - 1][1] = grad_values[slot * rows : (slot + 1) * rows].astype(bf16)


def attend_back(q, grad, ks, vs, lse, kpos, qpos, qstart, cosine, sines):
    rows, width = q.shape
    slots = len(ks)
    pairs = width // LANES
    keys = slots * rows
    col = pl.BlockSpec((rows, LANES), lambda i: (0, i))
    outs = pl.pallas_call(
        functools.partial(attend_back_body, slots),
        grid=(pairs,),
        in_specs=[col, col]
        + [col] * slots
        + [col] * slots
        + [pl.BlockSpec((1, 2, rows), lambda i: (i, 0, 0))]
        + [whole((keys, 1)), whole((1, rows)), whole((1, rows))]
        + [whole((rows, LANES))] * 2,
        out_specs=[col] * 3 + [pl.BlockSpec((2, rows, LANES), lambda i: (0, 0, i))] * (slots - 1),
        out_shape=[sds((rows, width), bf16)]
        + [sds((rows, width), f32)] * 2
        + [sds((2, rows, width), bf16)] * (slots - 1),
        scratch_shapes=[pltpu.VMEM((keys, rows), f32)],
        cost_estimate=cost(
            20 * pairs * rows * keys * LANES, 2 * rows * width * (7 + 4 * slots), 2 * pairs * rows * keys
        ),
        name="attend_back",
    )(q, grad, *ks, *vs, lse, kpos, qpos, qstart, cosine, sines)
    return (*outs[:3], outs[3:])


def middle_body(x_ref, att_ref, wout_ref, gain_ref, mid_ref, nffn_ref):
    middle = x_ref[...].astype(f32) + mm(att_ref[...], wout_ref[...], NN)
    mid_ref[...] = middle
    factor = lax.rsqrt(jnp.mean(middle * middle, axis=-1, keepdims=True) + epsilon)
    nffn_ref[...] = (middle * factor * gain_ref[...]).astype(bf16)


def middle_norm(x, attended, w_out, gain):
    rows, width = x.shape
    return resident_call(
        middle_body,
        (x, attended, w_out, gain),
        [sds((rows, width), f32), sds((rows, width), bf16)],
        "middle_norm",
        2 * rows * width * width,
        scalars=0,
    )


def ffn_acts_body(
    sizes,
    edge_ref,
    nffn_ref,
    cot_ref,
    wg_ref,
    wu_ref,
    wd_ref,
    hid_ref,
    gg_ref,
    gu_ref,
    hk_ref,
    hs_ref,
    ak_ref,
    as_ref,
    bk_ref,
    bs_ref,
):
    total, hid_half, a_half, b_half = sizes
    block = 256
    per = block // LANES
    for step in range(total // per):
        at = slice(step * block, (step + 1) * block)
        gate = mm(nffn_ref[...], wg_ref[:, at], NN)
        upward = mm(nffn_ref[...], wu_ref[:, at], NN)
        grad_hidden = mm(cot_ref[...], wd_ref[at, :], NT)
        sig = 1.0 / (1.0 + jnp.exp(-gate))
        silu = gate * sig
        hid_ref[:, at] = (silu * upward).astype(bf16)
        gg_ref[:, at] = (grad_hidden * upward * (sig * (1.0 + gate * (1.0 - sig)))).astype(bf16)
        gu_ref[:, at] = (grad_hidden * silu).astype(bf16)

    low_edge, high_edge = edge_ref[0], edge_ref[1]

    def halves(edge, keep_ref, send_ref, size, places):
        for half in range(2):
            runs = []
            for offset in range(size):
                source, start = places[half * size + offset]
                if runs and runs[-1][0] is source and runs[-1][2] == start:
                    runs[-1][2] += 1
                else:
                    runs.append([source, start, start + 1, offset])
            for source, start, stop, offset in runs:
                src = slice(start * LANES, stop * LANES)
                dst = slice(offset * LANES, (offset + stop - start) * LANES)

                @pl.when(edge == half)
                def _(source=source, src=src, dst=dst):
                    keep_ref[:, dst] = source[:, src]

                @pl.when(edge != half)
                def _(source=source, src=src, dst=dst):
                    send_ref[:, dst] = source[:, src]

    acts = [(gg_ref, i) for i in range(total)] + [(gu_ref, i) for i in range(total)]
    halves(high_edge, hk_ref, hs_ref, hid_half, [(hid_ref, i) for i in range(total)])
    halves(low_edge, ak_ref, as_ref, a_half, acts[: 2 * a_half])
    halves(low_edge, bk_ref, bs_ref, b_half, acts[2 * a_half :])


def half_blocks(ff):
    total = ff // LANES
    a_half = (total + 1) // 2 + (total // 2) % 2
    return total, total // 2, a_half, total - a_half


def ffn_acts(edges, nffn, cot, w_gate, w_up, w_down):
    rows, width = nffn.shape
    ff = w_gate.shape[1]
    sizes = half_blocks(ff)
    _, hid_half, a_half, b_half = sizes
    widths = [ff] * 3 + [hid_half * LANES] * 2 + [a_half * LANES] * 2 + [b_half * LANES] * 2
    return resident_call(
        functools.partial(ffn_acts_body, sizes),
        (edges, nffn, cot, w_gate, w_up, w_down),
        [sds((rows, w), bf16) for w in widths],
        "ffn_acts",
        6 * rows * width * ff,
    )


def ffn_back_body(
    seqs,
    edge_ref,
    hid_ref,
    gg_ref,
    gu_ref,
    wg_ref,
    wu_ref,
    wd_ref,
    mid_ref,
    cot_ref,
    wout_ref,
    gain_ref,
    *refs,
):
    out_refs = refs[:seqs]
    gmid_ref, keep_ref, send_ref, gatt_ref = refs[seqs:]
    length = out_refs[0].shape[0]
    middle = mid_ref[...]
    grads = mm(gg_ref[...], wg_ref[...], NT) + mm(gu_ref[...], wu_ref[...], NT)
    factor = lax.rsqrt(jnp.mean(middle * middle, axis=-1, keepdims=True) + epsilon)
    scaled = grads * gain_ref[...]
    inner = jnp.mean(scaled * middle, axis=-1, keepdims=True)
    grad_middle = cot_ref[...].astype(f32) + factor * (scaled - middle * (factor * factor * inner))
    gmid_ref[...] = grad_middle
    branch = grad_middle.astype(bf16)
    half = branch.shape[1] // 2

    @pl.when(edge_ref[1] == 0)
    def _():
        keep_ref[...] = branch[:, :half]
        send_ref[...] = branch[:, half:]

    @pl.when(edge_ref[1] != 0)
    def _():
        keep_ref[...] = branch[:, half:]
        send_ref[...] = branch[:, :half]

    gatt_ref[...] = mm(branch, wout_ref[...], NT).astype(bf16)
    out = middle + mm(hid_ref[...], wd_ref[...], NN)
    for s in range(seqs):
        out_refs[s][...] = out[s * length : (s + 1) * length].astype(bf16)


def ffn_back(seqs, edges, hidden, gg, gu, w_gate, w_up, w_down, middle, cot, w_out, gain):
    rows, width = cot.shape
    ff = w_gate.shape[1]
    outs = resident_call(
        functools.partial(ffn_back_body, seqs),
        (edges, hidden, gg, gu, w_gate, w_up, w_down, middle, cot, w_out, gain),
        [sds((rows // seqs, width), bf16)] * seqs
        + [
            sds((rows, width), f32),
            sds((rows, width // 2), bf16),
            sds((rows, width // 2), bf16),
            sds((rows, width), bf16),
        ],
        "ffn_back",
        6 * rows * width * ff + 2 * rows * width * width,
    )
    return outs[:seqs], outs[seqs:]


def grad_pack_body(seqs, received, edge_ref, *refs):
    gq_ref, gk_ref, gv_ref = refs[:3]
    others = refs[3 : 3 + received]
    cos_ref, sin_ref, packed_ref = refs[3 + received : 6 + received]
    first_refs = refs[6 + received : 6 + received + seqs]
    xk_ref, xs_ref, yk_ref, ys_ref = refs[6 + received + seqs :]
    width = gq_ref.shape[1]
    length = first_refs[0].shape[0]
    low_edge, high_edge = edge_ref[0], edge_ref[1]
    pairs = width // LANES
    quarter = pairs // 4
    for pair in range(pairs):
        at = slice(pair * LANES, (pair + 1) * LANES)
        at_v = slice(width + pair * LANES, width + (pair + 1) * LANES)
        grad_k, grad_v = gk_ref[:, at], gv_ref[:, at]
        for r in others:
            grad_k = grad_k + r[0, :, at].astype(f32)
            grad_v = grad_v + r[1, :, at].astype(f32)
        grad_k = (grad_k * cos_ref[...] - turn(grad_k) * sin_ref[...]).astype(bf16)
        grad_v = (0.5 * grad_v).astype(bf16)
        for s in range(seqs):
            first_refs[s][:, at] = grad_v[s * length : (s + 1) * length]
        packed_ref[:, at] = gq_ref[:, at]
        packed_ref[:, at_v] = grad_k
        packed_ref[:, 2 * width + pair * LANES : 2 * width + (pair + 1) * LANES] = grad_v
        packed = jnp.concatenate([gq_ref[:, at], grad_k, grad_v], axis=1)
        color, half = pair // (2 * quarter), pair // quarter % 2
        edge = high_edge if color else low_edge
        keep_ref, send_ref = (yk_ref, ys_ref) if color else (xk_ref, xs_ref)
        dst = slice(pair % quarter * 3 * LANES, (pair % quarter + 1) * 3 * LANES)

        @pl.when(edge == half)
        def _(keep_ref=keep_ref, dst=dst, packed=packed):
            keep_ref[:, dst] = packed

        @pl.when(edge != half)
        def _(send_ref=send_ref, dst=dst, packed=packed):
            send_ref[:, dst] = packed


def grad_pack(seqs, edges, gq, gk, gv, others, cosine, sines):
    rows, width = gq.shape
    outs = resident_call(
        functools.partial(grad_pack_body, seqs, len(others)),
        (edges, gq, gk, gv, *others, cosine, sines),
        [sds((rows, 3 * width), bf16)]
        + [sds((rows // seqs, width), bf16)] * seqs
        + [sds((rows, 3 * width // 4), bf16)] * 4,
        "grad_pack",
        20 * rows * width,
    )
    return outs[0], outs[1 : 1 + seqs], outs[1 + seqs :]


def grad_inputs_body(seqs, packed_ref, w_ref, x_ref, gain_ref, gmid_ref, *refs):
    first_refs, out_refs = refs[:seqs], refs[seqs:]
    grads = mm(packed_ref[...], w_ref[...], NT)
    inputs = x_ref[...].astype(f32)
    factor = lax.rsqrt(jnp.mean(inputs * inputs, axis=-1, keepdims=True) + epsilon)
    scaled = grads * gain_ref[...]
    inner = jnp.mean(scaled * inputs, axis=-1, keepdims=True)
    grads = gmid_ref[...] + factor * (scaled - inputs * (factor * factor * inner))
    grads = grads.astype(bf16)
    length = out_refs[0].shape[1]
    for s in range(seqs):
        out_refs[s][0] = grads[s * length : (s + 1) * length]
        out_refs[s][1] = first_refs[s][...]


def grad_inputs(seqs, packed, w_qkv, x, gain, grad_middle, first_blocks):
    rows, width = x.shape
    return resident_call(
        functools.partial(grad_inputs_body, seqs),
        (packed, w_qkv, x, gain, grad_middle, *first_blocks),
        [sds((2, rows // seqs, width), bf16)] * seqs,
        "grad_inputs",
        6 * rows * width * width,
        scalars=0,
    )


def place_body(seqs, shift_ref, *refs):
    for i, out_ref in enumerate(refs[seqs:]):
        for j in range(seqs):
            for s in range(seqs):

                @pl.when(lax.rem(shift_ref[0] + s, seqs) == j)
                def _(i=i, j=j, s=s, out_ref=out_ref):
                    out_ref[j] = refs[s][i]


def place(parts, seq):
    seqs = len(parts)
    count, length, width = parts[0].shape
    part = pl.BlockSpec((count, length, width // 4), lambda i: (0, 0, i))
    return pl.pallas_call(
        functools.partial(place_body, seqs),
        grid=(4,),
        in_specs=[scalar()] + [part] * seqs,
        out_specs=[pl.BlockSpec((seqs, length, width // 4), lambda i: (0, 0, i))] * count,
        out_shape=[sds((seqs, length, width), bf16)] * count,
        compiler_params=pltpu.CompilerParams(vmem_limit_bytes=VMEM_LIMIT),
        cost_estimate=cost(0, 4 * seqs * count * length * width),
        name="place",
    )(seq[None], *parts)


def outer_body(counts, per, core_ref, *refs):
    keep_ref, send_ref = refs[-2:]
    column = at = 0
    core = core_ref[0]
    for count in counts:
        lefts, rights = refs[at : at + count], refs[at + count : at + 2 * count]
        at += 2 * count
        total = None
        for left, right in zip(lefts, rights):
            part = mm(left[...], right[...], TN)
            total = part if total is None else total + part
        wide = total.shape[1]
        cut = slice(column, column + wide)
        column += wide
        total = total.astype(bf16)
        for i in range(total.shape[0] // (2 * per)):
            even = total[2 * i * per : (2 * i + 1) * per]
            odd = total[(2 * i + 1) * per : (2 * i + 2) * per]

            @pl.when(core == 0)
            def _(i=i, even=even, odd=odd, cut=cut):
                keep_ref[i, :, cut] = even
                send_ref[i, :, cut] = odd

            @pl.when(core != 0)
            def _(i=i, even=even, odd=odd, cut=cut):
                keep_ref[i, :, cut] = odd
                send_ref[i, :, cut] = even


def outer(core, per, *groups):
    rows, height = groups[0][0][0].shape
    width = sum(rights[0].shape[1] for _, rights in groups)
    block = 256 if height % 256 == 0 else height
    specs, args, flops = [], [], 0
    for lefts, rights in groups:
        wide = rights[0].shape[1]
        specs += [pl.BlockSpec((rows, block), lambda i: (0, i))] * len(lefts)
        specs += [whole((rows, wide))] * len(rights)
        args += [*lefts, *rights]
        flops += 2 * len(lefts) * rows * height * wide
    out_spec = pl.BlockSpec((block // (2 * per), per, width), lambda i: (i, 0, 0))
    return pl.pallas_call(
        functools.partial(outer_body, [len(lefts) for lefts, _ in groups], per),
        grid=(height // block,),
        in_specs=[scalar()] + specs,
        out_specs=[out_spec] * 2,
        out_shape=[sds((height // (2 * per), per, width), bf16)] * 2,
        cost_estimate=cost(flops, 2 * (sum(a.size for a in args) + height * width)),
        name="outer",
    )(core[None], *args)


def build(ndp, nblk):
    n = ndp * nblk
    nbits = n.bit_length() - 1
    blk_bits = nblk.bit_length() - 1
    if (1 << nbits) != n or (1 << blk_bits) != nblk:
        raise ValueError("mesh sizes")
    low_e, high_e = blk_bits, nbits - 1

    def send(value, target):
        pairs = [(i, target(i)) for i in range(n)]
        return lax.ppermute(value, AXES, pairs)

    def flip(value, bit):
        return send(value, lambda i: i ^ (1 << bit))

    def pick(value, index, axis=0):
        return lax.dynamic_index_in_dim(value, index, axis, keepdims=False)

    def shards(
        tokens, first_values, docs, cotangent, w_qkv, w_out, w_gate, w_up, w_down, gain_attn, gain_ffn
    ):
        seqs, length, width = tokens.shape
        ff = w_gate.shape[1]
        rows = seqs * length
        group = nblk // seqs
        blk = lax.axis_index("blk")
        index = lax.axis_index("dp") * nblk + blk
        seq, member = blk // group, blk % group

        def bit(t):
            return (index >> t) & 1

        core = bit(0)
        edges = jnp.stack([bit(low_e), bit(high_e)])

        def shift_seq(i, s):
            base, b = i - i % nblk, i % nblk
            return base + ((b // group + s) % seqs) * group + b % group

        def shift_member(i, s):
            base, b = i - i % nblk, i % nblk
            return base + (b // group) * group + (b % group + s) % group

        def to_sequence(value):
            parts = [pick(value, seq)]
            for s in range(1, seqs):
                out = pick(value, (seq + s) % seqs)
                parts.append(send(out, lambda i, s=s: shift_seq(i, s)))
            return parts

        def from_sequence(blocks):
            return [
                part if s == 0 else send(part, lambda i, s=s: shift_seq(i, -s))
                for s, part in enumerate(blocks)
            ]

        def others(value):
            return [send(value, lambda i, g=g: shift_member(i, g)) for g in range(1, group)]

        marks = jnp.pad(docs[:, None, :].astype(bf16), ((0, 0), (0, 7), (0, width - length)))
        parts = to_sequence(jnp.concatenate([tokens, marks, first_values], axis=1))

        base = jnp.arange(length, dtype=jnp.int32)
        qpos = jnp.concatenate(
            [(((seq - s) % seqs) * group + member) * length + base for s in range(seqs)]
        )
        kpos = jnp.concatenate(
            [
                (((seq - s) % seqs) * group + (member - g) % group) * length + base
                for g in range(group)
                for s in range(seqs)
            ]
        )
        half = HEAD_DIM // 2
        inverse = 10000.0 ** (-jnp.arange(half, dtype=f32) / half)
        angles = qpos.astype(f32)[:, None] * inverse[None, :]
        cos_half, sin_half = jnp.cos(angles), jnp.sin(angles)
        cosine = jnp.concatenate([cos_half] * 4, axis=1)
        sines = jnp.concatenate([-sin_half, sin_half] * 2, axis=1)
        qpos, kpos = qpos[None, :], kpos[:, None]
        gain_a, gain_f = gain_attn[None, :], gain_ffn[None, :]

        cosine, sines, qpos, kpos, parts, cotangent = tie(
            cosine, sines, qpos, kpos, parts, cotangent
        )
        x = jnp.concatenate([p[:length] for p in parts], axis=0)
        first = jnp.concatenate([p[-length:] for p in parts], axis=0)
        qdocs = jnp.concatenate([p[length, :length] for p in parts]).astype(jnp.int32)[None]
        normed, q, k = query_key(x, gain_a, w_qkv, cosine, sines)
        other_docs = others(qdocs)
        ks = [k] + others(k)
        cot_parts = to_sequence(cotangent)
        all_docs = jnp.concatenate([qdocs] + other_docs, axis=1)
        qstart = jnp.sum((all_docs[0][:, None] < qdocs).astype(jnp.int32), axis=0, keepdims=True)
        v = value_mix(normed, w_qkv, first)
        normed_x = flip(normed, low_e)
        normed_y = flip(normed, high_e)
        vs = [v] + others(v)
        attended, lse = attend(q, ks, vs, kpos, qpos, qstart)
        attended, normed_x, normed_y, cot_parts = tie(attended, normed_x, normed_y, cot_parts)
        cot = jnp.concatenate(cot_parts, axis=0)
        attended_y = flip(attended, high_e)
        cot_y = flip(cot, high_e)
        middle, nffn = middle_norm(x, attended, w_out, gain_f)
        nffn_x = flip(nffn, low_e)
        hidden, gg, gu, hk, hs, ak, a_s, bk, bs = ffn_acts(edges, nffn, cot, w_gate, w_up, w_down)
        hidden, gg, gu, hs, a_s, bs, nffn_x, cot_y, attended_y = tie(
            hidden, gg, gu, hs, a_s, bs, nffn_x, cot_y, attended_y
        )
        h_y = flip(hs, high_e)
        a_x = flip(a_s, low_e)
        out_blocks, (grad_mid, gbk, gbs, grad_att) = ffn_back(
            seqs, edges, hidden, gg, gu, w_gate, w_up, w_down, middle, cot, w_out, gain_f
        )
        gbs, bs, grad_att = tie(gbs, bs, grad_att)
        out_parts = from_sequence(out_blocks)
        b_x = flip(bs, low_e)
        gb_y = flip(gbs, high_e)
        gq, gk, gv, other_kv = attend_back(
            q, grad_att, ks, vs, lse, kpos, qpos, qstart, cosine, sines
        )
        gq, gk, gv, other_kv, h_y, a_x, out_parts = tie(
            gq, gk, gv, other_kv, h_y, a_x, out_parts
        )
        got_kv = [send(v, lambda i, g=g: shift_member(i, -g)) for g, v in enumerate(other_kv, 1)]
        per_down = ff // n
        per = width // n

        class Rows:
            def __init__(self, keep, got, top, skip):
                dims = (2,) * top + keep.shape[1:]
                self.terms = [keep.reshape(dims), got.reshape(dims)]
                self.left = list(range(top, 0, -1))
                self.order = [t for t in self.left if t >= blk_bits and t != skip]
                self.order += list(range(1, min(blk_bits, top + 1)))
                self.skip, self.swapped = skip, False

            def total(self, terms):
                return functools.reduce(lambda a, b: a + b, [t.astype(f32) for t in terms])

            def go(self):
                t = self.order.pop(0)
                axis, b = self.left.index(t), bit(t)
                out = self.total([pick(v, 1 - b, axis) for v in self.terms]).astype(bf16)
                self.terms = [pick(v, b, axis) for v in self.terms] + [flip(out, t)]
                self.left.pop(axis)

            def next(self):
                if self.order:
                    self.go()
                elif self.skip >= 0 and not self.swapped:
                    value, b = self.total(self.terms), bit(self.skip)
                    self.swapped = True
                    out = flip(pick(value, 1 - b).astype(bf16), self.skip)
                    self.terms = [pick(value, b), out]
                else:
                    return False
                return True

            def halves(self):
                mine, other = self.terms[0], self.terms[1].astype(f32)
                b = bit(self.skip)
                return jnp.stack([jnp.where(b == 0, mine, other), jnp.where(b == 0, other, mine)])

        def settle(values, *reductions):
            last = [r.terms[-1] for r in reductions]
            values, last = tie(values, last)
            for r, got in zip(reductions, last):
                r.terms[-1] = got
            return values

        ak2, as2 = outer(core, per, ([nffn, nffn_x], [ak, a_x]))
        ak2, as2, got_kv = tie(ak2, as2, got_kv)
        a_c = flip(as2, 0)
        packed, first_blocks, (qxk, qxs, qyk, qys) = grad_pack(
            seqs, edges, gq, gk, gv, got_kv, cosine, sines
        )
        packed, first_blocks, qxs, qys, a_c, hk, h_y = tie(
            packed, first_blocks, qxs, qys, a_c, hk, h_y
        )
        part_a = Rows(ak2, a_c, nbits - 1, low_e)
        part_a.next()
        q_x = flip(qxs, low_e)
        q_y = flip(qys, high_e)
        dk, ds = outer(core, per_down, ([hk, h_y], [cot, cot_y]))
        blocks = grad_inputs(seqs, packed, w_qkv, x, gain_a, grad_mid, first_blocks)
        blocks, dk, ds, bk, b_x, gb_y = settle((blocks, dk, ds, bk, b_x, gb_y), part_a)
        d_c = flip(ds, 0)
        moved = from_sequence(blocks)
        bk2, bs2 = outer(core, per, ([nffn, nffn_x], [bk, b_x]))
        bk2, bs2, d_c, q_x, q_y = tie(bk2, bs2, d_c, q_x, q_y)
        b_c = flip(bs2, 0)
        down = Rows(dk, d_c, nbits - 2, -1)
        down.next()
        qyk2, qys2 = outer(
            core, per, ([normed, normed_y], [qyk, q_y]), ([attended, attended_y], [gbk, gb_y])
        )
        qyk2, qys2, b_c, moved[1::2] = tie(qyk2, qys2, b_c, moved[1::2])
        qy_c = flip(qys2, 0)
        part_b = Rows(bk2, b_c, nbits - 1, low_e)
        part_b.next()
        part_a.next()
        qxk2, qxs2 = outer(core, per, ([normed, normed_x], [qxk, q_x]))
        qxk2, qxs2, qy_c = settle((qxk2, qxs2, qy_c), part_a, down)
        qx_c = flip(qxs2, 0)
        part_y = Rows(qyk2, qy_c, nbits - 1, high_e)
        part_y.next()
        part_a.next()
        down.next()
        (qx_c,) = settle((qx_c,), part_a, part_b, down)
        part_x = Rows(qxk2, qx_c, nbits - 1, low_e)
        part_x.next()
        part_b.next()
        down.next()
        part_a.next()
        (moved,) = settle((moved,), part_a, part_b, part_y, down)
        everything = (part_a, part_b, part_y, part_x, down)
        while True:
            busy = [part for part in everything if part.next()]
            if not busy:
                break
            settle((), *busy)
        grad_down = down.total(down.terms)
        a_done, b_done, qx_done, qy_done = (
            part.halves() for part in (part_a, part_b, part_x, part_y)
        )
        (output,) = place([part[None] for part in out_parts], seq)
        grad_tokens, grad_first_values = place(moved, seq)

        acts = jnp.concatenate([a_done[0], a_done[1], b_done[0], b_done[1]], axis=1)
        grad_gate, grad_up = acts[:, :ff], acts[:, ff:]
        q_wide = 3 * width // 4
        grad_out = jnp.concatenate([qy_done[0, :, q_wide:], qy_done[1, :, q_wide:]], axis=1)
        qy_done = qy_done[:, :, :q_wide]
        pairs = width // LANES
        grad_qkv = jnp.concatenate([qx_done, qy_done], axis=0)
        grad_qkv = grad_qkv.reshape(4, per, pairs // 4, 3, LANES)
        grad_qkv = jnp.transpose(grad_qkv, (1, 3, 0, 2, 4)).reshape(per, 3 * width)

        def own(value):
            return lax.dynamic_slice_in_dim(value, index * per, per, 0)

        grad_gain_attn = jnp.sum(grad_qkv * own(w_qkv).astype(f32), axis=1) / own(gain_attn)
        grad_gain_ffn = (
            jnp.sum(
                grad_gate * own(w_gate).astype(f32) + grad_up * own(w_up).astype(f32), axis=1
            )
            / own(gain_ffn)
        )
        return (
            output,
            grad_tokens,
            grad_first_values,
            grad_qkv,
            grad_out,
            grad_gate,
            grad_up,
            grad_down,
            grad_gain_attn,
            grad_gain_ffn,
        )

    return shards


def solution(mesh):
    seq = P("dp", "blk", None)
    rows = P(AXES, None)
    vec = P(AXES)
    in_specs = (seq, seq, P("dp", "blk"), seq) + (P(),) * 7
    out_specs = (seq, seq, seq, rows, rows, rows, rows, rows, vec, vec)
    return jax.shard_map(
        build(mesh.shape["dp"], mesh.shape["blk"]),
        mesh=mesh,
        in_specs=in_specs,
        out_specs=out_specs,
        check_vma=False,
    )
```
